32 devices in a mesh: ctx: 16 (over z, x, core), fsdp: 2 (over y).
Axes of the slice: x: 2, y: 2, z: 4, core: 2. Of those that a mesh axis runs over, the one named last changes fastest.
Arguments:
- tokens: bfloat16 [2, 4096, 768], P('fsdp', 'ctx'), may hold values from -6 to 6
- query_weight: bfloat16 [768, 768], P('fsdp'), may hold values from -0.21875 to 0.21875
- query_bias: bfloat16 [768], P('fsdp'), may hold values from -1.5 to 1.5
- key_weight: bfloat16 [768, 768], P('fsdp'), may hold values from -0.21875 to 0.21875
- value_weight: bfloat16 [768, 768], P('fsdp'), may hold values from -0.21875 to 0.21875
- value_bias: bfloat16 [768], P('fsdp'), may hold values from -1.5 to 1.5
- out_weight: bfloat16 [768, 768], P('fsdp'), may hold values from -1.25 to 1.25
- out_bias: bfloat16 [768], P('fsdp'), may hold values from -1.5 to 1.5
- first_gain: bfloat16 [768], P('fsdp'), may hold values from 0.5 to 1.5
- first_shift: bfloat16 [768], P('fsdp'), may hold values from -1.5 to 1.5
- inner_weight: bfloat16 [768, 3072], P('fsdp'), may hold values from -0.21875 to 0.21875
- inner_bias: bfloat16 [3072], P('fsdp'), may hold values from -1.5 to 1.5
- outer_weight: bfloat16 [3072, 768], P('fsdp'), may hold values from -0.109375 to 0.109375
- outer_bias: bfloat16 [768], P('fsdp'), may hold values from -1.5 to 1.5
- second_gain: bfloat16 [768], P('fsdp'), may hold values from 0.5 to 1.5
- second_shift: bfloat16 [768], P('fsdp'), may hold values from -1.5 to 1.5
- doc_lengths: int32 [2, 48], P('fsdp'), may hold values from 1 to 2304, 4096 in all within a row
- grad_output: bfloat16 [2, 4096, 768], P('fsdp', 'ctx'), may hold values from -6 to 6
Outputs:
- output: bfloat16 [2, 4096, 768], P('fsdp', 'ctx')
- grad_tokens: float32 [2, 4096, 768], P('fsdp', 'ctx')
- grad_query_weight: float32 [768, 768], P('fsdp')
- grad_query_bias: float32 [768], P('fsdp')
- grad_key_weight: float32 [768, 768], P('fsdp')
- grad_value_weight: float32 [768, 768], P('fsdp')
- grad_value_bias: float32 [768], P('fsdp')
- grad_out_weight: float32 [768, 768], P('fsdp')
- grad_out_bias: float32 [768], P('fsdp')
- grad_first_gain: float32 [768], P('fsdp')
- grad_first_shift: float32 [768], P('fsdp')
- grad_inner_weight: float32 [768, 3072], P('fsdp')
- grad_inner_bias: float32 [3072], P('fsdp')
- grad_outer_weight: float32 [3072, 768], P('fsdp')
- grad_outer_bias: float32 [768], P('fsdp')
- grad_second_gain: float32 [768], P('fsdp')
- grad_second_shift: float32 [768], P('fsdp')
The draws below stay inside these ranges and needn't reach their ends.
Inputs may be any that keep to these rules, and one draw needn't show every extreme that they name: `doc_lengths`: each row holds the 48 document lengths of one sequence in order; they sum to 4096 and the longest is exactly 2304.
All inputs are finite; a program needn't handle non-finite values.
Results may differ from the reference program's by a relative error of at most 0.018.
Values may be sent and summed in bfloat16 or wider, within the bound.
No kernel may reach another device: no remote copies, remote signals or barrier semaphores. Data moves between devices by JAX's collectives and lax.ppermute only.
A program may use at most 384 MiB of HBM per device.

```python
import math
import jax
import jax.numpy as jnp
import numpy as np
from jax import lax

D = 768
H = 12
HD = 64
FF = 3072
DOCS = 48
LEN = 4096
SEQS = 2
DOC_MOST = 2304


def steps_of(stream_key, extent, cuts, smallest, top_value):
    level = 1.0
    for dim, blocks in cuts:
        steps = jax.random.uniform(jax.random.fold_in(jax.random.fold_in(stream_key, 6), dim), (blocks,), jnp.float32, smallest / len(cuts), top_value / len(cuts))
        level = level * jnp.repeat(jnp.exp(steps), extent[dim] // blocks).reshape((-1,) + (1,) * (len(extent) - 1 - dim))
    return level


def profile(amount, total, most, skew):
    weights = [(1 << 20) // math.isqrt(standing ** skew) + 1 for standing in range(2, amount + 1)]
    spare, given = total - most - (amount - 1), [1] * (amount - 1)
    while spare > 0:
        free = [i for i in range(amount - 1) if given[i] < most]
        whole, left = sum([weights[i] for i in free]), spare
        for i in free:
            extra = min(most - given[i], max(1, left * weights[i] // whole), spare)
            given[i] = given[i] + extra
            spare = spare - extra
    return np.array([most] + given)


def ragged(own_key, amount, total, limit, lean):
    if amount == 2:
        one = jax.random.randint(own_key, (), max(1, total - limit), min(limit, total - 1) + 1)
        return jnp.stack([one, total - one])
    sizes = jnp.asarray(profile(amount, total, limit, lean), jnp.int32)
    couples = (amount - 1) // 2
    source_of, sink = sizes[1:1 + 2 * couples:2], sizes[2:2 + 2 * couples:2]
    slack = jnp.minimum(source_of - 1, limit - sink)
    moved = jax.random.randint(jax.random.fold_in(own_key, 1), (couples,), 0, 1 << 20) % (slack + 1)
    sizes = sizes.at[1:1 + 2 * couples:2].set(source_of - moved).at[2:2 + 2 * couples:2].set(sink + moved)
    return sizes[jax.random.permutation(jax.random.fold_in(own_key, 2), amount)]


def scatter_about(own_key, dims, spread, limit, split=(), held_as=jnp.bfloat16):
    drawn = spread * jax.random.normal(own_key, dims, jnp.float32)
    if split:
        drawn = drawn * steps_of(own_key, dims, split, -0.22, 0.18)
    return jnp.clip(drawn, -limit, limit).astype(held_as)


def setup_inputs(seed: int = 0) -> dict:
    key_of = jax.random.split(jax.random.key(seed), 19)
    tokens = scatter_about(key_of[0], (SEQS, LEN, D), 1.0, 6.0, ((0, 2), (1, 16)))
    query_weight = scatter_about(key_of[1], (D, D), D ** -0.5, 0.21875, ((0, 2),))
    query_bias = scatter_about(key_of[2], (D,), 0.3, 1.5, ((0, 2),))
    key_weight = scatter_about(key_of[3], (D, D), D ** -0.5, 0.21875, ((0, 2),))
    value_weight = scatter_about(key_of[4], (D, D), D ** -0.5, 0.21875, ((0, 2),))
    value_bias = scatter_about(key_of[5], (D,), 0.3, 1.5, ((0, 2),))
    out_weight = scatter_about(key_of[6], (D, D), (D // 32) ** -0.5, 1.25, ((0, 2),))
    out_bias = scatter_about(key_of[7], (D,), 0.3, 1.5, ((0, 2),))
    first_gain = jnp.clip(1.0 + 0.1 * jax.random.normal(key_of[8], (D,), jnp.float32), 0.5, 1.5).astype(jnp.bfloat16)
    first_shift = scatter_about(key_of[9], (D,), 0.3, 1.5, ((0, 2),))
    inner_weight = scatter_about(key_of[10], (D, FF), D ** -0.5, 0.21875, ((0, 2),))
    inner_bias = scatter_about(key_of[11], (FF,), 0.3, 1.5, ((0, 2),))
    outer_weight = scatter_about(key_of[12], (FF, D), FF ** -0.5, 0.109375, ((0, 2),))
    outer_bias = scatter_about(key_of[13], (D,), 0.3, 1.5, ((0, 2),))
    second_gain = jnp.clip(1.0 + 0.1 * jax.random.normal(key_of[14], (D,), jnp.float32), 0.5, 1.5).astype(jnp.bfloat16)
    second_shift = scatter_about(key_of[15], (D,), 0.3, 1.5, ((0, 2),))
    doc_lengths = jax.vmap(lambda own: ragged(own, DOCS, LEN, DOC_MOST, 2))(jax.random.split(key_of[16], SEQS)).reshape((SEQS, DOCS)).astype(jnp.int32)
    grad_output = scatter_about(key_of[17], (SEQS, LEN, D), 1.0, 6.0, ((0, 2), (1, 16)))
    return {"tokens": tokens, "query_weight": query_weight, "query_bias": query_bias, "key_weight": key_weight, "value_weight": value_weight, "value_bias": value_bias, "out_weight": out_weight, "out_bias": out_bias, "first_gain": first_gain, "first_shift": first_shift, "inner_weight": inner_weight, "inner_bias": inner_bias, "outer_weight": outer_weight, "outer_bias": outer_bias, "second_gain": second_gain, "second_shift": second_shift, "doc_lengths": doc_lengths, "grad_output": grad_output}


@jax.custom_vjp
def low(v):
    return lax.optimization_barrier(v.astype(jnp.bfloat16)).astype(jnp.float32)

@jax.custom_vjp
def low_back(v):
    return v

def low_keep(v):
    return (low(v), None)

def low_pass(kept, grad):
    return (grad,)

def back_keep(v):
    return (v, None)

def back_low(kept, grad):
    return (low(grad),)
low.defvjp(low_keep, low_pass)
low_back.defvjp(back_keep, back_low)
eps = 1e-12

def layer_norm(r, gain, shift):
    mean = lax.optimization_barrier(jnp.mean(r, axis=-1, keepdims=True))
    centered = r - mean
    var = lax.optimization_barrier(jnp.mean(centered * centered, axis=-1, keepdims=True))
    return centered * lax.rsqrt(var + eps) * gain + shift

def matmul(a, b):
    return jnp.dot(a, b, precision=lax.Precision.HIGHEST, preferred_element_type=jnp.float32)

def segment_of(lengths):
    ends = jnp.cumsum(lengths).astype(jnp.int32)
    places = jnp.arange(LEN, dtype=jnp.int32)
    return lax.optimization_barrier(jnp.sum((places[:, None] >= ends[None, :]).astype(jnp.int32), axis=1)).astype(jnp.int32)

def attend_block(query_block, seg_block, keys, values, segs):
    scale = 1.0 / math.sqrt(HD)
    raw = jnp.einsum('qhd,khd->hqk', query_block, keys, precision=lax.Precision.HIGHEST) * scale
    allowed = (seg_block[:, None] == segs[None, :])[None]
    scores = low_back(jnp.where(allowed, raw, jnp.float32(-1e+30)))
    top = lax.optimization_barrier(jnp.max(scores, axis=-1, keepdims=True))
    expd = jnp.exp(scores - top)
    probs = low(expd / lax.optimization_barrier(jnp.sum(expd, axis=-1, keepdims=True)))
    return jnp.einsum('hqk,khd->qhd', probs, values, precision=lax.Precision.HIGHEST)

def attend_sequence(pieces):
    queries, keys, values, lengths = pieces
    segs = segment_of(lengths)
    block = math.gcd(LEN, 512)
    q_blocks = queries.reshape(LEN // block, block, H, HD)
    seg_blocks = segs.reshape(LEN // block, block)
    step = jax.checkpoint(lambda pair: attend_block(pair[0], pair[1], keys, values, segs))
    return lax.map(step, (q_blocks, seg_blocks)).reshape(LEN, H, HD)

def forward(tokens, query_weight, query_bias, key_weight, value_weight, value_bias, out_weight, out_bias, first_gain, first_shift, inner_weight, inner_bias, outer_weight, outer_bias, second_gain, second_shift, doc_lengths):
    flat = tokens.reshape(SEQS * LEN, D)
    queries = low_back(low(matmul(flat, query_weight) + query_bias))
    keys = low_back(low(matmul(flat, key_weight)))
    values = low_back(low(matmul(flat, value_weight) + value_bias))
    shaped = (queries.reshape(SEQS, LEN, H, HD), keys.reshape(SEQS, LEN, H, HD), values.reshape(SEQS, LEN, H, HD), doc_lengths)
    attended = lax.map(attend_sequence, shaped).reshape(SEQS * LEN, D)
    attended = low_back(low(attended))
    branch = low_back(matmul(attended, out_weight) + out_bias)
    hidden = layer_norm(flat + branch, first_gain, first_shift)
    inner = low_back(matmul(low(hidden), inner_weight) + inner_bias)
    act = low(jax.nn.gelu(inner, approximate=False))
    outer = low_back(matmul(act, outer_weight) + outer_bias)
    result = layer_norm(hidden + outer, second_gain, second_shift)
    return result.reshape(SEQS, LEN, D)

def reference(tokens, query_weight, query_bias, key_weight, value_weight, value_bias, out_weight, out_bias, first_gain, first_shift, inner_weight, inner_bias, outer_weight, outer_bias, second_gain, second_shift, doc_lengths, grad_output):
    floats = [a.astype(jnp.float32) for a in (tokens, query_weight, query_bias, key_weight, value_weight, value_bias, out_weight, out_bias, first_gain, first_shift, inner_weight, inner_bias, outer_weight, outer_bias, second_gain, second_shift)]
    result, pullback = jax.vjp(lambda *p: forward(*p, doc_lengths), *floats)
    grads = pullback(grad_output.astype(jnp.float32))
    return (result.astype(jnp.bfloat16), grads[0], grads[1], grads[2], grads[3], grads[4], grads[5], grads[6], grads[7], grads[8], grads[9], grads[10], grads[11], grads[12], grads[13], grads[14], grads[15])
```

```python
import functools
import math

import jax
import jax.numpy as jnp
from jax import lax
from jax.experimental import pallas as pl
from jax.experimental.pallas import tpu as pltpu
from jax.sharding import PartitionSpec as P

H = 12
HD = 64
NG = 4
HG = H // NG
GW = HG * HD

eps = 1e-12
NEG = -1e30
LOG2E = 1.4426950408889634
SCALE = 1.0 / math.sqrt(HD)
bf16 = jnp.bfloat16
f32 = jnp.float32


def layer_norm(r, gain, shift):
    mean = jnp.mean(r, axis=-1, keepdims=True)
    centered = r - mean
    var = jnp.mean(centered * centered, axis=-1, keepdims=True)
    return centered * lax.rsqrt(var + eps) * gain + shift


def gelu_exact(v):
    return jax.nn.gelu(v, approximate=False)


def dot(left, right, ldim=1, rdim=0):
    return lax.dot_general(
        left, right, (((ldim,), (rdim,)), ((), ())), preferred_element_type=f32
    )


def swap(v, axis, bit):
    n = lax.axis_size(axis)
    return lax.ppermute(v, axis, [(i, i ^ bit) for i in range(n)])


def pick(v, index, axis=0):
    return lax.dynamic_index_in_dim(v, index, axis, keepdims=False)


def ordered(bit, own, other):
    return jnp.where(bit == 0, jnp.stack([own, other]), jnp.stack([other, own]))


def slot_of(t, m, g, members):
    shift = members.bit_length() - 1
    return jnp.bitwise_xor(jnp.bitwise_and(t, members - 1), m) * NG + jnp.bitwise_xor(
        jnp.right_shift(t, shift), g
    )


def fwd_kernel(members, block, scal, st_ref, en_ref, q_ref, *rest):
    kv_refs = rest[:members]
    o_ref, ob_ref, lse_ref, k_scr, v_scr = rest[members:]
    m_id, g_id = scal[0], scal[1]
    cols = NG * block
    for s in range(members):
        for h in range(HG):
            k_scr[h, s * cols : (s + 1) * cols, :] = kv_refs[s][h * HD : (h + 1) * HD, :].T
        v_scr[:, s * cols : (s + 1) * cols] = kv_refs[s][GW:, :]
    for j in range(NG):
        qs = slice(j * block, (j + 1) * block)
        start = st_ref[:, qs]
        end = en_ref[:, qs]
        qts = [q_ref[h * HD : (h + 1) * HD, qs] for h in range(HG)]

        def step(t, carry, start=start, end=end, qts=qts):
            off = pl.multiple_of(slot_of(t, m_id, g_id, members) * block, block)
            kpos = t * block + lax.broadcasted_iota(jnp.int32, (block, block), 0)
            allowed = (kpos >= start) & (kpos < end)
            out = []
            for h in range(HG):
                top, total, acc = carry[h]
                s = dot(k_scr[h, pl.ds(off, block), :], qts[h]) * (SCALE * LOG2E)
                s = jnp.where(allowed, s, NEG)
                new = jnp.maximum(top, jnp.max(s, axis=0, keepdims=True))
                alpha = jnp.exp2(top - new)
                p = jnp.exp2(s - new)
                total = total * alpha + jnp.sum(p, axis=0, keepdims=True)
                acc = acc * alpha + dot(
                    v_scr[h * HD : (h + 1) * HD, pl.ds(off, block)], p.astype(bf16)
                )
                out.append((new, total, acc))
            return tuple(out)

        init = tuple(
            (
                jnp.full((1, block), NEG, f32),
                jnp.zeros((1, block), f32),
                jnp.zeros((HD, block), f32),
            )
            for _ in range(HG)
        )
        done = lax.fori_loop(scal[2 + j], scal[2 + NG + j], step, init)
        for h in range(HG):
            top, total, acc = done[h]
            o = acc / total
            o_ref[h * HD : (h + 1) * HD, qs] = o
            ob_ref[h * HD : (h + 1) * HD, qs] = o.astype(bf16)
            lse_ref[h : h + 1, qs] = top + jnp.log2(total)


def bwd_kernel(members, block, scal, st_ref, en_ref, q_ref, o_ref, lse_ref, do_ref, *rest):
    kv_refs = rest[:members]
    dq_ref, dkv_ref, k_scr, v_scr, kt_scr, dk_scr, dv_scr = rest[members:]
    m_id, g_id = scal[0], scal[1]
    cols = NG * block
    for s in range(members):
        part = slice(s * cols, (s + 1) * cols)
        for h in range(HG):
            k_scr[h, part, :] = kv_refs[s][h * HD : (h + 1) * HD, :].T
            v_scr[h, part, :] = kv_refs[s][GW + h * HD : GW + (h + 1) * HD, :].T
        kt_scr[:, part] = kv_refs[s][:GW, :]
    dk_scr[...] = jnp.zeros_like(dk_scr)
    dv_scr[...] = jnp.zeros_like(dv_scr)
    for j in range(NG):
        qs = slice(j * block, (j + 1) * block)
        start = st_ref[:, qs]
        end = en_ref[:, qs]
        per_head = []
        for h in range(HG):
            hr = slice(h * HD, (h + 1) * HD)
            qt = q_ref[hr, qs]
            dot_t = do_ref[hr, qs]
            delta = jnp.sum(dot_t.astype(f32) * o_ref[hr, qs], axis=0, keepdims=True)
            per_head.append((qt, qt.T, dot_t, dot_t.T, delta, lse_ref[h : h + 1, qs]))

        def step(t, carry, start=start, end=end, per_head=per_head):
            off = pl.multiple_of(slot_of(t, m_id, g_id, members) * block, block)
            kpos = t * block + lax.broadcasted_iota(jnp.int32, (block, block), 0)
            allowed = (kpos >= start) & (kpos < end)
            out = []
            for h in range(HG):
                qt, q, dot_t, do, delta, lse = per_head[h]
                s = dot(k_scr[h, pl.ds(off, block), :], qt) * (SCALE * LOG2E)
                p = jnp.where(allowed, jnp.exp2(s - lse), 0.0)
                dp = dot(v_scr[h, pl.ds(off, block), :], dot_t)
                ds = (p * (dp - delta)).astype(bf16)
                dv_scr[h, pl.ds(off, block), :] += dot(p.astype(bf16), do)
                dk_scr[h, pl.ds(off, block), :] += dot(ds, q)
                out.append(
                    carry[h] + dot(kt_scr[h * HD : (h + 1) * HD, pl.ds(off, block)], ds)
                )
            return tuple(out)

        init = tuple(jnp.zeros((HD, block), f32) for _ in range(HG))
        done = lax.fori_loop(scal[2 + j], scal[2 + NG + j], step, init)
        for h in range(HG):
            dq_ref[h * HD : (h + 1) * HD, qs] = (done[h] * SCALE).astype(bf16)
    for s in range(members):
        part = slice(s * cols, (s + 1) * cols)
        for h in range(HG):
            dkv_ref[s, h * HD : (h + 1) * HD, :] = (dk_scr[h, part, :] * SCALE).T.astype(bf16)
            dkv_ref[s, GW + h * HD : GW + (h + 1) * HD, :] = dv_scr[h, part, :].T.astype(bf16)


def whole_specs(n):
    return [pl.BlockSpec(memory_space=pltpu.SMEM)] + [
        pl.BlockSpec(memory_space=pltpu.VMEM) for _ in range(n)
    ]


def attend(members, block, scal, starts, ends, q, kvs):
    keys = members * NG * block
    rows = NG * block
    return pl.pallas_call(
        functools.partial(fwd_kernel, members, block),
        out_shape=(
            jax.ShapeDtypeStruct((GW, rows), f32),
            jax.ShapeDtypeStruct((GW, rows), bf16),
            jax.ShapeDtypeStruct((HG, rows), f32),
        ),
        in_specs=whole_specs(3 + members),
        out_specs=[pl.BlockSpec(memory_space=pltpu.VMEM) for _ in range(3)],
        scratch_shapes=[
            pltpu.VMEM((HG, keys, HD), bf16),
            pltpu.VMEM((GW, keys), bf16),
        ],
        compiler_params=pltpu.CompilerParams(vmem_limit_bytes=50 << 20),
        name="attend",
    )(scal, starts, ends, q, *kvs)


def attend_back(members, block, scal, starts, ends, q, o, lse, do, kvs):
    keys = members * NG * block
    rows = NG * block
    return pl.pallas_call(
        functools.partial(bwd_kernel, members, block),
        out_shape=(
            jax.ShapeDtypeStruct((GW, rows), bf16),
            jax.ShapeDtypeStruct((members, 2 * GW, rows), bf16),
        ),
        in_specs=whole_specs(6 + members),
        out_specs=[pl.BlockSpec(memory_space=pltpu.VMEM) for _ in range(2)],
        scratch_shapes=[
            pltpu.VMEM((HG, keys, HD), bf16),
            pltpu.VMEM((HG, keys, HD), bf16),
            pltpu.VMEM((GW, keys), bf16),
            pltpu.VMEM((HG, keys, HD), f32),
            pltpu.VMEM((HG, keys, HD), f32),
        ],
        compiler_params=pltpu.CompilerParams(vmem_limit_bytes=56 << 20),
        name="attend_back",
    )(scal, starts, ends, q, o, lse, do, *kvs)


def on_device(
    tokens,
    query_weight,
    query_bias,
    key_weight,
    value_weight,
    value_bias,
    out_weight,
    out_bias,
    first_gain,
    first_shift,
    inner_weight,
    inner_bias,
    outer_weight,
    outer_bias,
    second_gain,
    second_shift,
    doc_lengths,
    grad_output,
):
    block = tokens.shape[1]
    width = tokens.shape[2]
    ctx = lax.axis_size("ctx")
    fs = lax.axis_size("fsdp")
    members = ctx // NG
    ci = lax.axis_index("ctx")
    fi = lax.axis_index("fsdp")
    g_id = ci // members
    m_id = ci % members
    core = ci % 2
    own_rows = width // fs
    m_bits = []
    b = members // 2
    while b >= 1:
        m_bits.append(b)
        b //= 2
    g_slots = range(NG)

    def bit_of(index, bit):
        return (index // bit) % 2

    def gather_rows(w):
        rows = w.shape[0]
        if fs != 2:
            return lax.all_gather(w, "fsdp", axis=0, tiled=True)
        half = rows // 2
        mine = swap(lax.dynamic_slice_in_dim(w, core * half, half, 0), "fsdp", 1)
        others = swap(mine, "ctx", 1)
        other = ordered(core, mine, others).reshape(w.shape)
        return ordered(fi, w, other).reshape((2 * rows,) + w.shape[1:])

    local = tokens[0]
    x_slots = {0: local}
    x_slots[2] = swap(local, "ctx", 2 * members)
    x_slots[1] = swap(local, "ctx", members)
    x_slots[3] = swap(x_slots[2], "ctx", members)
    x_all = jnp.concatenate([x_slots[j] for j in g_slots], axis=0)

    vectors = [
        query_bias,
        value_bias,
        out_bias,
        first_gain,
        first_shift,
        inner_bias,
        outer_bias,
        second_gain,
        second_shift,
    ]
    sizes = [v.shape[0] for v in vectors]
    packed = lax.all_gather(jnp.concatenate(vectors), "fsdp", axis=0, tiled=False)
    at = 0
    full = []
    for n in sizes:
        full.append(packed[:, at : at + n].reshape(-1).astype(f32))
        at += n
    qbias, vbias, obias, gain_one, shift_one, ibias, outbias, gain_two, shift_two = full

    group_cols = [
        lax.dynamic_slice_in_dim(w, g_id * GW, GW, 1)
        for w in (query_weight, key_weight, value_weight)
    ]
    w_group = lax.all_gather(
        jnp.concatenate(group_cols, axis=1), "fsdp", axis=0, tiled=True
    ) if fs != 2 else None
    if fs == 2:
        mine = jnp.concatenate(group_cols, axis=1)
        w_group = ordered(fi, mine, swap(mine, "fsdp", 1)).reshape(width, 3 * GW)
    out_full = gather_rows(out_weight)
    inner_full = gather_rows(inner_weight)
    outer_full = gather_rows(outer_weight)
    qkv_full = gather_rows(jnp.concatenate([query_weight, key_weight, value_weight], axis=1))

    bias_group = jnp.concatenate(
        [
            lax.dynamic_slice_in_dim(qbias, g_id * GW, GW, 0),
            jnp.zeros((GW,), f32),
            lax.dynamic_slice_in_dim(vbias, g_id * GW, GW, 0),
        ]
    )
    qkv = (dot(w_group, x_all, 0, 1) + bias_group[:, None]).astype(bf16)
    q_t = qkv[:GW]
    kv_slots = {0: qkv[GW:]}
    for b in m_bits:
        for s in sorted(kv_slots):
            kv_slots[s ^ b] = swap(kv_slots[s], "ctx", b)
    kvs = [kv_slots[s] for s in range(members)]

    doc_ends = jnp.cumsum(doc_lengths[0])
    first = jnp.stack([(jnp.bitwise_xor(g_id, j) * members + m_id) * block for j in g_slots])
    places = (first[:, None] + jnp.arange(block, dtype=jnp.int32)[None, :]).reshape(-1)
    before = places[:, None] >= doc_ends[None, :]
    starts = jnp.max(jnp.where(before, doc_ends[None, :], 0), axis=1).astype(jnp.int32)
    ends = jnp.min(jnp.where(before, ctx * block, doc_ends[None, :]), axis=1).astype(jnp.int32)
    low = starts.reshape(NG, block)[:, 0] // block
    high = (ends.reshape(NG, block)[:, -1] + block - 1) // block
    scal = jnp.concatenate([jnp.stack([m_id, g_id]), low, high]).astype(jnp.int32)
    starts = starts[None]
    ends = ends[None]

    o_t, ob_t, lse = attend(members, block, scal, starts, ends, q_t, kvs)

    def column(v, j):
        return v[:, j * block : (j + 1) * block]

    def exchange(parts):
        return [parts[0]] + [swap(parts[j], "ctx", j * members) for j in range(1, NG)]

    def by_group(slots):
        return [
            lax.select_n(g_id, *[slots[a ^ k] for k in g_slots]) for a in g_slots
        ]

    attn_t = jnp.concatenate(by_group(exchange([column(ob_t, j) for j in g_slots])), axis=0)
    branch = dot(attn_t, out_full, 0, 0) + obias
    local_float = local.astype(f32)
    hidden, first_back = jax.vjp(layer_norm, local_float + branch, gain_one, shift_one)
    hidden_low = hidden.astype(bf16)
    inner = dot(hidden_low, inner_full) + ibias
    active, gelu_back = jax.vjp(gelu_exact, inner)
    active_low = active.astype(bf16)
    outer = dot(active_low, outer_full) + outbias
    result, second_back = jax.vjp(layer_norm, hidden + outer, gain_two, shift_two)
    output = result.astype(bf16)[None]
    grad_y = grad_output[0].astype(f32)
    d_second, grad_gain_two, grad_shift_two = second_back(grad_y)
    d_outer_low = d_second.astype(bf16)
    grad_outbias = jnp.sum(d_outer_low.astype(f32), axis=0)
    (d_inner,) = gelu_back(dot(d_outer_low, outer_full, 1, 1))
    d_inner_low = d_inner.astype(bf16)
    grad_ibias = jnp.sum(d_inner_low.astype(f32), axis=0)
    d_hidden = d_second + dot(d_inner_low, inner_full, 1, 1)
    d_first, grad_gain_one, grad_shift_one = first_back(d_hidden)
    d_branch_low = d_first.astype(bf16)
    grad_obias = jnp.sum(d_branch_low.astype(f32), axis=0)
    do_t = dot(out_full, d_branch_low, 1, 1).astype(bf16).reshape(NG, GW, block)
    do_parts = [pick(do_t, jnp.bitwise_xor(g_id, j)) for j in g_slots]
    do_all = jnp.concatenate(exchange(do_parts), axis=1)

    def halve(acc, axis, bit, index):
        acc = acc.reshape((2, acc.shape[0] // 2) + acc.shape[1:])
        mine = bit_of(index, bit)
        got = swap(pick(acc, 1 - mine), axis, bit)
        return (pick(acc, mine).astype(f32) + got.astype(f32)).astype(bf16)

    def reduce_rows(product, left, bits):
        rows = left.shape[0] // (2 * fs)
        split = left.reshape(fs, 2, rows, left.shape[1])
        send = product(pick(split, 1 - core, 1).reshape(fs * rows, -1)).astype(bf16)
        keep = product(pick(split, core, 1).reshape(fs * rows, -1))
        acc = (keep + swap(send, "ctx", 1).astype(f32)).astype(bf16)
        n = fs
        while n > 1:
            n //= 2
            acc = halve(acc, "fsdp", n, fi)
        for b in bits:
            acc = halve(acc, "ctx", b, ci)
        return acc

    def join(acc, bit):
        both = ordered(bit_of(ci, bit), acc, swap(acc, "ctx", bit))
        return both.reshape((2 * acc.shape[0],) + acc.shape[1:])

    x_bits = [b for b in m_bits if b > 1]
    all_bits = x_bits + [members, 2 * members]

    def weight_grad(left_t, right, rdim=0):
        acc = reduce_rows(lambda part: dot(part, right, 1, rdim), left_t, all_bits)
        for b in all_bits[::-1]:
            acc = join(acc, b)
        return join(acc, 1).astype(f32)

    grad_outer = weight_grad(active_low.T, d_outer_low)
    grad_inner = weight_grad(hidden_low.T, d_inner_low)
    grad_out = weight_grad(attn_t, d_branch_low)

    dq_t, dkv = attend_back(members, block, scal, starts, ends, q_t, o_t, lse, do_all, kvs)
    dkv_slots = {s: dkv[s] for s in range(members)}
    for b in m_bits[::-1]:
        for s in sorted(dkv_slots):
            if s & b:
                got = swap(dkv_slots.pop(s), "ctx", b)
                dkv_slots[s ^ b] = (dkv_slots[s ^ b].astype(f32) + got.astype(f32)).astype(bf16)
    d_qkv = jnp.concatenate([dq_t, dkv_slots[0]], axis=0)
    back = by_group(exchange([column(d_qkv, j) for j in g_slots]))
    d_all = jnp.stack(back).reshape(NG, 3, GW, block).transpose(1, 0, 2, 3).reshape(3 * width, block)
    grad_input = d_first + dot(d_all, qkv_full, 0, 1)

    acc = reduce_rows(lambda part: dot(part, d_qkv, 1, 1), x_all.T, x_bits)
    acc = ordered(bit_of(ci, 2 * members), acc, swap(acc, "ctx", 2 * members))
    acc = ordered(bit_of(ci, members), acc, swap(acc, "ctx", members))
    lead = []
    for b in x_bits[::-1] + [1]:
        acc = ordered(bit_of(ci, b), acc, swap(acc, "ctx", b))
        lead.append(2)
    nb = len(lead)
    acc = acc.astype(f32)
    order = tuple(range(nb)) + (nb + 2, nb + 1, nb, nb + 3)
    acc = acc.transpose(order).reshape(own_rows, NG, 3, GW).transpose(2, 0, 1, 3)
    grad_query, grad_key, grad_value = acc.reshape(3, own_rows, width)

    group_sums = jnp.sum(d_qkv.astype(f32), axis=1)
    spread = (jnp.arange(NG) == g_id)[:, None]
    grad_qbias = jnp.where(spread, group_sums[None, :GW], 0.0).reshape(-1)
    grad_vbias = jnp.where(spread, group_sums[None, 2 * GW :], 0.0).reshape(-1)
    terms = [
        grad_qbias,
        grad_vbias,
        grad_obias,
        grad_gain_one,
        grad_shift_one,
        grad_ibias,
        grad_outbias,
        grad_gain_two,
        grad_shift_two,
    ]
    summed = lax.psum(jnp.concatenate([t.reshape(fs, -1) for t in terms], axis=1), ("fsdp", "ctx"))
    mine = pick(summed, fi)
    shares = []
    at = 0
    for n in sizes:
        shares.append(mine[at : at + n])
        at += n
    s_q, s_v, s_o, s_g1, s_s1, s_i, s_out, s_g2, s_s2 = shares
    return (
        output,
        grad_input[None],
        grad_query,
        s_q,
        grad_key,
        grad_value,
        s_v,
        grad_out,
        s_o,
        s_g1,
        s_s1,
        grad_inner,
        s_i,
        grad_outer,
        s_out,
        s_g2,
        s_s2,
    )


def solution(mesh):
    placed = (
        P("fsdp", "ctx", None),
        P("fsdp", None),
        P("fsdp"),
        P("fsdp", None),
        P("fsdp", None),
        P("fsdp"),
        P("fsdp", None),
        P("fsdp"),
        P("fsdp"),
        P("fsdp"),
        P("fsdp", None),
        P("fsdp"),
        P("fsdp", None),
        P("fsdp"),
        P("fsdp"),
        P("fsdp"),
        P("fsdp", None),
        P("fsdp", "ctx", None),
    )
    return jax.shard_map(
        on_device,
        mesh=mesh,
        in_specs=placed,
        out_specs=(
            P("fsdp", "ctx", None),
            P("fsdp", "ctx", None),
            P("fsdp", None),
            P("fsdp"),
            P("fsdp", None),
            P("fsdp", None),
            P("fsdp"),
            P("fsdp", None),
            P("fsdp"),
            P("fsdp"),
            P("fsdp"),
            P("fsdp", None),
            P("fsdp"),
            P("fsdp", None),
            P("fsdp"),
            P("fsdp"),
            P("fsdp"),
        ),
        check_vma=False,
    )
```

```python
import functools
import math

import jax
import jax.numpy as jnp
from jax import lax
from jax.experimental import pallas as pl
from jax.experimental.pallas import tpu as pltpu
from jax.sharding import PartitionSpec as P

H = 12
HD = 64
NG = 4
HG = H // NG
GW = HG * HD

eps = 1e-12
NEG = -1e30
LOG2E = 1.4426950408889634
SCALE = 1.0 / math.sqrt(HD)
bf16 = jnp.bfloat16
f32 = jnp.float32


def layer_norm(r, gain, shift):
    mean = jnp.mean(r, axis=-1, keepdims=True)
    centered = r - mean
    var = jnp.mean(centered * centered, axis=-1, keepdims=True)
    return centered * lax.rsqrt(var + eps) * gain + shift


def gelu_exact(v):
    return jax.nn.gelu(v, approximate=False)


def dot(left, right, ldim=1, rdim=0):
    return lax.dot_general(
        left, right, (((ldim,), (rdim,)), ((), ())), preferred_element_type=f32
    )


def swap(v, axis, bit):
    n = lax.axis_size(axis)
    return lax.ppermute(v, axis, [(i, i ^ bit) for i in range(n)])


def pick(v, index, axis=0):
    return lax.dynamic_index_in_dim(v, index, axis, keepdims=False)


def ordered(bit, own, other):
    return jnp.where(bit == 0, jnp.stack([own, other]), jnp.stack([other, own]))


def slot_of(t, m, g, members):
    shift = members.bit_length() - 1
    return jnp.bitwise_xor(jnp.bitwise_and(t, members - 1), m) * NG + jnp.bitwise_xor(
        jnp.right_shift(t, shift), g
    )


def fwd_kernel(members, block, scal, st_ref, en_ref, q_ref, *rest):
    kv_refs = rest[:members]
    o_ref, ob_ref, lse_ref, k_scr, v_scr = rest[members:]
    m_id, g_id = scal[0], scal[1]
    cols = NG * block
    for s in range(members):
        for h in range(HG):
            k_scr[h, s * cols : (s + 1) * cols, :] = kv_refs[s][h * HD : (h + 1) * HD, :].T
        v_scr[:, s * cols : (s + 1) * cols] = kv_refs[s][GW:, :]
    for j in range(NG):
        qs = slice(j * block, (j + 1) * block)
        start = st_ref[:, qs]
        end = en_ref[:, qs]
        qts = [q_ref[h * HD : (h + 1) * HD, qs] for h in range(HG)]

        def step(t, carry, start=start, end=end, qts=qts):
            off = pl.multiple_of(slot_of(t, m_id, g_id, members) * block, block)
            kpos = t * block + lax.broadcasted_iota(jnp.int32, (block, block), 0)
            allowed = (kpos >= start) & (kpos < end)
            out = []
            for h in range(HG):
                top, total, acc = carry[h]
                s = dot(k_scr[h, pl.ds(off, block), :], qts[h]) * (SCALE * LOG2E)
                s = jnp.where(allowed, s, NEG)
                new = jnp.maximum(top, jnp.max(s, axis=0, keepdims=True))
                alpha = jnp.exp2(top - new)
                p = jnp.exp2(s - new)
                total = total * alpha + jnp.sum(p, axis=0, keepdims=True)
                acc = acc * alpha + dot(
                    v_scr[h * HD : (h + 1) * HD, pl.ds(off, block)], p.astype(bf16)
                )
                out.append((new, total, acc))
            return tuple(out)

        init = tuple(
            (
                jnp.full((1, block), NEG, f32),
                jnp.zeros((1, block), f32),
                jnp.zeros((HD, block), f32),
            )
            for _ in range(HG)
        )
        done = lax.fori_loop(scal[2 + j], scal[2 + NG + j], step, init)
        for h in range(HG):
            top, total, acc = done[h]
            o = acc / total
            o_ref[h * HD : (h + 1) * HD, qs] = o
            ob_ref[h * HD : (h + 1) * HD, qs] = o.astype(bf16)
            lse_ref[h : h + 1, qs] = top + jnp.log2(total)


def bwd_kernel(members, block, scal, st_ref, en_ref, q_ref, o_ref, lse_ref, do_ref, *rest):
    kv_refs = rest[:members]
    dq_ref, dkv_ref, k_scr, v_scr, kt_scr, dk_scr, dv_scr = rest[members:]
    m_id, g_id = scal[0], scal[1]
    cols = NG * block
    for s in range(members):
        part = slice(s * cols, (s + 1) * cols)
        for h in range(HG):
            k_scr[h, part, :] = kv_refs[s][h * HD : (h + 1) * HD, :].T
            v_scr[h, part, :] = kv_refs[s][GW + h * HD : GW + (h + 1) * HD, :].T
        kt_scr[:, part] = kv_refs[s][:GW, :]
    dk_scr[...] = jnp.zeros_like(dk_scr)
    dv_scr[...] = jnp.zeros_like(dv_scr)
    for j in range(NG):
        qs = slice(j * block, (j + 1) * block)
        start = st_ref[:, qs]
        end = en_ref[:, qs]
        per_head = []
        for h in range(HG):
            hr = slice(h * HD, (h + 1) * HD)
            qt = q_ref[hr, qs]
            dot_t = do_ref[hr, qs]
            delta = jnp.sum(dot_t.astype(f32) * o_ref[hr, qs], axis=0, keepdims=True)
            per_head.append((qt, qt.T, dot_t, dot_t.T, delta, lse_ref[h : h + 1, qs]))

        def step(t, carry, start=start, end=end, per_head=per_head):
            off = pl.multiple_of(slot_of(t, m_id, g_id, members) * block, block)
            kpos = t * block + lax.broadcasted_iota(jnp.int32, (block, block), 0)
            allowed = (kpos >= start) & (kpos < end)
            out = []
            for h in range(HG):
                qt, q, dot_t, do, delta, lse = per_head[h]
                s = dot(k_scr[h, pl.ds(off, block), :], qt) * (SCALE * LOG2E)
                p = jnp.where(allowed, jnp.exp2(s - lse), 0.0)
                dp = dot(v_scr[h, pl.ds(off, block), :], dot_t)
                ds = (p * (dp - delta)).astype(bf16)
                dv_scr[h, pl.ds(off, block), :] += dot(p.astype(bf16), do)
                dk_scr[h, pl.ds(off, block), :] += dot(ds, q)
                out.append(
                    carry[h] + dot(kt_scr[h * HD : (h + 1) * HD, pl.ds(off, block)], ds)
                )
            return tuple(out)

        init = tuple(jnp.zeros((HD, block), f32) for _ in range(HG))
        done = lax.fori_loop(scal[2 + j], scal[2 + NG + j], step, init)
        for h in range(HG):
            dq_ref[h * HD : (h + 1) * HD, qs] = (done[h] * SCALE).astype(bf16)
    for s in range(members):
        part = slice(s * cols, (s + 1) * cols)
        for h in range(HG):
            dkv_ref[s, h * HD : (h + 1) * HD, :] = (dk_scr[h, part, :] * SCALE).T.astype(bf16)
            dkv_ref[s, GW + h * HD : GW + (h + 1) * HD, :] = dv_scr[h, part, :].T.astype(bf16)


def whole_specs(n):
    return [pl.BlockSpec(memory_space=pltpu.SMEM)] + [
        pl.BlockSpec(memory_space=pltpu.VMEM) for _ in range(n)
    ]


def attend(members, block, scal, starts, ends, q, kvs):
    keys = members * NG * block
    rows = NG * block
    return pl.pallas_call(
        functools.partial(fwd_kernel, members, block),
        out_shape=(
            jax.ShapeDtypeStruct((GW, rows), f32),
            jax.ShapeDtypeStruct((GW, rows), bf16),
            jax.ShapeDtypeStruct((HG, rows), f32),
        ),
        in_specs=whole_specs(3 + members),
        out_specs=[pl.BlockSpec(memory_space=pltpu.VMEM) for _ in range(3)],
        scratch_shapes=[
            pltpu.VMEM((HG, keys, HD), bf16),
            pltpu.VMEM((GW, keys), bf16),
        ],
        compiler_params=pltpu.CompilerParams(vmem_limit_bytes=50 << 20),
        name="attend",
    )(scal, starts, ends, q, *kvs)


def attend_back(members, block, scal, starts, ends, q, o, lse, do, kvs):
    keys = members * NG * block
    rows = NG * block
    return pl.pallas_call(
        functools.partial(bwd_kernel, members, block),
        out_shape=(
            jax.ShapeDtypeStruct((GW, rows), bf16),
            jax.ShapeDtypeStruct((members, 2 * GW, rows), bf16),
        ),
        in_specs=whole_specs(6 + members),
        out_specs=[pl.BlockSpec(memory_space=pltpu.VMEM) for _ in range(2)],
        scratch_shapes=[
            pltpu.VMEM((HG, keys, HD), bf16),
            pltpu.VMEM((HG, keys, HD), bf16),
            pltpu.VMEM((GW, keys), bf16),
            pltpu.VMEM((HG, keys, HD), f32),
            pltpu.VMEM((HG, keys, HD), f32),
        ],
        compiler_params=pltpu.CompilerParams(vmem_limit_bytes=56 << 20),
        name="attend_back",
    )(scal, starts, ends, q, o, lse, do, *kvs)


def on_device(
    tokens,
    query_weight,
    query_bias,
    key_weight,
    value_weight,
    value_bias,
    out_weight,
    out_bias,
    first_gain,
    first_shift,
    inner_weight,
    inner_bias,
    outer_weight,
    outer_bias,
    second_gain,
    second_shift,
    doc_lengths,
    grad_output,
):
    block = tokens.shape[1]
    width = tokens.shape[2]
    ctx = lax.axis_size("ctx")
    fs = lax.axis_size("fsdp")
    members = ctx // NG
    ci = lax.axis_index("ctx")
    fi = lax.axis_index("fsdp")
    g_id = ci // members
    m_id = ci % members
    core = ci % 2
    own_rows = width // fs
    m_bits = []
    b = members // 2
    while b >= 1:
        m_bits.append(b)
        b //= 2
    g_slots = range(NG)

    def bit_of(index, bit):
        return (index // bit) % 2

    def gather_rows(w):
        rows = w.shape[0]
        if fs != 2:
            return lax.all_gather(w, "fsdp", axis=0, tiled=True)
        half = rows // 2
        mine = swap(lax.dynamic_slice_in_dim(w, core * half, half, 0), "fsdp", 1)
        others = swap(mine, "ctx", 1)
        other = ordered(core, mine, others).reshape(w.shape)
        return ordered(fi, w, other).reshape((2 * rows,) + w.shape[1:])

    local = tokens[0]
    x_slots = {0: local}
    x_slots[2] = swap(local, "ctx", 2 * members)
    x_slots[1] = swap(local, "ctx", members)
    x_slots[3] = swap(x_slots[2], "ctx", members)
    x_all = jnp.concatenate([x_slots[j] for j in g_slots], axis=0)

    vectors = [
        query_bias,
        value_bias,
        out_bias,
        first_gain,
        first_shift,
        inner_bias,
        outer_bias,
        second_gain,
        second_shift,
    ]
    sizes = [v.shape[0] for v in vectors]
    packed = lax.all_gather(jnp.concatenate(vectors), "fsdp", axis=0, tiled=False)
    at = 0
    full = []
    for n in sizes:
        full.append(packed[:, at : at + n].reshape(-1).astype(f32))
        at += n
    qbias, vbias, obias, gain_one, shift_one, ibias, outbias, gain_two, shift_two = full

    group_cols = [
        lax.dynamic_slice_in_dim(w, g_id * GW, GW, 1)
        for w in (query_weight, key_weight, value_weight)
    ]
    w_group = lax.all_gather(
        jnp.concatenate(group_cols, axis=1), "fsdp", axis=0, tiled=True
    ) if fs != 2 else None
    if fs == 2:
        mine = jnp.concatenate(group_cols, axis=1)
        w_group = ordered(fi, mine, swap(mine, "fsdp", 1)).reshape(width, 3 * GW)
    out_full = gather_rows(out_weight)
    inner_full = gather_rows(inner_weight)
    outer_full = gather_rows(outer_weight)
    qkv_full = gather_rows(jnp.concatenate([query_weight, key_weight, value_weight], axis=1))

    bias_group = jnp.concatenate(
        [
            lax.dynamic_slice_in_dim(qbias, g_id * GW, GW, 0),
            jnp.zeros((GW,), f32),
            lax.dynamic_slice_in_dim(vbias, g_id * GW, GW, 0),
        ]
    )
    qkv = (dot(w_group, x_all, 0, 1) + bias_group[:, None]).astype(bf16)
    q_t = qkv[:GW]
    kv_slots = {0: qkv[GW:]}
    for b in m_bits:
        for s in sorted(kv_slots):
            kv_slots[s ^ b] = swap(kv_slots[s], "ctx", b)
    kvs = [kv_slots[s] for s in range(members)]

    doc_ends = jnp.cumsum(doc_lengths[0])
    first = jnp.stack([(jnp.bitwise_xor(g_id, j) * members + m_id) * block for j in g_slots])
    places = (first[:, None] + jnp.arange(block, dtype=jnp.int32)[None, :]).reshape(-1)
    before = places[:, None] >= doc_ends[None, :]
    starts = jnp.max(jnp.where(before, doc_ends[None, :], 0), axis=1).astype(jnp.int32)
    ends = jnp.min(jnp.where(before, ctx * block, doc_ends[None, :]), axis=1).astype(jnp.int32)
    low = starts.reshape(NG, block)[:, 0] // block
    high = (ends.reshape(NG, block)[:, -1] + block - 1) // block
    scal = jnp.concatenate([jnp.stack([m_id, g_id]), low, high]).astype(jnp.int32)
    starts = starts[None]
    ends = ends[None]

    o_t, ob_t, lse = attend(members, block, scal, starts, ends, q_t, kvs)

    def column(v, j):
        return v[:, j * block : (j + 1) * block]

    def exchange(parts):
        return [parts[0]] + [swap(parts[j], "ctx", j * members) for j in range(1, NG)]

    def by_group(slots):
        return [
            lax.select_n(g_id, *[slots[a ^ k] for k in g_slots]) for a in g_slots
        ]

    attn_t = jnp.concatenate(by_group(exchange([column(ob_t, j) for j in g_slots])), axis=0)
    branch = dot(attn_t, out_full, 0, 0) + obias
    local_float = local.astype(f32)
    hidden, first_back = jax.vjp(layer_norm, local_float + branch, gain_one, shift_one)
    hidden_low = hidden.astype(bf16)
    inner = dot(hidden_low, inner_full) + ibias
    active, gelu_back = jax.vjp(gelu_exact, inner)
    active_low = active.astype(bf16)
    outer = dot(active_low, outer_full) + outbias
    result, second_back = jax.vjp(layer_norm, hidden + outer, gain_two, shift_two)
    output = result.astype(bf16)[None]
    grad_y = grad_output[0].astype(f32)
    d_second, grad_gain_two, grad_shift_two = second_back(grad_y)
    d_outer_low = d_second.astype(bf16)
    grad_outbias = jnp.sum(d_outer_low.astype(f32), axis=0)
    (d_inner,) = gelu_back(dot(d_outer_low, outer_full, 1, 1))
    d_inner_low = d_inner.astype(bf16)
    grad_ibias = jnp.sum(d_inner_low.astype(f32), axis=0)
    d_hidden = d_second + dot(d_inner_low, inner_full, 1, 1)
    d_first, grad_gain_one, grad_shift_one = first_back(d_hidden)
    d_branch_low = d_first.astype(bf16)
    grad_obias = jnp.sum(d_branch_low.astype(f32), axis=0)
    do_t = dot(out_full, d_branch_low, 1, 1).astype(bf16).reshape(NG, GW, block)
    do_parts = [pick(do_t, jnp.bitwise_xor(g_id, j)) for j in g_slots]
    do_all = jnp.concatenate(exchange(do_parts), axis=1)

    def halve(acc, axis, bit, index):
        acc = acc.reshape((2, acc.shape[0] // 2) + acc.shape[1:])
        mine = bit_of(index, bit)
        got = swap(pick(acc, 1 - mine), axis, bit)
        return (pick(acc, mine).astype(f32) + got.astype(f32)).astype(bf16)

    def reduce_rows(product, left, bits):
        rows = left.shape[0] // (2 * fs)
        split = left.reshape(fs, 2, rows, left.shape[1])
        send = product(pick(split, 1 - core, 1).reshape(fs * rows, -1)).astype(bf16)
        keep = product(pick(split, core, 1).reshape(fs * rows, -1))
        acc = (keep + swap(send, "ctx", 1).astype(f32)).astype(bf16)
        n = fs
        while n > 1:
            n //= 2
            acc = halve(acc, "fsdp", n, fi)
        for b in bits:
            acc = halve(acc, "ctx", b, ci)
        return acc

    def join(acc, bit):
        both = ordered(bit_of(ci, bit), acc, swap(acc, "ctx", bit))
        return both.reshape((2 * acc.shape[0],) + acc.shape[1:])

    x_bits = [b for b in m_bits if b > 1]
    all_bits = x_bits + [members, 2 * members]

    def weight_grad(left_t, right, rdim=0):
        acc = reduce_rows(lambda part: dot(part, right, 1, rdim), left_t, all_bits)
        for b in all_bits[::-1]:
            acc = join(acc, b)
        return join(acc, 1).astype(f32)

    grad_outer = weight_grad(active_low.T, d_outer_low)
    grad_inner = weight_grad(hidden_low.T, d_inner_low)
    grad_out = weight_grad(attn_t, d_branch_low)

    dq_t, dkv = attend_back(members, block, scal, starts, ends, q_t, o_t, lse, do_all, kvs)
    dkv_slots = {s: dkv[s] for s in range(members)}
    for b in m_bits[::-1]:
        for s in sorted(dkv_slots):
            if s & b:
                got = swap(dkv_slots.pop(s), "ctx", b)
                dkv_slots[s ^ b] = (dkv_slots[s ^ b].astype(f32) + got.astype(f32)).astype(bf16)
    d_qkv = jnp.concatenate([dq_t, dkv_slots[0]], axis=0)
    back = by_group(exchange([column(d_qkv, j) for j in g_slots]))
    d_all = jnp.stack(back).reshape(NG, 3, GW, block).transpose(1, 0, 2, 3).reshape(3 * width, block)
    grad_input = d_first + dot(d_all, qkv_full, 0, 1)

    acc = reduce_rows(lambda part: dot(part, d_qkv, 1, 1), x_all.T, x_bits)
    acc = ordered(bit_of(ci, 2 * members), acc, swap(acc, "ctx", 2 * members))
    acc = ordered(bit_of(ci, members), acc, swap(acc, "ctx", members))
    lead = []
    for b in x_bits[::-1] + [1]:
        acc = ordered(bit_of(ci, b), acc, swap(acc, "ctx", b))
        lead.append(2)
    nb = len(lead)
    acc = acc.astype(f32)
    order = tuple(range(nb)) + (nb + 2, nb + 1, nb, nb + 3)
    acc = acc.transpose(order).reshape(own_rows, NG, 3, GW).transpose(2, 0, 1, 3)
    grad_query, grad_key, grad_value = acc.reshape(3, own_rows, width)

    group_sums = jnp.sum(d_qkv.astype(f32), axis=1)
    spread = (jnp.arange(NG) == g_id)[:, None]
    grad_qbias = jnp.where(spread, group_sums[None, :GW], 0.0).reshape(-1)
    grad_vbias = jnp.where(spread, group_sums[None, 2 * GW :], 0.0).reshape(-1)
    terms = [
        grad_qbias,
        grad_vbias,
        grad_obias,
        grad_gain_one,
        grad_shift_one,
        grad_ibias,
        grad_outbias,
        grad_gain_two,
        grad_shift_two,
    ]
    summed = lax.psum(jnp.concatenate([t.reshape(fs, -1) for t in terms], axis=1), ("fsdp", "ctx"))
    mine = pick(summed, fi)
    shares = []
    at = 0
    for n in sizes:
        shares.append(mine[at : at + n])
        at += n
    s_q, s_v, s_o, s_g1, s_s1, s_i, s_out, s_g2, s_s2 = shares
    return (
        output,
        grad_input[None],
        grad_query,
        s_q,
        grad_key,
        grad_value,
        s_v,
        grad_out,
        s_o,
        s_g1,
        s_s1,
        grad_inner,
        s_i,
        grad_outer,
        s_out,
        s_g2,
        s_s2,
    )


def vmem(n):
    return [pl.BlockSpec(memory_space=pltpu.VMEM) for _ in range(n)]


def anyspec(n):
    return [pl.BlockSpec(memory_space=pl.ANY) for _ in range(n)]


CHEAP = pl.CostEstimate(flops=1, transcendentals=0, bytes_accessed=1)
SMEM = pl.BlockSpec(memory_space=pltpu.SMEM)


def params(mib=56):
    return pltpu.CompilerParams(vmem_limit_bytes=mib << 20)


def project_kernel(
    block, scal, x0, x1, x2, x3, own, small, small_oth, mine, sib, q_ref, kv_ref, row_scr, bias_scr, w_scr, sems
):
    g_id, fi, core = scal[0], scal[1], scal[2]
    half = own.shape[0]
    quarter = half // 2
    copies = [
        pltpu.make_async_copy(
            part, w_scr.at[pl.ds(pl.multiple_of(c * quarter, 64), quarter), :], sems.at[k]
        )
        for k, (part, c) in enumerate(((mine, core), (sib, 1 - core)))
    ]
    for c in copies:
        c.start()
    w_own = own[...].T
    at_own = pl.multiple_of(fi * half, 128)
    at_oth = pl.multiple_of((1 - fi) * half, 128)
    row_scr[:, pl.ds(at_own, half)] = small[6:8, :].astype(f32)
    row_scr[:, pl.ds(at_oth, half)] = small_oth[6:8, :].astype(f32)
    bias_scr[...] = jnp.zeros_like(bias_scr)
    for g in range(NG):

        @pl.when(g_id == g)
        def _(g=g):
            bias_scr[0:1, :GW] = row_scr[0:1, g * GW : (g + 1) * GW]
            bias_scr[0:1, 2 * GW :] = row_scr[1:2, g * GW : (g + 1) * GW]

    bias = bias_scr[...].T[:, :1]
    for c in copies:
        c.wait()
    w_oth = w_scr[...].T
    for j, x in enumerate((x0, x1, x2, x3)):
        cols = slice(j * block, (j + 1) * block)
        res = dot(w_own, x[:, pl.ds(at_own, half)], 1, 1)
        res += dot(w_oth, x[:, pl.ds(at_oth, half)], 1, 1)
        res = (res + bias).astype(bf16)
        q_ref[:, cols] = res[:GW]
        kv_ref[:, cols] = res[GW:]


def project(block, scal, xs, own, mine, sib, small, small_oth):
    rows = NG * block
    return pl.pallas_call(
        functools.partial(project_kernel, block),
        out_shape=(
            jax.ShapeDtypeStruct((GW, rows), bf16),
            jax.ShapeDtypeStruct((2 * GW, rows), bf16),
        ),
        in_specs=[SMEM] + vmem(7) + anyspec(2),
        out_specs=vmem(2),
        scratch_shapes=[
            pltpu.VMEM((2, 2 * own.shape[0]), f32),
            pltpu.VMEM((8, 3 * GW), f32),
            pltpu.VMEM(own.shape, bf16),
            pltpu.SemaphoreType.DMA((2,)),
        ],
        cost_estimate=CHEAP,
        compiler_params=params(),
        name="project",
    )(scal, *xs, own, small, small_oth, mine, sib)


def pack_kernel(*refs):
    out = refs[-1]
    n = out.shape[1]
    at = 0
    for ref in refs[:-1]:
        for k in range(ref.shape[0] // n):
            out[at : at + 1, :] = ref[k * n : (k + 1) * n].reshape(1, n)
            at += 1


def pack(vectors):
    n = vectors[0].shape[0]
    rows = sum(v.shape[0] for v in vectors) // n
    return pl.pallas_call(
        pack_kernel,
        out_shape=jax.ShapeDtypeStruct((rows, n), bf16),
        in_specs=vmem(len(vectors)),
        out_specs=vmem(1)[0],
        compiler_params=params(),
        name="pack",
    )(*vectors)


def tile_offset(t, scal, members, block):
    return pl.multiple_of(slot_of(t, scal[0], scal[1], members) * block, block)


UNROLL = 4


def key_loop(scal, j, tiles, init):
    low, high, inner_low, inner_high = (scal[2 + NG * i + j] for i in range(4))
    carry = lax.fori_loop(low, inner_low, lambda t, c: tiles([t], c, True), init)
    many = (inner_high - inner_low) // UNROLL

    def several(i, c):
        return tiles([inner_low + UNROLL * i + u for u in range(UNROLL)], c, False)

    carry = lax.fori_loop(0, many, several, carry)
    carry = lax.fori_loop(
        inner_low + UNROLL * many, inner_high, lambda t, c: tiles([t], c, False), carry
    )
    return lax.fori_loop(inner_high, high, lambda t, c: tiles([t], c, True), carry)


def inside(t, start, end, block):
    kpos = t * block + lax.broadcasted_iota(jnp.int32, (block, block), 0)
    return (kpos >= start) & (kpos < end)


def staged(n, first, second, third):
    one, two = {}, {}
    for i in range(n + 2):
        if i < n:
            one[i] = first(i)
        if 0 <= i - 1 < n:
            two[i - 1] = second(i - 1, one.pop(i - 1))
        if 0 <= i - 2 < n:
            third(i - 2, two.pop(i - 2))


def group_fwd_kernel(members, block, scal, st_ref, en_ref, q_ref, *rest):
    kv_refs = rest[:members]
    o_ref, lse_ref = rest[members : members + 2]
    ob_refs = rest[members + 2 : members + 2 + NG]
    k_scr, v_scr = rest[members + 2 + NG :]
    cols = NG * block
    for s in range(members):
        for h in range(HG):
            k_scr[h, s * cols : (s + 1) * cols, :] = kv_refs[s][h * HD : (h + 1) * HD, :].T
        v_scr[:, s * cols : (s + 1) * cols] = kv_refs[s][GW:, :]
    for j in range(NG):
        cut = slice(j * block, (j + 1) * block)
        start = st_ref[:, cut]
        end = en_ref[:, cut]
        qts = [q_ref[h * HD : (h + 1) * HD, cut] for h in range(HG)]

        def tiles(ts, carry, masked, start=start, end=end, qts=qts):
            offs = [tile_offset(t, scal, members, block) for t in ts]
            allowed = [inside(t, start, end, block) for t in ts] if masked else None
            out = [None] * HG

            def first(h):
                return [dot(k_scr[h, pl.ds(off, block), :], qts[h]) for off in offs]

            def second(h, scores):
                top, total, acc = carry[h]
                if masked:
                    scores = [jnp.where(a, s, NEG) for a, s in zip(allowed, scores)]
                new = top
                for s in scores:
                    new = jnp.maximum(new, jnp.max(s, axis=0, keepdims=True))
                alpha = jnp.exp2((top - new) * (SCALE * LOG2E))
                total = total * alpha
                probs = []
                for s in scores:
                    p = jnp.exp2((s - new) * (SCALE * LOG2E))
                    total += jnp.sum(p, axis=0, keepdims=True)
                    probs.append(p.astype(bf16))
                return probs, new, total, acc * alpha

            def third(h, state):
                probs, new, total, acc = state
                for p, off in zip(probs, offs):
                    acc += dot(v_scr[h * HD : (h + 1) * HD, pl.ds(off, block)], p)
                out[h] = (new, total, acc)

            staged(HG, first, second, third)
            return tuple(out)

        init = tuple(
            (
                jnp.full((1, block), NEG, f32),
                jnp.zeros((1, block), f32),
                jnp.zeros((HD, block), f32),
            )
            for _ in range(HG)
        )
        done = key_loop(scal, j, tiles, init)
        for h in range(HG):
            top, total, acc = done[h]
            o = acc / total
            o_ref[h * HD : (h + 1) * HD, cut] = o
            ob_refs[j][h * HD : (h + 1) * HD, :] = o.astype(bf16)
            lse_ref[h : h + 1, cut] = top * (SCALE * LOG2E) + jnp.log2(total)


def group_fwd(members, block, scal, starts, ends, q, kvs):
    keys = members * NG * block
    rows = NG * block
    return pl.pallas_call(
        functools.partial(group_fwd_kernel, members, block),
        out_shape=(
            jax.ShapeDtypeStruct((GW, rows), f32),
            jax.ShapeDtypeStruct((HG, rows), f32),
        )
        + tuple(jax.ShapeDtypeStruct((GW, block), bf16) for _ in range(NG)),
        in_specs=[SMEM] + vmem(3 + members),
        out_specs=vmem(2 + NG),
        scratch_shapes=[
            pltpu.VMEM((HG, keys, HD), bf16),
            pltpu.VMEM((GW, keys), bf16),
        ],
        cost_estimate=CHEAP,
        compiler_params=params(),
        name="group_fwd",
    )(scal, starts, ends, q, *kvs)


def group_bwd_kernel(members, block, scal, st_ref, en_ref, q_ref, o_ref, lse_ref, *rest):
    do_refs = rest[:NG]
    kv_refs = rest[NG : NG + members]
    dq_ref = rest[NG + members]
    dkv_refs = rest[NG + members + 1 : NG + 2 * members + 1]
    k_scr, v_scr, dk_scr, dv_scr = rest[NG + 2 * members + 1 :]
    cols = NG * block
    heads = [slice(h * HD, (h + 1) * HD) for h in range(HG)]
    for s in range(members):
        part = slice(s * cols, (s + 1) * cols)
        k_scr[:, part] = kv_refs[s][:GW, :]
        v_scr[:, part] = kv_refs[s][GW:, :]
    dk_scr[...] = jnp.zeros_like(dk_scr)
    dv_scr[...] = jnp.zeros_like(dv_scr)
    for j in range(NG):
        cut = slice(j * block, (j + 1) * block)
        start = st_ref[:, cut]
        end = en_ref[:, cut]
        per_head = []
        for h in range(HG):
            do = do_refs[j][heads[h], :]
            delta = jnp.sum(do.astype(f32) * o_ref[heads[h], cut], axis=0, keepdims=True)
            per_head.append((q_ref[heads[h], cut], do, delta, lse_ref[h : h + 1, cut]))

        def tiles(ts, carry, masked, start=start, end=end, per_head=per_head):
            out = list(carry)
            work = []
            for t in ts:
                cols = pl.ds(tile_offset(t, scal, members, block), block)
                allowed = inside(t, start, end, block) if masked else None
                work += [(h, cols, allowed) for h in range(HG)]

            def first(i):
                h, cols, _ = work[i]
                q, do, _, _ = per_head[h]
                return dot(k_scr[heads[h], cols], q, 0, 0), dot(v_scr[heads[h], cols], do, 0, 0)

            def second(i, pair):
                h, _, allowed = work[i]
                _, _, delta, lse = per_head[h]
                s, dp = pair
                p = jnp.exp2(s * (SCALE * LOG2E) - lse)
                if masked:
                    p = jnp.where(allowed, p, 0.0)
                return p.astype(bf16), (p * (dp - delta)).astype(bf16)

            def third(i, pair):
                h, cols, _ = work[i]
                q, do, _, _ = per_head[h]
                p, ds = pair
                dv_scr[heads[h], cols] += dot(do, p, 1, 1)
                dk_scr[heads[h], cols] += dot(q, ds, 1, 1)
                out[h] = out[h] + dot(k_scr[heads[h], cols], ds)

            staged(len(work), first, second, third)
            return tuple(out)

        done = key_loop(scal, j, tiles, tuple(jnp.zeros((HD, block), f32) for _ in range(HG)))
        for h in range(HG):
            dq_ref[heads[h], cut] = (done[h] * SCALE).astype(bf16)
    for s in range(members):
        part = slice(s * cols, (s + 1) * cols)
        dkv_refs[s][:GW, :] = (dk_scr[:, part] * SCALE).astype(bf16)
        dkv_refs[s][GW:, :] = dv_scr[:, part].astype(bf16)


def group_bwd(members, block, scal, starts, ends, q, o, lse, dos, kvs):
    keys = members * NG * block
    rows = NG * block
    return pl.pallas_call(
        functools.partial(group_bwd_kernel, members, block),
        out_shape=(jax.ShapeDtypeStruct((GW, rows), bf16),)
        + tuple(jax.ShapeDtypeStruct((2 * GW, rows), bf16) for _ in range(members)),
        in_specs=[SMEM] + vmem(5 + NG + members),
        out_specs=vmem(1 + members),
        scratch_shapes=[
            pltpu.VMEM((GW, keys), bf16),
            pltpu.VMEM((GW, keys), bf16),
            pltpu.VMEM((GW, keys), f32),
            pltpu.VMEM((GW, keys), f32),
        ],
        cost_estimate=CHEAP,
        compiler_params=params(),
        name="group_bwd",
    )(scal, starts, ends, q, o, lse, *dos, *kvs)


def normalize(r, width):
    mean = jnp.sum(r, axis=1, keepdims=True) * (1.0 / width)
    centered = r - mean
    var = jnp.sum(centered * centered, axis=1, keepdims=True) * (1.0 / width)
    rstd = lax.rsqrt(var + eps)
    return centered * rstd, rstd


def norm_back(dy, hat, rstd, gain, width):
    dhat = dy * gain
    one = jnp.sum(dhat, axis=1, keepdims=True) * (1.0 / width)
    two = jnp.sum(dhat * hat, axis=1, keepdims=True) * (1.0 / width)
    return rstd * (dhat - one - hat * two)


INV_SQRT2 = 0.7071067811865476
INV_SQRT2PI = 0.3989422804014327


def middle_kernel(block, *refs):
    scal = refs[0]
    at = 1
    o_refs = refs[at : at + NG]
    at += NG
    x_ref, dy_ref, small, small_oth = refs[at : at + 4]
    at += 4
    out_parts = refs[at : at + 3]
    inner_parts = refs[at + 3 : at + 8]
    outer_parts = refs[at + 8 : at + 13]
    at += 13
    y_ref, dr_ref, sums_ref = refs[at : at + 3]
    at += 3
    do_refs = refs[at : at + NG]
    at += NG
    keeps = refs[at : at + 2]
    sends = refs[at + 2 : at + 4]
    at += 4
    ot_scr, wout, winner, wouter, hbt, gt_scr, gp_scr, dot_scr, vec_ref, ib_ref, sems = refs[at:]
    g_id, fi, core = scal[0], scal[1], scal[2]
    width = x_ref.shape[1]
    ffq = winner.shape[2]
    half = width // 2
    quarter = width // 4

    copies = []

    def load(src, dst):
        copies.append(pltpu.make_async_copy(src, dst, sems.at[len(copies)]))
        copies[-1].start()

    def rows_of(full):
        own = fi * (full // 2)
        oth = (1 - fi) * (full // 2)
        q = full // 4
        return (
            pl.ds(pl.multiple_of(own, 64), full // 2),
            pl.ds(pl.multiple_of(oth + core * q, 64), q),
            pl.ds(pl.multiple_of(oth + (1 - core) * q, 64), q),
        )

    for part, rows in zip(out_parts, rows_of(width)):
        load(part, wout.at[rows, :])
    own, mine, sib = (r.start for r in rows_of(width))
    unit = width // 16
    inner_rows = [pl.ds(own, 8 * unit)] + [
        pl.ds(pl.multiple_of(first + k * unit, 16), n * unit)
        for first in (mine, sib)
        for k, n in ((0, 1), (1, 3))
    ]
    for a in range(4):
        for part, rows in zip(inner_parts, inner_rows):
            load(part.at[:, a * ffq : (a + 1) * ffq], winner.at[a, rows, :])
    own, mine, sib = (r.start for r in rows_of(4 * ffq))
    unit = ffq // 4
    outer_rows = [pl.ds(own, 8 * unit)] + [
        pl.ds(pl.multiple_of(first + k * unit, 16), n * unit)
        for first in (mine, sib)
        for k, n in ((0, 1), (1, 3))
    ]
    for part, rows in zip(outer_parts, outer_rows):
        load(part, wouter.at[rows, :])

    for j in range(NG):
        row = pl.multiple_of(jnp.bitwise_xor(g_id, j) * GW, HD)
        ot_scr[pl.ds(row, GW), :] = o_refs[j][...]
    for side, y in ((small, fi), (small_oth, 1 - fi)):
        vec_ref[:, pl.ds(pl.multiple_of(y * half, 128), half)] = side[:8, :].astype(f32)
        for c in range(2):
            for k in range(2):
                ib_ref[pl.ds(2 * y + c, 1), k * half : (k + 1) * half] = side[
                    8 + 2 * c + k : 9 + 2 * c + k, :
                ].astype(f32)
    for c in copies[:3]:
        c.wait()
    vec = [vec_ref[i : i + 1, :] for i in range(8)]
    obias, gain1, shift1, outbias, gain2, shift2 = vec[:6]
    attn = ot_scr[...].T
    r1 = x_ref[...].astype(f32) + dot(attn, wout[...]) + obias
    hat1, rstd1 = normalize(r1, width)
    hn = hat1 * gain1 + shift1
    hb = hn.astype(bf16)
    hb_t = hb.T
    for y in range(2):
        for c in range(2):
            piece = hb_t[(2 * y + c) * quarter : (2 * y + c + 1) * quarter]

            @pl.when(core == c)
            def _(piece=piece, y=y):
                hbt[y * quarter : (y + 1) * quarter, :] = piece

            @pl.when(core != c)
            def _(piece=piece, y=y):
                hbt[half + y * quarter : half + (y + 1) * quarter, :] = piece

    for c in copies[3:23]:
        c.wait()
    z = hn + outbias
    for a in range(4):
        u = dot(hb, winner[a]) + ib_ref[a : a + 1, :]
        phi = 0.5 + 0.5 * lax.erf(u * INV_SQRT2)
        g = (u * phi).astype(bf16)
        gp_scr[a] = phi + u * (jnp.exp(u * u * -0.5) * INV_SQRT2PI)
        gt_scr[a] = g.T
        if a == 0:
            for c in copies[23:]:
                c.wait()
        z += dot(g, wouter[a * ffq : (a + 1) * ffq, :])
    hat2, rstd2 = normalize(z, width)
    y_ref[...] = (hat2 * gain2 + shift2).astype(bf16)
    dy = dy_ref[...].astype(f32)
    sums_ref[4:5, :] = jnp.sum(dy * hat2, axis=0, keepdims=True)
    sums_ref[5:6, :] = jnp.sum(dy, axis=0, keepdims=True)
    dz = norm_back(dy, hat2, rstd2, gain2, width)
    dzb = dz.astype(bf16)
    sums_ref[3:4, :] = jnp.sum(dzb.astype(f32), axis=0, keepdims=True)
    dh = dz
    for a in range(4):
        dg = dot(dzb, wouter[a * ffq : (a + 1) * ffq, :], 1, 1)
        du = (dg * gp_scr[a]).astype(bf16)
        sums_ref[6 + a : 7 + a, :] = jnp.sum(du.astype(f32), axis=0, keepdims=True)
        dh += dot(du, winner[a], 1, 1)
        grad = dot(hbt[...], du).astype(bf16)
        for y in range(2):
            rows = slice(a * quarter, (a + 1) * quarter)
            keeps[0][y, rows] = grad[y * quarter : (y + 1) * quarter]
            sends[0][y, rows] = grad[half + y * quarter : half + (y + 1) * quarter]
        grad = dot(gt_scr[a], dzb).astype(bf16)
        for c in range(2):
            if a % 2 != c:
                continue

            @pl.when(core == c)
            def _(grad=grad, a=a):
                keeps[1][a // 2, :ffq] = grad

            @pl.when(core != c)
            def _(grad=grad, a=a):
                sends[1][a // 2, :ffq] = grad

    sums_ref[1:2, :] = jnp.sum(dh * hat1, axis=0, keepdims=True)
    sums_ref[2:3, :] = jnp.sum(dh, axis=0, keepdims=True)
    dr = norm_back(dh, hat1, rstd1, gain1, width)
    dr_ref[...] = dr
    dab = dr.astype(bf16)
    sums_ref[0:1, :] = jnp.sum(dab.astype(f32), axis=0, keepdims=True)
    sums_ref[10:16, :] = jnp.zeros((6, width), f32)
    dot_scr[...] = dot(wout[...], dab, 1, 1).astype(bf16)
    for j in range(NG):
        row = pl.multiple_of(jnp.bitwise_xor(g_id, j) * GW, HD)
        do_refs[j][...] = dot_scr[pl.ds(row, GW), :]
    grad = dot(ot_scr[...], dab).astype(bf16)
    for y in range(2):
        for c in range(2):
            piece = grad[(2 * y + c) * quarter : (2 * y + c + 1) * quarter]

            @pl.when(core == c)
            def _(piece=piece, y=y):
                keeps[1][y, ffq:] = piece

            @pl.when(core != c)
            def _(piece=piece, y=y):
                sends[1][y, ffq:] = piece


def middle(block, scal, os, x, dy, small, small_oth, outs, inners, outers):
    width = x.shape[1]
    ffq = inners[0].shape[1] // 4
    q = width // 4
    grads = [
        jax.ShapeDtypeStruct((2, 4 * q, ffq), bf16),
        jax.ShapeDtypeStruct((2, ffq + q, width), bf16),
    ]
    return pl.pallas_call(
        functools.partial(middle_kernel, block),
        out_shape=(
            jax.ShapeDtypeStruct((block, width), bf16),
            jax.ShapeDtypeStruct((block, width), f32),
            jax.ShapeDtypeStruct((16, width), f32),
        )
        + tuple(jax.ShapeDtypeStruct((GW, block), bf16) for _ in range(NG))
        + tuple(grads)
        + tuple(grads),
        in_specs=[SMEM] + vmem(NG + 4) + anyspec(13),
        out_specs=vmem(3 + NG + 4),
        scratch_shapes=[
            pltpu.VMEM((width, block), bf16),
            pltpu.VMEM((width, width), bf16),
            pltpu.VMEM((4, width, ffq), bf16),
            pltpu.VMEM((4 * ffq, width), bf16),
            pltpu.VMEM((width, block), bf16),
            pltpu.VMEM((4, ffq, block), bf16),
            pltpu.VMEM((4, block, ffq), f32),
            pltpu.VMEM((width, block), bf16),
            pltpu.VMEM((8, width), f32),
            pltpu.VMEM((4, ffq), f32),
            pltpu.SemaphoreType.DMA((28,)),
        ],
        cost_estimate=CHEAP,
        compiler_params=params(60),
        name="middle",
    )(scal, *os, x, dy, small, small_oth, *outs, *inners, *outers)


def turn_kernel(scal, x0, x1, x2, x3, xt):
    core = scal[1]
    block, width = x0.shape
    half, quarter = width // 2, width // 4
    for j, x in enumerate((x0, x1, x2, x3)):
        cols = slice(j * block, (j + 1) * block)
        turned = x[...].T
        for y in range(2):
            for c in range(2):
                piece = turned[(2 * y + c) * quarter : (2 * y + c + 1) * quarter]

                @pl.when(core == c)
                def _(piece=piece, y=y):
                    xt[y * quarter : (y + 1) * quarter, cols] = piece

                @pl.when(core != c)
                def _(piece=piece, y=y):
                    xt[half + y * quarter : half + (y + 1) * quarter, cols] = piece


def turn(scal, xs):
    block, width = xs[0].shape
    return pl.pallas_call(
        turn_kernel,
        out_shape=jax.ShapeDtypeStruct((width, NG * block), bf16),
        in_specs=[SMEM] + vmem(NG),
        out_specs=vmem(1)[0],
        compiler_params=params(),
        name="turn",
    )(scal, *xs)


def qkv_grad_kernel(xt, dq_ref, dkv_ref, keep, send, sums, d_scr):
    d_scr[:GW, :] = dq_ref[...]
    d_scr[GW:, :] = dkv_ref[...]
    d = d_scr[...]
    half = xt.shape[0] // 2
    quarter = half // 2
    grad = dot(xt[...], d, 1, 1).astype(bf16)
    for y in range(2):
        keep[y] = grad[y * quarter : (y + 1) * quarter]
        send[y] = grad[half + y * quarter : half + (y + 1) * quarter]
    sums[...] = dot(jnp.ones((8, d.shape[1]), bf16), d, 1, 1)


def qkv_grad(xt, dq, dkv):
    width, rows = xt.shape
    q = width // 4
    return pl.pallas_call(
        qkv_grad_kernel,
        out_shape=(
            jax.ShapeDtypeStruct((2, q, 3 * GW), bf16),
            jax.ShapeDtypeStruct((2, q, 3 * GW), bf16),
            jax.ShapeDtypeStruct((8, 3 * GW), f32),
        ),
        in_specs=vmem(3),
        out_specs=vmem(3),
        scratch_shapes=[pltpu.VMEM((3 * GW, rows), bf16)],
        compiler_params=params(),
        name="qkv_grad",
    )(xt, dq, dkv)


def input_grad_kernel(scal, dr_ref, *refs):
    d_refs = refs[: 2 * NG]
    parts = refs[2 * NG : 2 * NG + 3]
    out, w_scr, d_scr, sems = refs[2 * NG + 3 :]
    g_id, fi, core = scal[0], scal[1], scal[2]
    width = w_scr.shape[0]
    q = width // 4
    oth = (1 - fi) * 2 * q
    rows = (
        pl.ds(pl.multiple_of(fi * 2 * q, 64), 2 * q),
        pl.ds(pl.multiple_of(oth + core * q, 64), q),
        pl.ds(pl.multiple_of(oth + (1 - core) * q, 64), q),
    )
    copies = [
        pltpu.make_async_copy(p, w_scr.at[r, :], sems.at[i])
        for i, (p, r) in enumerate(zip(parts, rows))
    ]
    for c in copies:
        c.start()
    for j in range(NG):
        base = jnp.bitwise_xor(g_id, j) * GW
        for part in range(3):
            at = pl.multiple_of(part * width + base, HD)
            src = d_refs[j][...] if part == 0 else d_refs[NG + j][(part - 1) * GW : part * GW, :]
            d_scr[pl.ds(at, GW), :] = src
    for c in copies:
        c.wait()
    out[...] = dr_ref[...] + dot(w_scr[...], d_scr[...]).T


def input_grad(scal, dr, ds, parts):
    block, width = dr.shape
    return pl.pallas_call(
        input_grad_kernel,
        out_shape=jax.ShapeDtypeStruct((block, width), f32),
        in_specs=[SMEM] + vmem(1 + 2 * NG) + anyspec(3),
        out_specs=vmem(1)[0],
        scratch_shapes=[
            pltpu.VMEM((width, 3 * width), bf16),
            pltpu.VMEM((3 * width, block), bf16),
            pltpu.SemaphoreType.DMA((3,)),
        ],
        cost_estimate=CHEAP,
        compiler_params=params(),
        name="input_grad",
    )(scal, dr, *ds, *parts)


def each_part(scal, fn):
    xi, core = scal[1], scal[2]
    for c in range(2):
        for x in range(2):
            here = jnp.bitwise_xor(core, c) * 2 + jnp.bitwise_xor(xi, x)
            for s in range(4):
                pl.when(here == s)(functools.partial(fn, c, x, s))


def unpack_kernel(scal, *refs):
    parts, outs = refs[:4], refs[4:]
    rows = parts[0].shape[1]

    def put(c, x, s):
        at = (2 * c + x) * rows
        for g in range(NG):
            v = parts[s][g].astype(f32)
            for part in range(3):
                outs[part][at : at + rows, g * GW : (g + 1) * GW] = v[
                    :, part * GW : (part + 1) * GW
                ]

    each_part(scal, put)


def unpack(scal, parts):
    rows = parts[0].shape[1]
    return pl.pallas_call(
        unpack_kernel,
        out_shape=tuple(jax.ShapeDtypeStruct((4 * rows, NG * GW), f32) for _ in range(3)),
        in_specs=[SMEM] + vmem(4),
        out_specs=vmem(3),
        cost_estimate=CHEAP,
        compiler_params=params(),
        name="unpack",
    )(scal, *parts)


def spread_rows(segments, first, v):
    base = 0
    for n, place in segments:
        lo, hi = max(first, base), min(first + v.shape[0], base + n)
        if lo < hi:
            place(lo - base, v[lo - first : hi - first])
        base += n


def finish_kernel(n_a, n_b, whole, outer_ref, inner_ref, out_ref):
    ffq = inner_ref.shape[1] // 4
    quarter = inner_ref.shape[0] // 2
    for i in range(whole.shape[0]):
        g, x, c = i >> 2, i >> 1 & 1, i & 1

        def outer(row, v, c=c):
            outer_ref[c * ffq + row : c * ffq + row + v.shape[0], :] = v

        def out(row, v, c=c):
            out_ref[c * quarter + row : c * quarter + row + v.shape[0], :] = v

        def inner(a, row, v, c=c):
            at = c * quarter + row
            inner_ref[at : at + v.shape[0], a * ffq : (a + 1) * ffq] = v

        v = whole[i].astype(f32)
        at_a = (NG * x + g) * n_a
        at_b = (NG * x + g) * n_b
        spread_rows(((ffq, outer), (quarter, out)), at_a, v[:n_a])
        spread_rows(
            tuple((quarter, functools.partial(inner, a)) for a in range(4)), at_b, v[n_a:]
        )


def finish(whole, n_a, n_b, shapes):
    return pl.pallas_call(
        functools.partial(finish_kernel, n_a, n_b),
        out_shape=tuple(jax.ShapeDtypeStruct(s, f32) for s in shapes),
        in_specs=vmem(1),
        out_specs=vmem(3),
        cost_estimate=CHEAP,
        compiler_params=params(),
        name="finish",
    )(whole)


def fast_device(
    tokens,
    query_weight,
    query_bias,
    key_weight,
    value_weight,
    value_bias,
    out_weight,
    out_bias,
    first_gain,
    first_shift,
    inner_weight,
    inner_bias,
    outer_weight,
    outer_bias,
    second_gain,
    second_shift,
    doc_lengths,
    grad_output,
):
    block = tokens.shape[1]
    width = tokens.shape[2]
    ctx = lax.axis_size("ctx")
    members = ctx // NG
    ci = lax.axis_index("ctx")
    fi = lax.axis_index("fsdp")
    g_id = ci // members
    m_id = ci % members
    core = ci % 2
    xi = m_id // 2
    half = width // 2
    tie = lax.optimization_barrier

    def zswap(v, j):
        return swap(v, "ctx", j * members)

    def xswap(v):
        return swap(v, "ctx", 2)

    def cswap(v):
        return swap(v, "ctx", 1)

    def yswap(v):
        return swap(v, "fsdp", 1)

    local = tokens[0]
    x2 = zswap(local, 2)
    x1 = zswap(local, 1)
    w_own = jnp.concatenate(
        [
            lax.dynamic_slice_in_dim(w, g_id * GW, GW, 1)
            for w in (query_weight, key_weight, value_weight)
        ],
        axis=1,
    )
    small = pack(
        [
            out_bias,
            first_gain,
            first_shift,
            outer_bias,
            second_gain,
            second_shift,
            query_bias,
            value_bias,
            inner_bias,
        ]
    )

    def half_of(w):
        rows = w.shape[0] // 2
        return lax.dynamic_slice_in_dim(w, core * rows, rows, 0)

    w_mine = yswap(half_of(w_own))
    out_mine = yswap(half_of(out_weight))
    w_sib = cswap(w_mine)
    out_mine, small, w_mine, w_sib, x2, x1, inner_raw, outer_raw, doc_lengths = tie(
        (out_mine, small, w_mine, w_sib, x2, x1, inner_weight, outer_weight, doc_lengths)
    )
    x3 = zswap(x2, 1)
    small_oth = yswap(small)
    inner_half, outer_half = half_of(inner_raw), half_of(outer_raw)
    cut = inner_half.shape[0] // 4
    inner_one = yswap(inner_half[:cut])

    doc_ends = jnp.cumsum(doc_lengths[0])
    first = jnp.stack([(jnp.bitwise_xor(g_id, j) * members + m_id) * block for j in range(NG)])
    places = (first[:, None] + jnp.arange(block, dtype=jnp.int32)[None, :]).reshape(-1)
    before = places[:, None] >= doc_ends[None, :]
    starts = jnp.max(jnp.where(before, doc_ends[None, :], 0), axis=1).astype(jnp.int32)
    ends = jnp.min(jnp.where(before, ctx * block, doc_ends[None, :]), axis=1).astype(jnp.int32)
    low = starts.reshape(NG, block)[:, 0] // block
    high = (ends.reshape(NG, block)[:, -1] + block - 1) // block
    plain_low = (starts.reshape(NG, block)[:, -1] + block - 1) // block
    plain_high = ends.reshape(NG, block)[:, 0] // block
    whole = plain_low < plain_high
    plain_low = jnp.where(whole, plain_low, high)
    plain_high = jnp.where(whole, plain_high, high)
    scal = jnp.concatenate(
        [jnp.stack([m_id, g_id]), low, high, plain_low, plain_high]
    ).astype(jnp.int32)
    starts = starts[None]
    ends = ends[None]
    place = jnp.stack([g_id, fi, core]).astype(jnp.int32)
    spot = jnp.stack([g_id, xi, core]).astype(jnp.int32)
    dev = jnp.stack([fi, core]).astype(jnp.int32)
    tied = (small_oth, place, spot, dev, x3, inner_one, inner_half, outer_half, scal, starts, ends)
    small_oth, place, spot, dev, x3, inner_one, inner_half, outer_half, scal, starts, ends = tie(tied)

    xs = [local, x1, x2, x3]
    q_t, kv = project(block, place, xs, w_own, w_mine, w_sib, small, small_oth)

    kv_x = xswap(kv)
    inner_two = yswap(inner_half[cut:])
    cut = outer_half.shape[0] // 4
    outer_one = yswap(outer_half[:cut])
    sibs = [cswap(out_mine), cswap(inner_one)]
    tied = tie((kv_x, inner_two, outer_one) + tuple(sibs))
    (kv_x, inner_two, outer_one), sibs = tied[:3], list(tied[3:])
    kv_c = cswap(kv)
    kv_xc = cswap(kv_x)
    kv, kv_c, kv_x, kv_xc, inner_two, outer_one, outer_half = tie(
        (kv, kv_c, kv_x, kv_xc, inner_two, outer_one, outer_half)
    )
    kvs = [kv, kv_c, kv_x, kv_xc]
    outer_two = yswap(outer_half[cut:])
    sibs += [cswap(inner_two), cswap(outer_one)]
    res = group_fwd(members, block, scal, starts, ends, q_t, kvs)
    qkv_shard = jnp.concatenate([query_weight, key_weight, value_weight], axis=1)
    qkv_half = half_of(qkv_shard)
    tied = tie(tuple(res) + (outer_two, qkv_shard, qkv_half) + tuple(sibs))
    res, (outer_two, qkv_shard, qkv_half), sibs = tied[: 2 + NG], tied[2 + NG : 5 + NG], list(tied[5 + NG :])
    o_t, lse = res[:2]
    o_cols = list(res[2:])
    o_parts = [o_cols[0]] + [zswap(o_cols[j], j) for j in range(1, NG)]
    sibs.append(cswap(outer_two))
    tied = tie(tuple(o_parts) + (sibs[-1], qkv_half))
    o_parts, sibs[-1], qkv_half = list(tied[:NG]), tied[NG], tied[NG + 1]
    outs = (out_weight, out_mine, sibs[0])
    inners = (inner_weight, inner_one, inner_two, sibs[1], sibs[2])
    outers = (outer_weight, outer_one, outer_two, sibs[3], sibs[4])
    qkv_mine = yswap(qkv_half)

    mid = middle(block, place, o_parts, local, grad_output[0], small, small_oth, outs, inners, outers)
    tied = tie(tuple(mid) + (qkv_mine,))
    mid, qkv_mine = tied[:-1], tied[-1]
    output, d_first, sums = mid[:3]
    dos = list(mid[3 : 3 + NG])
    keep_a, keep_b, send_a, send_b = mid[3 + NG :]

    state = [output]

    def then(v):
        v, _ = tie((v, state[0]))
        state[0] = v
        return v

    def rows_at(v, index, parts, axis=0):
        n = v.shape[axis] // parts
        return lax.dynamic_slice_in_dim(v, index * n, n, axis)

    def low_sum(terms, cut):
        return then(sum(cut(t).astype(f32) for t in terms).astype(bf16))

    z1 = g_id % 2
    z2 = g_id // 2

    keep_a, keep_b, send_a, send_b = keep_b, keep_a, send_b, send_a
    core_a = cswap(send_a)
    core_b = cswap(send_b)
    dos = [dos[0]] + [zswap(dos[j], j) for j in range(1, NG)]
    terms_b = [keep_b, core_b]
    terms_a = [keep_a, core_a]
    send_a = low_sum(terms_a, lambda v: pick(v, 1 - fi))
    send_b = low_sum(terms_b, lambda v: rows_at(v, 1 - xi, 2, 1))
    tied = tie(tuple(dos) + (send_a, send_b))
    dos, (send_a, send_b) = list(tied[:NG]), tied[NG:]
    got_a = yswap(send_a)
    got_b = xswap(send_b)
    res = group_bwd(members, block, scal, starts, ends, q_t, o_t, lse, dos, kvs)
    tied = tie(tuple(res) + (got_a, got_b))
    res, (got_a, got_b) = tied[:-2], tied[-2:]
    state[0] = got_b
    terms_a = [pick(t, fi) for t in terms_a] + [got_a]
    terms_b = [rows_at(t, xi, 2, 1) for t in terms_b] + [got_b]

    send_a = low_sum(terms_a, lambda v: rows_at(v, 1 - xi, 2))
    send_b = low_sum(terms_b, lambda v: pick(v, 1 - fi))
    got_a, got_b = xswap(send_a), yswap(send_b)
    dq, slots = res[0], res[1:]
    k1, k3 = cswap(slots[1]), cswap(slots[3])
    qkv_sib = cswap(qkv_mine)
    got_a, got_b, k1, k3, qkv_sib = tie((got_a, got_b, k1, k3, qkv_sib))
    terms_a = [rows_at(t, xi, 2) for t in terms_a] + [got_a]
    terms_b = [pick(t, fi) for t in terms_b] + [got_b]
    sum_a = sum(t.astype(f32) for t in terms_a).astype(bf16).reshape(NG, -1, width)
    sum_b = sum(t.astype(f32) for t in terms_b).astype(bf16).reshape(NG, -1, width)
    n_a, n_b = sum_a.shape[1], sum_b.shape[1]
    chunk = then(jnp.concatenate([sum_a, sum_b], axis=1).reshape(-1, width))
    columns = [[m + members * g for g in range(NG)] for m in range(members)]
    piece = lax.psum_scatter(
        chunk, "ctx", scatter_dimension=0, tiled=True, axis_index_groups=columns
    )
    got_kv = xswap(low_sum([slots[2], k3], lambda v: v))
    xt = turn(dev, tie(tuple(xs) + (state[0],))[:NG])
    dq_parts = [dq[:, j * block : (j + 1) * block] for j in range(NG)]
    dq_parts = tie(tuple(dq_parts) + (state[0],))[:NG]
    dq_parts = [dq_parts[0]] + [zswap(dq_parts[j], j) for j in range(1, NG)]
    tied = tie((got_kv, xt) + tuple(dq_parts))
    got_kv, xt, dq_parts = tied[0], tied[1], list(tied[2:])
    dkv = low_sum([slots[0], k1, got_kv], lambda v: v)
    dkv_parts = [dkv[:, j * block : (j + 1) * block] for j in range(NG)]
    dkv_parts = [dkv_parts[0]] + [zswap(dkv_parts[j], j) for j in range(1, NG)]
    keep_q, send_q, bias_sums = qkv_grad(xt, dq, dkv)
    terms_q = [keep_q, cswap(send_q)]
    piece, terms_q[1], bias_sums = tie((piece, terms_q[1], bias_sums))
    whole = lax.all_gather(piece, "ctx", axis=0)
    spread = (jnp.arange(NG) == g_id)[:, None]
    bias_rows = jnp.where(spread[None], bias_sums[0].reshape(3, 1, GW), 0.0).reshape(3, width)
    vecs = jnp.concatenate([sums[:10], bias_rows[::2]], axis=0)
    vecs = then(vecs + cswap(vecs))
    send_q = low_sum(terms_q, lambda v: pick(v, 1 - fi))
    got_q = yswap(send_q)
    terms_q = [pick(t, fi) for t in terms_q] + [got_q]

    send_q = low_sum(terms_q, lambda v: rows_at(v, 1 - xi, 2))
    got_q, got_v = xswap(send_q), yswap(vecs)
    got_q, got_v = tie((got_q, got_v))
    terms_q = [rows_at(t, xi, 2) for t in terms_q] + [got_q]
    vecs = then(vecs + got_v)
    piece_q = low_sum(terms_q, lambda v: v)
    tied = tie(tuple(dq_parts) + tuple(dkv_parts) + (state[0],))
    grad_input = then(
        input_grad(place, d_first, tied[: 2 * NG], (qkv_shard, qkv_mine, qkv_sib))
    )
    far_q, got_v = zswap(piece_q, 2), xswap(vecs)
    far_q, got_v = tie((far_q, got_v))
    vecs = then(vecs + got_v)
    piece_q = then(ordered(z2, piece_q, far_q))
    near_q, got_v = zswap(piece_q, 1), zswap(vecs, 1)
    near_q, got_v = tie((near_q, got_v))
    vecs = then(vecs + got_v)
    piece_q = then(ordered(z1, piece_q, near_q).transpose(1, 0, 2, 3).reshape(NG, -1, 3 * GW))
    side_q, got_v = xswap(piece_q), zswap(vecs, 2)
    side_q, got_v = tie((side_q, got_v))
    vecs = then(vecs + got_v)
    parts_q = [piece_q, side_q, cswap(piece_q), cswap(side_q)]
    grad_query, grad_key, grad_value = unpack(spot, parts_q)
    state[0] = grad_query
    whole, grad_query = tie((whole, grad_query))
    grad_outer, grad_inner, grad_out = finish(
        whole, n_a, n_b, (outer_weight.shape, inner_weight.shape, out_weight.shape)
    )

    mine = lax.dynamic_slice_in_dim(vecs, fi * half, half, 1)
    s_i = lax.dynamic_slice_in_dim(vecs[6:10], fi * 2, 2, 0).reshape(-1)
    return (
        output[None],
        grad_input[None],
        grad_query,
        mine[10],
        grad_key,
        grad_value,
        mine[11],
        grad_out,
        mine[0],
        mine[1],
        mine[2],
        grad_inner,
        s_i,
        grad_outer,
        mine[3],
        mine[4],
        mine[5],
    )


def solution(mesh):
    placed = (
        P("fsdp", "ctx", None),
        P("fsdp", None),
        P("fsdp"),
        P("fsdp", None),
        P("fsdp", None),
        P("fsdp"),
        P("fsdp", None),
        P("fsdp"),
        P("fsdp"),
        P("fsdp"),
        P("fsdp", None),
        P("fsdp"),
        P("fsdp", None),
        P("fsdp"),
        P("fsdp"),
        P("fsdp"),
        P("fsdp", None),
        P("fsdp", "ctx", None),
    )
    quick = mesh.shape["fsdp"] == 2 and mesh.shape["ctx"] == 4 * NG
    return jax.shard_map(
        fast_device if quick else on_device,
        mesh=mesh,
        in_specs=placed,
        out_specs=(
            P("fsdp", "ctx", None),
            P("fsdp", "ctx", None),
            P("fsdp", None),
            P("fsdp"),
            P("fsdp", None),
            P("fsdp", None),
            P("fsdp"),
            P("fsdp", None),
            P("fsdp"),
            P("fsdp"),
            P("fsdp"),
            P("fsdp", None),
            P("fsdp"),
            P("fsdp", None),
            P("fsdp"),
            P("fsdp"),
            P("fsdp"),
        ),
        check_vma=False,
    )
```

```python
import functools
import math

import jax
import jax.numpy as jnp
from jax import lax
from jax.experimental import pallas as pl
from jax.experimental.pallas import tpu as pltpu
from jax.sharding import PartitionSpec as P

H = 12
HD = 64
NG = 4
HG = H // NG
GW = HG * HD

eps = 1e-12
NEG = -1e30
LOG2E = 1.4426950408889634
SCALE = 1.0 / math.sqrt(HD)
bf16 = jnp.bfloat16
f32 = jnp.float32


def layer_norm(r, gain, shift):
    mean = jnp.mean(r, axis=-1, keepdims=True)
    centered = r - mean
    var = jnp.mean(centered * centered, axis=-1, keepdims=True)
    return centered * lax.rsqrt(var + eps) * gain + shift


def gelu_exact(v):
    return jax.nn.gelu(v, approximate=False)


def dot(left, right, ldim=1, rdim=0):
    return lax.dot_general(
        left, right, (((ldim,), (rdim,)), ((), ())), preferred_element_type=f32
    )


def swap(v, axis, bit):
    n = lax.axis_size(axis)
    return lax.ppermute(v, axis, [(i, i ^ bit) for i in range(n)])


def pick(v, index, axis=0):
    return lax.dynamic_index_in_dim(v, index, axis, keepdims=False)


def ordered(bit, own, other):
    return jnp.where(bit == 0, jnp.stack([own, other]), jnp.stack([other, own]))


def slot_of(t, m, g, members):
    shift = members.bit_length() - 1
    return jnp.bitwise_xor(jnp.bitwise_and(t, members - 1), m) * NG + jnp.bitwise_xor(
        jnp.right_shift(t, shift), g
    )


def fwd_kernel(members, block, scal, st_ref, en_ref, q_ref, *rest):
    kv_refs = rest[:members]
    o_ref, ob_ref, lse_ref, k_scr, v_scr = rest[members:]
    m_id, g_id = scal[0], scal[1]
    cols = NG * block
    for s in range(members):
        for h in range(HG):
            k_scr[h, s * cols : (s + 1) * cols, :] = kv_refs[s][h * HD : (h + 1) * HD, :].T
        v_scr[:, s * cols : (s + 1) * cols] = kv_refs[s][GW:, :]
    for j in range(NG):
        qs = slice(j * block, (j + 1) * block)
        start = st_ref[:, qs]
        end = en_ref[:, qs]
        qts = [q_ref[h * HD : (h + 1) * HD, qs] for h in range(HG)]

        def step(t, carry, start=start, end=end, qts=qts):
            off = pl.multiple_of(slot_of(t, m_id, g_id, members) * block, block)
            kpos = t * block + lax.broadcasted_iota(jnp.int32, (block, block), 0)
            allowed = (kpos >= start) & (kpos < end)
            out = []
            for h in range(HG):
                top, total, acc = carry[h]
                s = dot(k_scr[h, pl.ds(off, block), :], qts[h]) * (SCALE * LOG2E)
                s = jnp.where(allowed, s, NEG)
                new = jnp.maximum(top, jnp.max(s, axis=0, keepdims=True))
                alpha = jnp.exp2(top - new)
                p = jnp.exp2(s - new)
                total = total * alpha + jnp.sum(p, axis=0, keepdims=True)
                acc = acc * alpha + dot(
                    v_scr[h * HD : (h + 1) * HD, pl.ds(off, block)], p.astype(bf16)
                )
                out.append((new, total, acc))
            return tuple(out)

        init = tuple(
            (
                jnp.full((1, block), NEG, f32),
                jnp.zeros((1, block), f32),
                jnp.zeros((HD, block), f32),
            )
            for _ in range(HG)
        )
        done = lax.fori_loop(scal[2 + j], scal[2 + NG + j], step, init)
        for h in range(HG):
            top, total, acc = done[h]
            o = acc / total
            o_ref[h * HD : (h + 1) * HD, qs] = o
            ob_ref[h * HD : (h + 1) * HD, qs] = o.astype(bf16)
            lse_ref[h : h + 1, qs] = top + jnp.log2(total)


def bwd_kernel(members, block, scal, st_ref, en_ref, q_ref, o_ref, lse_ref, do_ref, *rest):
    kv_refs = rest[:members]
    dq_ref, dkv_ref, k_scr, v_scr, kt_scr, dk_scr, dv_scr = rest[members:]
    m_id, g_id = scal[0], scal[1]
    cols = NG * block
    for s in range(members):
        part = slice(s * cols, (s + 1) * cols)
        for h in range(HG):
            k_scr[h, part, :] = kv_refs[s][h * HD : (h + 1) * HD, :].T
            v_scr[h, part, :] = kv_refs[s][GW + h * HD : GW + (h + 1) * HD, :].T
        kt_scr[:, part] = kv_refs[s][:GW, :]
    dk_scr[...] = jnp.zeros_like(dk_scr)
    dv_scr[...] = jnp.zeros_like(dv_scr)
    for j in range(NG):
        qs = slice(j * block, (j + 1) * block)
        start = st_ref[:, qs]
        end = en_ref[:, qs]
        per_head = []
        for h in range(HG):
            hr = slice(h * HD, (h + 1) * HD)
            qt = q_ref[hr, qs]
            dot_t = do_ref[hr, qs]
            delta = jnp.sum(dot_t.astype(f32) * o_ref[hr, qs], axis=0, keepdims=True)
            per_head.append((qt, qt.T, dot_t, dot_t.T, delta, lse_ref[h : h + 1, qs]))

        def step(t, carry, start=start, end=end, per_head=per_head):
            off = pl.multiple_of(slot_of(t, m_id, g_id, members) * block, block)
            kpos = t * block + lax.broadcasted_iota(jnp.int32, (block, block), 0)
            allowed = (kpos >= start) & (kpos < end)
            out = []
            for h in range(HG):
                qt, q, dot_t, do, delta, lse = per_head[h]
                s = dot(k_scr[h, pl.ds(off, block), :], qt) * (SCALE * LOG2E)
                p = jnp.where(allowed, jnp.exp2(s - lse), 0.0)
                dp = dot(v_scr[h, pl.ds(off, block), :], dot_t)
                ds = (p * (dp - delta)).astype(bf16)
                dv_scr[h, pl.ds(off, block), :] += dot(p.astype(bf16), do)
                dk_scr[h, pl.ds(off, block), :] += dot(ds, q)
                out.append(
                    carry[h] + dot(kt_scr[h * HD : (h + 1) * HD, pl.ds(off, block)], ds)
                )
            return tuple(out)

        init = tuple(jnp.zeros((HD, block), f32) for _ in range(HG))
        done = lax.fori_loop(scal[2 + j], scal[2 + NG + j], step, init)
        for h in range(HG):
            dq_ref[h * HD : (h + 1) * HD, qs] = (done[h] * SCALE).astype(bf16)
    for s in range(members):
        part = slice(s * cols, (s + 1) * cols)
        for h in range(HG):
            dkv_ref[s, h * HD : (h + 1) * HD, :] = (dk_scr[h, part, :] * SCALE).T.astype(bf16)
            dkv_ref[s, GW + h * HD : GW + (h + 1) * HD, :] = dv_scr[h, part, :].T.astype(bf16)


def whole_specs(n):
    return [pl.BlockSpec(memory_space=pltpu.SMEM)] + [
        pl.BlockSpec(memory_space=pltpu.VMEM) for _ in range(n)
    ]


def attend(members, block, scal, starts, ends, q, kvs):
    keys = members * NG * block
    rows = NG * block
    return pl.pallas_call(
        functools.partial(fwd_kernel, members, block),
        out_shape=(
            jax.ShapeDtypeStruct((GW, rows), f32),
            jax.ShapeDtypeStruct((GW, rows), bf16),
            jax.ShapeDtypeStruct((HG, rows), f32),
        ),
        in_specs=whole_specs(3 + members),
        out_specs=[pl.BlockSpec(memory_space=pltpu.VMEM) for _ in range(3)],
        scratch_shapes=[
            pltpu.VMEM((HG, keys, HD), bf16),
            pltpu.VMEM((GW, keys), bf16),
        ],
        compiler_params=pltpu.CompilerParams(vmem_limit_bytes=50 << 20),
        name="attend",
    )(scal, starts, ends, q, *kvs)


def attend_back(members, block, scal, starts, ends, q, o, lse, do, kvs):
    keys = members * NG * block
    rows = NG * block
    return pl.pallas_call(
        functools.partial(bwd_kernel, members, block),
        out_shape=(
            jax.ShapeDtypeStruct((GW, rows), bf16),
            jax.ShapeDtypeStruct((members, 2 * GW, rows), bf16),
        ),
        in_specs=whole_specs(6 + members),
        out_specs=[pl.BlockSpec(memory_space=pltpu.VMEM) for _ in range(2)],
        scratch_shapes=[
            pltpu.VMEM((HG, keys, HD), bf16),
            pltpu.VMEM((HG, keys, HD), bf16),
            pltpu.VMEM((GW, keys), bf16),
            pltpu.VMEM((HG, keys, HD), f32),
            pltpu.VMEM((HG, keys, HD), f32),
        ],
        compiler_params=pltpu.CompilerParams(vmem_limit_bytes=56 << 20),
        name="attend_back",
    )(scal, starts, ends, q, o, lse, do, *kvs)


def on_device(
    tokens,
    query_weight,
    query_bias,
    key_weight,
    value_weight,
    value_bias,
    out_weight,
    out_bias,
    first_gain,
    first_shift,
    inner_weight,
    inner_bias,
    outer_weight,
    outer_bias,
    second_gain,
    second_shift,
    doc_lengths,
    grad_output,
):
    block = tokens.shape[1]
    width = tokens.shape[2]
    ctx = lax.axis_size("ctx")
    fs = lax.axis_size("fsdp")
    members = ctx // NG
    ci = lax.axis_index("ctx")
    fi = lax.axis_index("fsdp")
    g_id = ci // members
    m_id = ci % members
    core = ci % 2
    own_rows = width // fs
    m_bits = []
    b = members // 2
    while b >= 1:
        m_bits.append(b)
        b //= 2
    g_slots = range(NG)

    def bit_of(index, bit):
        return (index // bit) % 2

    def gather_rows(w):
        rows = w.shape[0]
        if fs != 2:
            return lax.all_gather(w, "fsdp", axis=0, tiled=True)
        half = rows // 2
        mine = swap(lax.dynamic_slice_in_dim(w, core * half, half, 0), "fsdp", 1)
        others = swap(mine, "ctx", 1)
        other = ordered(core, mine, others).reshape(w.shape)
        return ordered(fi, w, other).reshape((2 * rows,) + w.shape[1:])

    local = tokens[0]
    x_slots = {0: local}
    x_slots[2] = swap(local, "ctx", 2 * members)
    x_slots[1] = swap(local, "ctx", members)
    x_slots[3] = swap(x_slots[2], "ctx", members)
    x_all = jnp.concatenate([x_slots[j] for j in g_slots], axis=0)

    vectors = [
        query_bias,
        value_bias,
        out_bias,
        first_gain,
        first_shift,
        inner_bias,
        outer_bias,
        second_gain,
        second_shift,
    ]
    sizes = [v.shape[0] for v in vectors]
    packed = lax.all_gather(jnp.concatenate(vectors), "fsdp", axis=0, tiled=False)
    at = 0
    full = []
    for n in sizes:
        full.append(packed[:, at : at + n].reshape(-1).astype(f32))
        at += n
    qbias, vbias, obias, gain_one, shift_one, ibias, outbias, gain_two, shift_two = full

    group_cols = [
        lax.dynamic_slice_in_dim(w, g_id * GW, GW, 1)
        for w in (query_weight, key_weight, value_weight)
    ]
    w_group = lax.all_gather(
        jnp.concatenate(group_cols, axis=1), "fsdp", axis=0, tiled=True
    ) if fs != 2 else None
    if fs == 2:
        mine = jnp.concatenate(group_cols, axis=1)
        w_group = ordered(fi, mine, swap(mine, "fsdp", 1)).reshape(width, 3 * GW)
    out_full = gather_rows(out_weight)
    inner_full = gather_rows(inner_weight)
    outer_full = gather_rows(outer_weight)
    qkv_full = gather_rows(jnp.concatenate([query_weight, key_weight, value_weight], axis=1))

    bias_group = jnp.concatenate(
        [
            lax.dynamic_slice_in_dim(qbias, g_id * GW, GW, 0),
            jnp.zeros((GW,), f32),
            lax.dynamic_slice_in_dim(vbias, g_id * GW, GW, 0),
        ]
    )
    qkv = (dot(w_group, x_all, 0, 1) + bias_group[:, None]).astype(bf16)
    q_t = qkv[:GW]
    kv_slots = {0: qkv[GW:]}
    for b in m_bits:
        for s in sorted(kv_slots):
            kv_slots[s ^ b] = swap(kv_slots[s], "ctx", b)
    kvs = [kv_slots[s] for s in range(members)]

    doc_ends = jnp.cumsum(doc_lengths[0])
    first = jnp.stack([(jnp.bitwise_xor(g_id, j) * members + m_id) * block for j in g_slots])
    places = (first[:, None] + jnp.arange(block, dtype=jnp.int32)[None, :]).reshape(-1)
    before = places[:, None] >= doc_ends[None, :]
    starts = jnp.max(jnp.where(before, doc_ends[None, :], 0), axis=1).astype(jnp.int32)
    ends = jnp.min(jnp.where(before, ctx * block, doc_ends[None, :]), axis=1).astype(jnp.int32)
    low = starts.reshape(NG, block)[:, 0] // block
    high = (ends.reshape(NG, block)[:, -1] + block - 1) // block
    scal = jnp.concatenate([jnp.stack([m_id, g_id]), low, high]).astype(jnp.int32)
    starts = starts[None]
    ends = ends[None]

    o_t, ob_t, lse = attend(members, block, scal, starts, ends, q_t, kvs)

    def column(v, j):
        return v[:, j * block : (j + 1) * block]

    def exchange(parts):
        return [parts[0]] + [swap(parts[j], "ctx", j * members) for j in range(1, NG)]

    def by_group(slots):
        return [
            lax.select_n(g_id, *[slots[a ^ k] for k in g_slots]) for a in g_slots
        ]

    attn_t = jnp.concatenate(by_group(exchange([column(ob_t, j) for j in g_slots])), axis=0)
    branch = dot(attn_t, out_full, 0, 0) + obias
    local_float = local.astype(f32)
    hidden, first_back = jax.vjp(layer_norm, local_float + branch, gain_one, shift_one)
    hidden_low = hidden.astype(bf16)
    inner = dot(hidden_low, inner_full) + ibias
    active, gelu_back = jax.vjp(gelu_exact, inner)
    active_low = active.astype(bf16)
    outer = dot(active_low, outer_full) + outbias
    result, second_back = jax.vjp(layer_norm, hidden + outer, gain_two, shift_two)
    output = result.astype(bf16)[None]
    grad_y = grad_output[0].astype(f32)
    d_second, grad_gain_two, grad_shift_two = second_back(grad_y)
    d_outer_low = d_second.astype(bf16)
    grad_outbias = jnp.sum(d_outer_low.astype(f32), axis=0)
    (d_inner,) = gelu_back(dot(d_outer_low, outer_full, 1, 1))
    d_inner_low = d_inner.astype(bf16)
    grad_ibias = jnp.sum(d_inner_low.astype(f32), axis=0)
    d_hidden = d_second + dot(d_inner_low, inner_full, 1, 1)
    d_first, grad_gain_one, grad_shift_one = first_back(d_hidden)
    d_branch_low = d_first.astype(bf16)
    grad_obias = jnp.sum(d_branch_low.astype(f32), axis=0)
    do_t = dot(out_full, d_branch_low, 1, 1).astype(bf16).reshape(NG, GW, block)
    do_parts = [pick(do_t, jnp.bitwise_xor(g_id, j)) for j in g_slots]
    do_all = jnp.concatenate(exchange(do_parts), axis=1)

    def halve(acc, axis, bit, index):
        acc = acc.reshape((2, acc.shape[0] // 2) + acc.shape[1:])
        mine = bit_of(index, bit)
        got = swap(pick(acc, 1 - mine), axis, bit)
        return (pick(acc, mine).astype(f32) + got.astype(f32)).astype(bf16)

    def reduce_rows(product, left, bits):
        rows = left.shape[0] // (2 * fs)
        split = left.reshape(fs, 2, rows, left.shape[1])
        send = product(pick(split, 1 - core, 1).reshape(fs * rows, -1)).astype(bf16)
        keep = product(pick(split, core, 1).reshape(fs * rows, -1))
        acc = (keep + swap(send, "ctx", 1).astype(f32)).astype(bf16)
        n = fs
        while n > 1:
            n //= 2
            acc = halve(acc, "fsdp", n, fi)
        for b in bits:
            acc = halve(acc, "ctx", b, ci)
        return acc

    def join(acc, bit):
        both = ordered(bit_of(ci, bit), acc, swap(acc, "ctx", bit))
        return both.reshape((2 * acc.shape[0],) + acc.shape[1:])

    x_bits = [b for b in m_bits if b > 1]
    all_bits = x_bits + [members, 2 * members]

    def weight_grad(left_t, right, rdim=0):
        acc = reduce_rows(lambda part: dot(part, right, 1, rdim), left_t, all_bits)
        for b in all_bits[::-1]:
            acc = join(acc, b)
        return join(acc, 1).astype(f32)

    grad_outer = weight_grad(active_low.T, d_outer_low)
    grad_inner = weight_grad(hidden_low.T, d_inner_low)
    grad_out = weight_grad(attn_t, d_branch_low)

    dq_t, dkv = attend_back(members, block, scal, starts, ends, q_t, o_t, lse, do_all, kvs)
    dkv_slots = {s: dkv[s] for s in range(members)}
    for b in m_bits[::-1]:
        for s in sorted(dkv_slots):
            if s & b:
                got = swap(dkv_slots.pop(s), "ctx", b)
                dkv_slots[s ^ b] = (dkv_slots[s ^ b].astype(f32) + got.astype(f32)).astype(bf16)
    d_qkv = jnp.concatenate([dq_t, dkv_slots[0]], axis=0)
    back = by_group(exchange([column(d_qkv, j) for j in g_slots]))
    d_all = jnp.stack(back).reshape(NG, 3, GW, block).transpose(1, 0, 2, 3).reshape(3 * width, block)
    grad_input = d_first + dot(d_all, qkv_full, 0, 1)

    acc = reduce_rows(lambda part: dot(part, d_qkv, 1, 1), x_all.T, x_bits)
    acc = ordered(bit_of(ci, 2 * members), acc, swap(acc, "ctx", 2 * members))
    acc = ordered(bit_of(ci, members), acc, swap(acc, "ctx", members))
    lead = []
    for b in x_bits[::-1] + [1]:
        acc = ordered(bit_of(ci, b), acc, swap(acc, "ctx", b))
        lead.append(2)
    nb = len(lead)
    acc = acc.astype(f32)
    order = tuple(range(nb)) + (nb + 2, nb + 1, nb, nb + 3)
    acc = acc.transpose(order).reshape(own_rows, NG, 3, GW).transpose(2, 0, 1, 3)
    grad_query, grad_key, grad_value = acc.reshape(3, own_rows, width)

    group_sums = jnp.sum(d_qkv.astype(f32), axis=1)
    spread = (jnp.arange(NG) == g_id)[:, None]
    grad_qbias = jnp.where(spread, group_sums[None, :GW], 0.0).reshape(-1)
    grad_vbias = jnp.where(spread, group_sums[None, 2 * GW :], 0.0).reshape(-1)
    terms = [
        grad_qbias,
        grad_vbias,
        grad_obias,
        grad_gain_one,
        grad_shift_one,
        grad_ibias,
        grad_outbias,
        grad_gain_two,
        grad_shift_two,
    ]
    summed = lax.psum(jnp.concatenate([t.reshape(fs, -1) for t in terms], axis=1), ("fsdp", "ctx"))
    mine = pick(summed, fi)
    shares = []
    at = 0
    for n in sizes:
        shares.append(mine[at : at + n])
        at += n
    s_q, s_v, s_o, s_g1, s_s1, s_i, s_out, s_g2, s_s2 = shares
    return (
        output,
        grad_input[None],
        grad_query,
        s_q,
        grad_key,
        grad_value,
        s_v,
        grad_out,
        s_o,
        s_g1,
        s_s1,
        grad_inner,
        s_i,
        grad_outer,
        s_out,
        s_g2,
        s_s2,
    )


def vmem(n):
    return [pl.BlockSpec(memory_space=pltpu.VMEM) for _ in range(n)]


def anyspec(n):
    return [pl.BlockSpec(memory_space=pl.ANY) for _ in range(n)]


CHEAP = pl.CostEstimate(flops=1, transcendentals=0, bytes_accessed=1)
EXTRA = 8
SPARE = 64
SMEM = pl.BlockSpec(memory_space=pltpu.SMEM)


def params(mib=56):
    return pltpu.CompilerParams(vmem_limit_bytes=mib << 20)


def project_kernel(
    block, scal, x0, x1, x2, x3, own, small, small_oth, mine, sib, q_ref, kv_ref, row_scr, bias_scr, w_scr, sems
):
    g_id, fi, core = scal[0], scal[1], scal[2]
    half = own.shape[0]
    quarter = half // 2
    copies = [
        pltpu.make_async_copy(
            part, w_scr.at[pl.ds(pl.multiple_of(c * quarter, 64), quarter), :], sems.at[k]
        )
        for k, (part, c) in enumerate(((mine, core), (sib, 1 - core)))
    ]
    for c in copies:
        c.start()
    w_own = own[...].T
    at_own = pl.multiple_of(fi * half, 128)
    at_oth = pl.multiple_of((1 - fi) * half, 128)
    row_scr[:, pl.ds(at_own, half)] = small[6:8, :].astype(f32)
    row_scr[:, pl.ds(at_oth, half)] = small_oth[6:8, :].astype(f32)
    bias_scr[...] = jnp.zeros_like(bias_scr)
    for g in range(NG):

        @pl.when(g_id == g)
        def _(g=g):
            bias_scr[0:1, :GW] = row_scr[0:1, g * GW : (g + 1) * GW]
            bias_scr[0:1, 2 * GW :] = row_scr[1:2, g * GW : (g + 1) * GW]

    bias = bias_scr[...].T[:, :1]
    for c in copies:
        c.wait()
    w_oth = w_scr[...].T
    for j, x in enumerate((x0, x1, x2, x3)):
        cols = slice(j * block, (j + 1) * block)
        res = dot(w_own, x[:, pl.ds(at_own, half)], 1, 1)
        res += dot(w_oth, x[:, pl.ds(at_oth, half)], 1, 1)
        res = (res + bias).astype(bf16)
        q_ref[:, cols] = res[:GW]
        kv_ref[:, cols] = res[GW:]


def project(block, scal, xs, own, mine, sib, small, small_oth):
    rows = NG * block
    return pl.pallas_call(
        functools.partial(project_kernel, block),
        out_shape=(
            jax.ShapeDtypeStruct((GW, rows), bf16),
            jax.ShapeDtypeStruct((2 * GW, rows), bf16),
        ),
        in_specs=[SMEM] + vmem(7) + anyspec(2),
        out_specs=vmem(2),
        scratch_shapes=[
            pltpu.VMEM((2, 2 * own.shape[0]), f32),
            pltpu.VMEM((8, 3 * GW), f32),
            pltpu.VMEM(own.shape, bf16),
            pltpu.SemaphoreType.DMA((2,)),
        ],
        cost_estimate=CHEAP,
        compiler_params=params(),
        name="project",
    )(scal, *xs, own, small, small_oth, mine, sib)


def pack_kernel(*refs):
    out = refs[-1]
    n = out.shape[1]
    at = 0
    for ref in refs[:-1]:
        for k in range(ref.shape[0] // n):
            out[at : at + 1, :] = ref[k * n : (k + 1) * n].reshape(1, n)
            at += 1


def pack(vectors):
    n = vectors[0].shape[0]
    rows = sum(v.shape[0] for v in vectors) // n
    return pl.pallas_call(
        pack_kernel,
        out_shape=jax.ShapeDtypeStruct((rows, n), bf16),
        in_specs=vmem(len(vectors)),
        out_specs=vmem(1)[0],
        compiler_params=params(),
        name="pack",
    )(*vectors)


def tile_offset(t, scal, members, block):
    return pl.multiple_of(slot_of(t, scal[0], scal[1], members) * block, block)


UNROLL = 4


def key_loop(scal, j, block, tiles, init):
    low, high, inner_low, inner_high = (scal[2 + NG * i + j] for i in range(4))
    many = (inner_high - inner_low) // UNROLL
    rest = inner_low + UNROLL * many
    before = inner_low - low
    edges = before + high - rest

    def several(i, c):
        return tiles([inner_low + UNROLL * i + u for u in range(UNROLL)], None, c)

    def pair(i, c):
        ts, firsts = [], []
        for u in range(2):
            e = 2 * i + u
            t = jnp.minimum(jnp.where(e < before, low + e, rest + e - before), high - 1)
            ts.append(t)
            firsts.append(jnp.where(e < edges, t * block, -(1 << 30)))
        return tiles(ts, firsts, c)

    carry = lax.fori_loop(0, many, several, init)
    return lax.fori_loop(0, (edges + 1) // 2, pair, carry)


def inside(first, start, end, block):
    kpos = first + lax.broadcasted_iota(jnp.int32, (block, block), 0)
    return (kpos >= start) & (kpos < end)


def staged(n, first, second, third):
    one, two = {}, {}
    for i in range(n + 2):
        if i < n:
            one[i] = first(i)
        if 0 <= i - 1 < n:
            two[i - 1] = second(i - 1, one.pop(i - 1))
        if 0 <= i - 2 < n:
            third(i - 2, two.pop(i - 2))


def group_fwd_kernel(members, block, scal, st_ref, en_ref, q_ref, *rest):
    kv_refs = rest[:members]
    o_ref, lse_ref = rest[members : members + 2]
    ob_refs = rest[members + 2 : members + 2 + NG]
    k_scr, v_scr = rest[members + 2 + NG :]
    cols = NG * block
    for s in range(members):
        for h in range(HG):
            k_scr[h, s * cols : (s + 1) * cols, :] = kv_refs[s][h * HD : (h + 1) * HD, :].T
        v_scr[:, s * cols : (s + 1) * cols] = kv_refs[s][GW:, :]

    @pl.loop(0, NG)
    def _(j):
        cut = pl.ds(pl.multiple_of(j * block, block), block)
        start = st_ref[:, cut]
        end = en_ref[:, cut]
        qts = [q_ref[h * HD : (h + 1) * HD, cut] for h in range(HG)]

        def tiles(ts, firsts, carry):
            offs = [tile_offset(t, scal, members, block) for t in ts]
            allowed = firsts and [inside(first, start, end, block) for first in firsts]
            out = [None] * HG

            def first(h):
                return [dot(k_scr[h, pl.ds(off, block), :], qts[h]) for off in offs]

            def second(h, scores):
                top, total, acc = carry[h]
                if allowed:
                    scores = [jnp.where(a, s, NEG) for a, s in zip(allowed, scores)]
                new = top
                for s in scores:
                    new = jnp.maximum(new, jnp.max(s, axis=0, keepdims=True))
                alpha = jnp.exp2((top - new) * (SCALE * LOG2E))
                total = total * alpha
                probs = []
                for s in scores:
                    p = jnp.exp2((s - new) * (SCALE * LOG2E))
                    total += jnp.sum(p, axis=0, keepdims=True)
                    probs.append(p.astype(bf16))
                return probs, new, total, acc * alpha

            def third(h, state):
                probs, new, total, acc = state
                for p, off in zip(probs, offs):
                    acc += dot(v_scr[h * HD : (h + 1) * HD, pl.ds(off, block)], p)
                out[h] = (new, total, acc)

            staged(HG, first, second, third)
            return tuple(out)

        init = tuple(
            (
                jnp.full((1, block), NEG, f32),
                jnp.zeros((1, block), f32),
                jnp.zeros((HD, block), f32),
            )
            for _ in range(HG)
        )
        done = key_loop(scal, j, block, tiles, init)
        for h in range(HG):
            top, total, acc = done[h]
            o = acc / total
            o_ref[h * HD : (h + 1) * HD, cut] = o
            lse_ref[h : h + 1, cut] = top * (SCALE * LOG2E) + jnp.log2(total)

    for k in range(NG):
        ob_refs[k][...] = o_ref[:, k * block : (k + 1) * block].astype(bf16)


def group_fwd(members, block, scal, starts, ends, q, kvs):
    keys = members * NG * block
    rows = NG * block
    return pl.pallas_call(
        functools.partial(group_fwd_kernel, members, block),
        out_shape=(
            jax.ShapeDtypeStruct((GW, rows), f32),
            jax.ShapeDtypeStruct((HG, rows), f32),
        )
        + tuple(jax.ShapeDtypeStruct((GW, block), bf16) for _ in range(NG)),
        in_specs=[SMEM] + vmem(3 + members),
        out_specs=vmem(2 + NG),
        scratch_shapes=[
            pltpu.VMEM((HG, keys, HD), bf16),
            pltpu.VMEM((GW, keys), bf16),
        ],
        cost_estimate=CHEAP,
        compiler_params=params(),
        name="group_fwd",
    )(scal, starts, ends, q, *kvs)


def group_bwd_kernel(members, block, scal, st_ref, en_ref, q_ref, o_ref, lse_ref, *rest):
    do_refs = rest[:NG]
    kv_refs = rest[NG : NG + members]
    dq_ref = rest[NG + members]
    dkv_refs = rest[NG + members + 1 : NG + 2 * members + 1]
    k_scr, v_scr, dk_scr, dv_scr, do_scr = rest[NG + 2 * members + 1 :]
    cols = NG * block
    heads = [slice(h * HD, (h + 1) * HD) for h in range(HG)]
    for s in range(members):
        part = slice(s * cols, (s + 1) * cols)
        k_scr[:, part] = kv_refs[s][:GW, :]
        v_scr[:, part] = kv_refs[s][GW:, :]
    dk_scr[...] = jnp.zeros_like(dk_scr)
    dv_scr[...] = jnp.zeros_like(dv_scr)
    for k in range(NG):
        do_scr[:, k * block : (k + 1) * block] = do_refs[k][...]

    @pl.loop(0, NG)
    def _(j):
        cut = pl.ds(pl.multiple_of(j * block, block), block)
        start = st_ref[:, cut]
        end = en_ref[:, cut]
        per_head = []
        for h in range(HG):
            do = do_scr[heads[h], cut]
            delta = jnp.sum(do.astype(f32) * o_ref[heads[h], cut], axis=0, keepdims=True)
            per_head.append((q_ref[heads[h], cut], do, delta, lse_ref[h : h + 1, cut]))

        def tiles(ts, firsts, carry):
            out = list(carry)
            work = []
            for u, t in enumerate(ts):
                keys = pl.ds(tile_offset(t, scal, members, block), block)
                allowed = None if firsts is None else inside(firsts[u], start, end, block)
                work += [(h, keys, allowed) for h in range(HG)]

            def first(i):
                h, keys, _ = work[i]
                q, do, _, _ = per_head[h]
                return dot(k_scr[heads[h], keys], q, 0, 0), dot(v_scr[heads[h], keys], do, 0, 0)

            def second(i, pair):
                h, _, allowed = work[i]
                _, _, delta, lse = per_head[h]
                s, dp = pair
                p = jnp.exp2(s * (SCALE * LOG2E) - lse)
                if allowed is not None:
                    p = jnp.where(allowed, p, 0.0)
                return p.astype(bf16), (p * (dp - delta)).astype(bf16)

            def third(i, pair):
                h, keys, _ = work[i]
                q, do, _, _ = per_head[h]
                p, ds = pair
                dv_scr[heads[h], keys] += dot(do, p, 1, 1)
                dk_scr[heads[h], keys] += dot(q, ds, 1, 1)
                out[h] = out[h] + dot(k_scr[heads[h], keys], ds)

            staged(len(work), first, second, third)
            return tuple(out)

        init = tuple(jnp.zeros((HD, block), f32) for _ in range(HG))
        done = key_loop(scal, j, block, tiles, init)
        for h in range(HG):
            dq_ref[heads[h], cut] = (done[h] * SCALE).astype(bf16)

    for s in range(members):
        part = slice(s * cols, (s + 1) * cols)
        dkv_refs[s][:GW, :] = (dk_scr[:, part] * SCALE).astype(bf16)
        dkv_refs[s][GW:, :] = dv_scr[:, part].astype(bf16)


def group_bwd(members, block, scal, starts, ends, q, o, lse, dos, kvs):
    keys = members * NG * block
    rows = NG * block
    return pl.pallas_call(
        functools.partial(group_bwd_kernel, members, block),
        out_shape=(jax.ShapeDtypeStruct((GW, rows), bf16),)
        + tuple(jax.ShapeDtypeStruct((2 * GW, rows), bf16) for _ in range(members)),
        in_specs=[SMEM] + vmem(5 + NG + members),
        out_specs=vmem(1 + members),
        scratch_shapes=[
            pltpu.VMEM((GW, keys), bf16),
            pltpu.VMEM((GW, keys), bf16),
            pltpu.VMEM((GW, keys), f32),
            pltpu.VMEM((GW, keys), f32),
            pltpu.VMEM((GW, rows), bf16),
        ],
        cost_estimate=CHEAP,
        compiler_params=params(),
        name="group_bwd",
    )(scal, starts, ends, q, o, lse, *dos, *kvs)


def normalize(r, width):
    mean = jnp.sum(r, axis=1, keepdims=True) * (1.0 / width)
    centered = r - mean
    var = jnp.sum(centered * centered, axis=1, keepdims=True) * (1.0 / width)
    rstd = lax.rsqrt(var + eps)
    return centered * rstd, rstd


def norm_back(dy, hat, rstd, gain, width):
    dhat = dy * gain
    one = jnp.sum(dhat, axis=1, keepdims=True) * (1.0 / width)
    two = jnp.sum(dhat * hat, axis=1, keepdims=True) * (1.0 / width)
    return rstd * (dhat - one - hat * two)


INV_SQRT2 = 0.7071067811865476
INV_SQRT2PI = 0.3989422804014327


def middle_kernel(block, *refs):
    scal = refs[0]
    at = 1
    o_refs = refs[at : at + NG]
    at += NG
    x_ref, dy_ref, small, small_oth = refs[at : at + 4]
    at += 4
    out_parts = refs[at : at + 3]
    inner_parts = refs[at + 3 : at + 8]
    outer_parts = refs[at + 8 : at + 13]
    at += 13
    y_ref, dr_ref = refs[at : at + 2]
    at += 2
    do_refs = refs[at : at + NG]
    at += NG
    grad_outs = refs[at : at + 4]
    at += 4
    ot_scr, wout, winner, wouter, hbt, gt_scr, gp_scr, dot_scr, vec_ref, ib_ref, sums_ref = refs[at : at + 11]
    grad_refs = refs[at + 11 : at + 15]
    keeps, sends = grad_refs[:2], grad_refs[2:]
    sems = refs[at + 15]
    g_id, fi, core = scal[0], scal[1], scal[2]
    width = x_ref.shape[1]
    ffq = winner.shape[2]
    half = width // 2
    quarter = width // 4

    copies = []

    def load(src, dst):
        copies.append(pltpu.make_async_copy(src, dst, sems.at[len(copies)]))
        copies[-1].start()

    def rows_of(full):
        own = fi * (full // 2)
        oth = (1 - fi) * (full // 2)
        q = full // 4
        return (
            pl.ds(pl.multiple_of(own, 64), full // 2),
            pl.ds(pl.multiple_of(oth + core * q, 64), q),
            pl.ds(pl.multiple_of(oth + (1 - core) * q, 64), q),
        )

    for part, rows in zip(out_parts, rows_of(width)):
        load(part, wout.at[rows, :])
    own, mine, sib = (r.start for r in rows_of(width))
    unit = width // 16
    inner_rows = [pl.ds(own, 8 * unit)] + [
        pl.ds(pl.multiple_of(first + k * unit, 16), n * unit)
        for first in (mine, sib)
        for k, n in ((0, 1), (1, 3))
    ]
    for a in range(4):
        for part, rows in zip(inner_parts, inner_rows):
            load(part.at[:, a * ffq : (a + 1) * ffq], winner.at[a, rows, :])
    own, mine, sib = (r.start for r in rows_of(4 * ffq))
    unit = ffq // 4
    outer_rows = [pl.ds(own, 8 * unit)] + [
        pl.ds(pl.multiple_of(first + k * unit, 16), n * unit)
        for first in (mine, sib)
        for k, n in ((0, 1), (1, 3))
    ]
    for part, rows in zip(outer_parts, outer_rows):
        load(part, wouter.at[rows, :])

    for j in range(NG):
        row = pl.multiple_of(jnp.bitwise_xor(g_id, j) * GW, HD)
        ot_scr[pl.ds(row, GW), :] = o_refs[j][...]
    for side, y in ((small, fi), (small_oth, 1 - fi)):
        vec_ref[:, pl.ds(pl.multiple_of(y * half, 128), half)] = side[:8, :].astype(f32)
        for c in range(2):
            for k in range(2):
                ib_ref[pl.ds(2 * y + c, 1), k * half : (k + 1) * half] = side[
                    8 + 2 * c + k : 9 + 2 * c + k, :
                ].astype(f32)
    for c in copies[:3]:
        c.wait()
    vec = [vec_ref[i : i + 1, :] for i in range(8)]
    obias, gain1, shift1, outbias, gain2, shift2 = vec[:6]
    attn = ot_scr[...].T
    r1 = x_ref[...].astype(f32) + dot(attn, wout[...]) + obias
    hat1, rstd1 = normalize(r1, width)
    hn = hat1 * gain1 + shift1
    hb = hn.astype(bf16)
    hb_t = hb.T
    for y in range(2):
        for c in range(2):
            piece = hb_t[(2 * y + c) * quarter : (2 * y + c + 1) * quarter]

            @pl.when(core == c)
            def _(piece=piece, y=y):
                hbt[y * quarter : (y + 1) * quarter, :] = piece

            @pl.when(core != c)
            def _(piece=piece, y=y):
                hbt[half + y * quarter : half + (y + 1) * quarter, :] = piece

    for c in copies[3:23]:
        c.wait()
    z = hn + outbias
    for a in range(4):
        u = dot(hb, winner[a]) + ib_ref[a : a + 1, :]
        phi = 0.5 + 0.5 * lax.erf(u * INV_SQRT2)
        g = (u * phi).astype(bf16)
        gp_scr[a] = phi + u * (jnp.exp(u * u * -0.5) * INV_SQRT2PI)
        gt_scr[a] = g.T
        if a == 0:
            for c in copies[23:]:
                c.wait()
        z += dot(g, wouter[a * ffq : (a + 1) * ffq, :])
    hat2, rstd2 = normalize(z, width)
    y_ref[...] = (hat2 * gain2 + shift2).astype(bf16)
    dy = dy_ref[...].astype(f32)
    sums_ref[4:5, :] = jnp.sum(dy * hat2, axis=0, keepdims=True)
    sums_ref[5:6, :] = jnp.sum(dy, axis=0, keepdims=True)
    dz = norm_back(dy, hat2, rstd2, gain2, width)
    dzb = dz.astype(bf16)
    sums_ref[3:4, :] = jnp.sum(dzb.astype(f32), axis=0, keepdims=True)
    dh = dz
    for a in range(4):
        dg = dot(dzb, wouter[a * ffq : (a + 1) * ffq, :], 1, 1)
        du = (dg * gp_scr[a]).astype(bf16)
        sums_ref[6 + a : 7 + a, :] = jnp.sum(du.astype(f32), axis=0, keepdims=True)
        dh += dot(du, winner[a], 1, 1)
        grad = dot(hbt[...], du).astype(bf16)
        for y in range(2):
            rows = slice(a * quarter, (a + 1) * quarter)
            keeps[0][y, rows] = grad[y * quarter : (y + 1) * quarter]
            sends[0][y, rows] = grad[half + y * quarter : half + (y + 1) * quarter]
        grad = dot(gt_scr[a], dzb).astype(bf16)
        for c in range(2):
            if a % 2 != c:
                continue

            @pl.when(core == c)
            def _(grad=grad, a=a):
                keeps[1][a // 2, :ffq] = grad

            @pl.when(core != c)
            def _(grad=grad, a=a):
                sends[1][a // 2, :ffq] = grad

    stored = []

    def store(rows):
        for src, dst in zip(grad_refs, grad_outs):
            part = slice(*rows(src.shape[1]))
            sem = sems.at[len(copies) + len(stored)]
            stored.append(pltpu.make_async_copy(src.at[:, part], dst.at[:, part], sem))
            stored[-1].start()

    store(lambda n: (0, ffq))
    sums_ref[1:2, :] = jnp.sum(dh * hat1, axis=0, keepdims=True)
    sums_ref[2:3, :] = jnp.sum(dh, axis=0, keepdims=True)
    dr = norm_back(dh, hat1, rstd1, gain1, width)
    dr_ref[...] = dr
    dab = dr.astype(bf16)
    sums_ref[0:1, :] = jnp.sum(dab.astype(f32), axis=0, keepdims=True)
    for y in range(2):
        top = jnp.concatenate([sums_ref[0:6, :], sums_ref[6 + 2 * y : 8 + 2 * y, :]], axis=0)
        spare = jnp.concatenate([top, jnp.zeros((SPARE - 8, width), f32)], axis=0).astype(bf16)
        none = jnp.zeros((SPARE, width), bf16)

        @pl.when(core == 0)
        def _(y=y, spare=spare, none=none):
            keeps[0][y, 4 * quarter :] = spare
            sends[0][y, 4 * quarter :] = none

        @pl.when(core != 0)
        def _(y=y, spare=spare, none=none):
            keeps[0][y, 4 * quarter :] = none
            sends[0][y, 4 * quarter :] = spare

    dot_scr[...] = dot(wout[...], dab, 1, 1).astype(bf16)
    for j in range(NG):
        row = pl.multiple_of(jnp.bitwise_xor(g_id, j) * GW, HD)
        do_refs[j][...] = dot_scr[pl.ds(row, GW), :]
    grad = dot(ot_scr[...], dab).astype(bf16)
    for y in range(2):
        for c in range(2):
            piece = grad[(2 * y + c) * quarter : (2 * y + c + 1) * quarter]

            @pl.when(core == c)
            def _(piece=piece, y=y):
                keeps[1][y, ffq:] = piece

            @pl.when(core != c)
            def _(piece=piece, y=y):
                sends[1][y, ffq:] = piece

    store(lambda n: (ffq, n))
    for c in stored:
        c.wait()


def middle(block, scal, os, x, dy, small, small_oth, outs, inners, outers):
    width = x.shape[1]
    ffq = inners[0].shape[1] // 4
    q = width // 4
    grads = [
        jax.ShapeDtypeStruct((2, 4 * q + SPARE, ffq), bf16),
        jax.ShapeDtypeStruct((2, ffq + q, width), bf16),
    ]
    return pl.pallas_call(
        functools.partial(middle_kernel, block),
        out_shape=(
            jax.ShapeDtypeStruct((block, width), bf16),
            jax.ShapeDtypeStruct((block, width), f32),
        )
        + tuple(jax.ShapeDtypeStruct((GW, block), bf16) for _ in range(NG))
        + tuple(grads)
        + tuple(grads),
        in_specs=[SMEM] + vmem(NG + 4) + anyspec(13),
        out_specs=vmem(2 + NG) + anyspec(4),
        scratch_shapes=[
            pltpu.VMEM((width, block), bf16),
            pltpu.VMEM((width, width), bf16),
            pltpu.VMEM((4, width, ffq), bf16),
            pltpu.VMEM((4 * ffq, width), bf16),
            pltpu.VMEM((width, block), bf16),
            pltpu.VMEM((4, ffq, block), bf16),
            pltpu.VMEM((4, block, ffq), f32),
            pltpu.VMEM((width, block), bf16),
            pltpu.VMEM((8, width), f32),
            pltpu.VMEM((4, ffq), f32),
            pltpu.VMEM((16, width), f32),
        ]
        + [pltpu.VMEM(g.shape, g.dtype) for g in grads + grads]
        + [
            pltpu.SemaphoreType.DMA((36,)),
        ],
        cost_estimate=CHEAP,
        compiler_params=params(60),
        name="middle",
    )(scal, *os, x, dy, small, small_oth, *outs, *inners, *outers)


def turn_kernel(scal, x0, x1, x2, x3, xt):
    core = scal[1]
    block, width = x0.shape
    half, quarter = width // 2, width // 4
    for j, x in enumerate((x0, x1, x2, x3)):
        cols = slice(j * block, (j + 1) * block)
        turned = x[...].T
        for y in range(2):
            for c in range(2):
                piece = turned[(2 * y + c) * quarter : (2 * y + c + 1) * quarter]

                @pl.when(core == c)
                def _(piece=piece, y=y):
                    xt[y * quarter : (y + 1) * quarter, cols] = piece

                @pl.when(core != c)
                def _(piece=piece, y=y):
                    xt[half + y * quarter : half + (y + 1) * quarter, cols] = piece


def turn(scal, xs):
    block, width = xs[0].shape
    return pl.pallas_call(
        turn_kernel,
        out_shape=jax.ShapeDtypeStruct((width, NG * block), bf16),
        in_specs=[SMEM] + vmem(NG),
        out_specs=vmem(1)[0],
        compiler_params=params(),
        name="turn",
    )(scal, *xs)


def qkv_grad_kernel(scal, xt, dq_ref, dkv_ref, keep, send, d_scr):
    g_id, core = scal[0], scal[2]
    d_scr[:GW, :] = dq_ref[...]
    d_scr[GW:, :] = dkv_ref[...]
    d = d_scr[...]
    quarter = xt.shape[0] // 4
    part = quarter // 2
    step = part + EXTRA
    grad = dot(xt[...], d, 1, 1).astype(bf16)
    ones = jnp.where(lax.broadcasted_iota(jnp.int32, (EXTRA, d.shape[1]), 0) == 0, 1.0, 0.0)
    sums = dot(ones.astype(bf16), d, 1, 1).astype(bf16)
    none = jnp.zeros_like(sums)
    for k, out in enumerate((keep, send)):
        for y in range(2):
            at = (2 * k + y) * quarter
            for x in range(2):
                out[y, x * step : x * step + part] = grad[at + x * part : at + (x + 1) * part]
                out[y, x * step + part : (x + 1) * step] = none
    for y in range(2):
        mine = jnp.right_shift(g_id, 1) == y

        @pl.when(mine & (core == 0))
        def _(y=y):
            keep[y, part:step] = sums

        @pl.when(mine & (core != 0))
        def _(y=y):
            send[y, part:step] = sums


def qkv_grad(scal, xt, dq, dkv):
    width, rows = xt.shape
    q = width // 4 + 2 * EXTRA
    return pl.pallas_call(
        qkv_grad_kernel,
        out_shape=(
            jax.ShapeDtypeStruct((2, q, 3 * GW), bf16),
            jax.ShapeDtypeStruct((2, q, 3 * GW), bf16),
        ),
        in_specs=[SMEM] + vmem(3),
        out_specs=vmem(2),
        scratch_shapes=[pltpu.VMEM((3 * GW, rows), bf16)],
        compiler_params=params(),
        name="qkv_grad",
    )(scal, xt, dq, dkv)


def each_part(scal, fn):
    xi, core = scal[1], scal[2]
    for c in range(2):
        for x in range(2):
            here = jnp.bitwise_xor(core, c) * 2 + jnp.bitwise_xor(xi, x)
            for s in range(4):
                pl.when(here == s)(functools.partial(fn, c, x, s))


def unpack_kernel(place, scal, *refs):
    parts, outs, bias_ref = refs[:4], refs[4:7], refs[7]
    rows = parts[0].shape[1] - EXTRA
    fi = place[1]

    def put(c, x, s):
        at = (2 * c + x) * rows
        for g in range(NG):
            v = parts[s][g, :rows].astype(f32)
            for part in range(3):
                outs[part][at : at + rows, g * GW : (g + 1) * GW] = v[
                    :, part * GW : (part + 1) * GW
                ]
        if (c, x) == (0, 0):
            for k in range(2):
                row = parts[s][2 * fi + k, rows:].astype(f32)
                bias_ref[0:1, k * GW : (k + 1) * GW] = row[:1, :GW]
                bias_ref[1:2, k * GW : (k + 1) * GW] = row[:1, 2 * GW :]

    each_part(scal, put)


def spread_rows(segments, first, v):
    base = 0
    for n, place in segments:
        lo, hi = max(first, base), min(first + v.shape[0], base + n)
        if lo < hi:
            place(lo - base, v[lo - first : hi - first])
        base += n


def finish_kernel(scal, *refs):
    parts_a, whole_b = refs[:4], refs[4]
    outer_ref, inner_ref, out_ref, vec_ref = refs[5:]
    ffq = inner_ref.shape[1] // 4
    quarter = inner_ref.shape[0] // 2
    g_id = scal[0]
    n_a, n_b = parts_a[0].shape[1], whole_b.shape[1]

    def put_a(c, x, s):
        def outer(row, v):
            outer_ref[c * ffq + row : c * ffq + row + v.shape[0], :] = v

        def out(row, v):
            out_ref[c * quarter + row : c * quarter + row + v.shape[0], :] = v

        for g in range(NG):
            j = jnp.bitwise_xor(g_id, g)
            v = parts_a[s][jnp.bitwise_and(j, 1) * 2 + jnp.right_shift(j, 1)].astype(f32)
            spread_rows(((ffq, outer), (quarter, out)), (NG * x + g) * n_a, v)

    each_part(scal, put_a)
    for i in range(whole_b.shape[0]):
        g, x, c = i >> 2, i >> 1 & 1, i & 1
        def inner(a, row, v, c=c):
            at = c * quarter + row
            inner_ref[at : at + v.shape[0], a * ffq : (a + 1) * ffq] = v

        def sums(row, v, c=c):
            if c == 0 and row < 8:
                vec_ref[row : min(8, row + v.shape[0]), :] = v[: 8 - row]

        spread_rows(
            tuple((quarter, functools.partial(inner, a)) for a in range(4)) + ((SPARE, sums),),
            (NG * x + g) * n_b,
            whole_b[i].astype(f32),
        )


def ending_kernel(place, spot, *refs):
    parts, whole_b, parts_q = refs[:4], refs[4], refs[5:9]
    dr_ref, d_refs, w_parts = refs[9], refs[10 : 10 + 2 * NG], refs[10 + 2 * NG : 13 + 2 * NG]
    outs = refs[13 + 2 * NG : 21 + 2 * NG]
    dx_ref = refs[21 + 2 * NG]
    staged_refs = refs[22 + 2 * NG : 30 + 2 * NG]
    w_scr, d_scr, sems = refs[30 + 2 * NG :]
    g_id, fi, core = place[0], place[1], place[2]
    width = w_scr.shape[0]
    q = width // 4
    oth = (1 - fi) * 2 * q
    rows = (
        pl.ds(pl.multiple_of(fi * 2 * q, 64), 2 * q),
        pl.ds(pl.multiple_of(oth + core * q, 64), q),
        pl.ds(pl.multiple_of(oth + (1 - core) * q, 64), q),
    )
    loads = [
        pltpu.make_async_copy(p, w_scr.at[r, :], sems.at[i])
        for i, (p, r) in enumerate(zip(w_parts, rows))
    ]
    for c in loads:
        c.start()
    stores = [
        pltpu.make_async_copy(src, dst, sems.at[3 + i])
        for i, (src, dst) in enumerate(zip(staged_refs, outs))
    ]
    finish_kernel(spot, *parts, whole_b, *staged_refs[:4])
    for c in stores[:4]:
        c.start()
    unpack_kernel(place, spot, *parts_q, *staged_refs[4:])
    for c in stores[4:]:
        c.start()
    for j in range(NG):
        base = jnp.bitwise_xor(g_id, j) * GW
        for part in range(3):
            at = pl.multiple_of(part * width + base, HD)
            src = d_refs[j][...] if part == 0 else d_refs[NG + j][(part - 1) * GW : part * GW, :]
            d_scr[pl.ds(at, GW), :] = src
    for c in loads:
        c.wait()
    dx_ref[...] = dr_ref[...] + dot(w_scr[...], d_scr[...]).T
    for c in stores:
        c.wait()


def ending(place, spot, parts_a, whole_b, parts_q, dr, d_parts, w_parts, shapes):
    block, width = dr.shape
    wide = [
        *shapes,
        (8, width),
        *((width // 2, width) for _ in range(3)),
        (2, 2 * GW),
    ]
    return pl.pallas_call(
        ending_kernel,
        out_shape=tuple(jax.ShapeDtypeStruct(s, f32) for s in wide)
        + (jax.ShapeDtypeStruct((block, width), f32),),
        in_specs=[SMEM, SMEM] + vmem(10 + 2 * NG) + anyspec(3),
        out_specs=anyspec(8) + vmem(1),
        scratch_shapes=[pltpu.VMEM(s, f32) for s in wide]
        + [
            pltpu.VMEM((width, 3 * width), bf16),
            pltpu.VMEM((3 * width, block), bf16),
            pltpu.SemaphoreType.DMA((11,)),
        ],
        cost_estimate=CHEAP,
        compiler_params=params(60),
        name="ending",
    )(place, spot, *parts_a, whole_b, *parts_q, dr, *d_parts, *w_parts)


def fast_device(
    tokens,
    query_weight,
    query_bias,
    key_weight,
    value_weight,
    value_bias,
    out_weight,
    out_bias,
    first_gain,
    first_shift,
    inner_weight,
    inner_bias,
    outer_weight,
    outer_bias,
    second_gain,
    second_shift,
    doc_lengths,
    grad_output,
):
    block = tokens.shape[1]
    width = tokens.shape[2]
    ctx = lax.axis_size("ctx")
    members = ctx // NG
    ci = lax.axis_index("ctx")
    fi = lax.axis_index("fsdp")
    g_id = ci // members
    m_id = ci % members
    core = ci % 2
    xi = m_id // 2
    half = width // 2
    tie = lax.optimization_barrier

    def zswap(v, j):
        return swap(v, "ctx", j * members)

    def xswap(v):
        return swap(v, "ctx", 2)

    def cswap(v):
        return swap(v, "ctx", 1)

    def yswap(v):
        return swap(v, "fsdp", 1)

    local = tokens[0]
    x2 = zswap(local, 2)
    x1 = zswap(local, 1)
    w_own = jnp.concatenate(
        [
            lax.dynamic_slice_in_dim(w, g_id * GW, GW, 1)
            for w in (query_weight, key_weight, value_weight)
        ],
        axis=1,
    )
    small = pack(
        [
            out_bias,
            first_gain,
            first_shift,
            outer_bias,
            second_gain,
            second_shift,
            query_bias,
            value_bias,
            inner_bias,
        ]
    )

    def half_of(w):
        rows = w.shape[0] // 2
        return lax.dynamic_slice_in_dim(w, core * rows, rows, 0)

    w_mine = yswap(half_of(w_own))
    out_mine = yswap(half_of(out_weight))
    w_sib = cswap(w_mine)
    out_mine, small, w_mine, w_sib, x2, x1, inner_raw, outer_raw, doc_lengths = tie(
        (out_mine, small, w_mine, w_sib, x2, x1, inner_weight, outer_weight, doc_lengths)
    )
    x3 = zswap(x2, 1)
    small_oth = yswap(small)
    inner_half, outer_half = half_of(inner_raw), half_of(outer_raw)
    cut = inner_half.shape[0] // 4
    inner_one = yswap(inner_half[:cut])

    doc_ends = jnp.cumsum(doc_lengths[0])
    first = jnp.stack([(jnp.bitwise_xor(g_id, j) * members + m_id) * block for j in range(NG)])
    places = (first[:, None] + jnp.arange(block, dtype=jnp.int32)[None, :]).reshape(-1)
    before = places[:, None] >= doc_ends[None, :]
    starts = jnp.max(jnp.where(before, doc_ends[None, :], 0), axis=1).astype(jnp.int32)
    ends = jnp.min(jnp.where(before, ctx * block, doc_ends[None, :]), axis=1).astype(jnp.int32)
    low = starts.reshape(NG, block)[:, 0] // block
    high = (ends.reshape(NG, block)[:, -1] + block - 1) // block
    plain_low = (starts.reshape(NG, block)[:, -1] + block - 1) // block
    plain_high = ends.reshape(NG, block)[:, 0] // block
    whole = plain_low < plain_high
    plain_low = jnp.where(whole, plain_low, high)
    plain_high = jnp.where(whole, plain_high, high)
    scal = jnp.concatenate(
        [jnp.stack([m_id, g_id]), low, high, plain_low, plain_high]
    ).astype(jnp.int32)
    starts = starts[None]
    ends = ends[None]
    place = jnp.stack([g_id, fi, core]).astype(jnp.int32)
    spot = jnp.stack([g_id, xi, core]).astype(jnp.int32)
    dev = jnp.stack([fi, core]).astype(jnp.int32)
    tied = (small_oth, place, spot, dev, x3, inner_one, inner_half, outer_half, scal, starts, ends)
    small_oth, place, spot, dev, x3, inner_one, inner_half, outer_half, scal, starts, ends = tie(tied)

    xs = [local, x1, x2, x3]
    q_t, kv = project(block, place, xs, w_own, w_mine, w_sib, small, small_oth)

    kv_x = xswap(kv)
    inner_two = yswap(inner_half[cut:])
    cut = outer_half.shape[0] // 4
    outer_one = yswap(outer_half[:cut])
    sibs = [cswap(out_mine), cswap(inner_one)]
    tied = tie((kv_x, inner_two, outer_one) + tuple(sibs))
    (kv_x, inner_two, outer_one), sibs = tied[:3], list(tied[3:])
    kv_c = cswap(kv)
    kv_xc = cswap(kv_x)
    kv, kv_c, kv_x, kv_xc, inner_two, outer_one, outer_half = tie(
        (kv, kv_c, kv_x, kv_xc, inner_two, outer_one, outer_half)
    )
    kvs = [kv, kv_c, kv_x, kv_xc]
    outer_two = yswap(outer_half[cut:])
    sibs += [cswap(inner_two), cswap(outer_one)]
    res = group_fwd(members, block, scal, starts, ends, q_t, kvs)
    qkv_shard = jnp.concatenate([query_weight, key_weight, value_weight], axis=1)
    qkv_half = half_of(qkv_shard)
    tied = tie(tuple(res) + (outer_two, qkv_shard, qkv_half) + tuple(sibs))
    res, (outer_two, qkv_shard, qkv_half), sibs = tied[: 2 + NG], tied[2 + NG : 5 + NG], list(tied[5 + NG :])
    o_t, lse = res[:2]
    o_cols = list(res[2:])
    o_parts = [o_cols[0]] + [zswap(o_cols[j], j) for j in range(1, NG)]
    sibs.append(cswap(outer_two))
    tied = tie(tuple(o_parts) + (sibs[-1], qkv_half))
    o_parts, sibs[-1], qkv_half = list(tied[:NG]), tied[NG], tied[NG + 1]
    outs = (out_weight, out_mine, sibs[0])
    inners = (inner_weight, inner_one, inner_two, sibs[1], sibs[2])
    outers = (outer_weight, outer_one, outer_two, sibs[3], sibs[4])
    qkv_mine = yswap(qkv_half)

    mid = middle(block, place, o_parts, local, grad_output[0], small, small_oth, outs, inners, outers)
    tied = tie(tuple(mid) + (qkv_mine,))
    mid, qkv_mine = tied[:-1], tied[-1]
    output, d_first = mid[:2]
    dos = list(mid[2 : 2 + NG])
    keep_a, keep_b, send_a, send_b = mid[2 + NG :]

    state = [output]

    def then(v):
        v, _ = tie((v, state[0]))
        state[0] = v
        return v

    def rows_at(v, index, parts, axis=0):
        n = v.shape[axis] // parts
        return lax.dynamic_slice_in_dim(v, index * n, n, axis)

    def low_sum(terms, cut):
        return then(sum(cut(t).astype(f32) for t in terms).astype(bf16))

    z1 = g_id % 2
    z2 = g_id // 2

    keep_a, keep_b, send_a, send_b = keep_b, keep_a, send_b, send_a
    core_a = cswap(send_a)
    core_b = cswap(send_b)
    dos = [dos[0]] + [zswap(dos[j], j) for j in range(1, NG)]
    terms_b = [keep_b, core_b]
    terms_a = [keep_a, core_a]
    send_a = low_sum(terms_a, lambda v: pick(v, 1 - fi))
    send_b = low_sum(terms_b, lambda v: rows_at(v, 1 - xi, 2, 1))
    tied = tie(tuple(dos) + (send_a, send_b))
    dos, (send_a, send_b) = list(tied[:NG]), tied[NG:]
    got_a = yswap(send_a)
    got_b = xswap(send_b)
    res = group_bwd(members, block, scal, starts, ends, q_t, o_t, lse, dos, kvs)
    tied = tie(tuple(res) + (got_a, got_b))
    res, (got_a, got_b) = tied[:-2], tied[-2:]
    state[0] = got_b
    terms_a = [pick(t, fi) for t in terms_a] + [got_a]
    terms_b = [rows_at(t, xi, 2, 1) for t in terms_b] + [got_b]

    send_a = low_sum(terms_a, lambda v: rows_at(v, 1 - xi, 2))
    send_b = low_sum(terms_b, lambda v: pick(v, 1 - fi))
    got_a, got_b = xswap(send_a), yswap(send_b)
    dq, slots = res[0], res[1:]
    k1, k3 = cswap(slots[1]), cswap(slots[3])
    qkv_sib = cswap(qkv_mine)
    got_a, got_b, k1, k3, qkv_sib = tie((got_a, got_b, k1, k3, qkv_sib))
    terms_a = [rows_at(t, xi, 2) for t in terms_a] + [got_a]
    terms_b = [pick(t, fi) for t in terms_b] + [got_b]
    sum_a = sum(t.astype(f32) for t in terms_a).astype(bf16).reshape(NG, -1, width)
    sum_b = sum(t.astype(f32) for t in terms_b).astype(bf16).reshape(NG, -1, width)
    n_a, n_b = sum_a.shape[1], sum_b.shape[1]
    chunk = then(jnp.concatenate([sum_a, sum_b], axis=1).reshape(-1, width))
    columns = [[m + members * g for g in range(NG)] for m in range(members)]
    piece = lax.psum_scatter(
        chunk, "ctx", scatter_dimension=0, tiled=True, axis_index_groups=columns
    )
    got_kv = xswap(low_sum([slots[2], k3], lambda v: v))
    xt = turn(dev, tie(tuple(xs) + (state[0],))[:NG])
    dq_parts = [dq[:, j * block : (j + 1) * block] for j in range(NG)]
    dq_parts = tie(tuple(dq_parts) + (state[0],))[:NG]
    dq_parts = [dq_parts[0]] + [zswap(dq_parts[j], j) for j in range(1, NG)]
    tied = tie((got_kv, xt) + tuple(dq_parts))
    got_kv, xt, dq_parts = tied[0], tied[1], list(tied[2:])
    dkv = low_sum([slots[0], k1, got_kv], lambda v: v)
    dkv_parts = [dkv[:, j * block : (j + 1) * block] for j in range(NG)]
    keep_q, send_q = qkv_grad(place, xt, dq, dkv)
    terms_q = [keep_q, cswap(send_q)]
    got_q = yswap(low_sum(terms_q, lambda v: pick(v, 1 - fi)))
    terms_q = [pick(t, fi) for t in terms_q] + [got_q]

    piece = tie((piece, state[0]))[0]
    piece_a = piece[:n_a]
    whole_b = lax.all_gather(piece[n_a:], "ctx", axis=0)
    far_a = zswap(piece_a, 2)
    got_q = xswap(low_sum(terms_q, lambda v: rows_at(v, 1 - xi, 2)))
    far_a = tie((far_a, state[0]))[0]
    pair_a = then(jnp.stack([piece_a, far_a]))
    near_a = zswap(pair_a, 1)
    got_q = tie((got_q, state[0]))[0]
    terms_q = [rows_at(t, xi, 2) for t in terms_q] + [got_q]
    piece_q = low_sum(terms_q, lambda v: v)
    far_q = zswap(piece_q, 2)
    near_a = tie((near_a, state[0]))[0]
    col_a = then(jnp.stack([pair_a, near_a]))
    side_a = xswap(col_a)
    far_q = tie((far_q, state[0]))[0]
    piece_q = then(ordered(z2, piece_q, far_q))
    near_q = zswap(piece_q, 1)
    piece_q = then(ordered(z1, piece_q, near_q).transpose(1, 0, 2, 3).reshape(NG, -1, 3 * GW))
    side_q = xswap(piece_q)
    dkv_parts = tie(tuple(dkv_parts) + (state[0],))[:NG]
    dkv_parts = [dkv_parts[0]] + [zswap(dkv_parts[j], j) for j in range(1, NG)]
    tied = tie((side_a, side_q) + tuple(dkv_parts))
    side_a, side_q, dkv_parts = tied[0], tied[1], tied[2:]
    parts_q = [piece_q, side_q, cswap(piece_q), cswap(side_q)]
    core_a, core_side = cswap(col_a), cswap(side_a)
    tied = tie(tuple(parts_q) + (core_a, core_side))
    parts_q, core_a, core_side = tied[:4], tied[4], tied[5]
    parts_a = [v.reshape(NG, n_a, width) for v in (col_a, side_a, core_a, core_side)]
    tied = tie(tuple(parts_q) + tuple(parts_a) + (whole_b,) + tuple(dq_parts) + tuple(dkv_parts))
    parts_q, parts_a, whole_b, d_parts = tied[:4], tied[4:8], tied[8], tied[9:]
    (
        grad_outer,
        grad_inner,
        grad_out,
        vecs,
        grad_query,
        grad_key,
        grad_value,
        bias_rows,
        grad_input,
    ) = ending(
        place,
        spot,
        parts_a,
        whole_b,
        parts_q,
        d_first,
        d_parts,
        (qkv_shard, qkv_mine, qkv_sib),
        (outer_weight.shape, inner_weight.shape, out_weight.shape),
    )

    mine = lax.dynamic_slice_in_dim(vecs, fi * half, half, 1)
    return (
        output[None],
        grad_input[None],
        grad_query,
        bias_rows[0],
        grad_key,
        grad_value,
        bias_rows[1],
        grad_out,
        mine[0],
        mine[1],
        mine[2],
        grad_inner,
        vecs[6:8].reshape(-1),
        grad_outer,
        mine[3],
        mine[4],
        mine[5],
    )


def solution(mesh):
    placed = (
        P("fsdp", "ctx", None),
        P("fsdp", None),
        P("fsdp"),
        P("fsdp", None),
        P("fsdp", None),
        P("fsdp"),
        P("fsdp", None),
        P("fsdp"),
        P("fsdp"),
        P("fsdp"),
        P("fsdp", None),
        P("fsdp"),
        P("fsdp", None),
        P("fsdp"),
        P("fsdp"),
        P("fsdp"),
        P("fsdp", None),
        P("fsdp", "ctx", None),
    )
    quick = mesh.shape["fsdp"] == 2 and mesh.shape["ctx"] == 4 * NG
    return jax.shard_map(
        fast_device if quick else on_device,
        mesh=mesh,
        in_specs=placed,
        out_specs=(
            P("fsdp", "ctx", None),
            P("fsdp", "ctx", None),
            P("fsdp", None),
            P("fsdp"),
            P("fsdp", None),
            P("fsdp", None),
            P("fsdp"),
            P("fsdp", None),
            P("fsdp"),
            P("fsdp"),
            P("fsdp"),
            P("fsdp", None),
            P("fsdp"),
            P("fsdp", None),
            P("fsdp"),
            P("fsdp"),
            P("fsdp"),
        ),
        check_vma=False,
    )
```

```python
import functools
import math

import jax
import jax.numpy as jnp
from jax import lax
from jax.experimental import pallas as pl
from jax.experimental.pallas import tpu as pltpu
from jax.sharding import PartitionSpec as P

H = 12
HD = 64
NG = 4
HG = H // NG
GW = HG * HD

eps = 1e-12
NEG = -1e30
LOG2E = 1.4426950408889634
SCALE = 1.0 / math.sqrt(HD)
bf16 = jnp.bfloat16
f32 = jnp.float32


def layer_norm(r, gain, shift):
    mean = jnp.mean(r, axis=-1, keepdims=True)
    centered = r - mean
    var = jnp.mean(centered * centered, axis=-1, keepdims=True)
    return centered * lax.rsqrt(var + eps) * gain + shift


def gelu_exact(v):
    return jax.nn.gelu(v, approximate=False)


def dot(left, right, ldim=1, rdim=0):
    return lax.dot_general(
        left, right, (((ldim,), (rdim,)), ((), ())), preferred_element_type=f32
    )


def swap(v, axis, bit):
    n = lax.axis_size(axis)
    return lax.ppermute(v, axis, [(i, i ^ bit) for i in range(n)])


def pick(v, index, axis=0):
    return lax.dynamic_index_in_dim(v, index, axis, keepdims=False)


def ordered(bit, own, other):
    return jnp.where(bit == 0, jnp.stack([own, other]), jnp.stack([other, own]))


def slot_of(t, m, g, members):
    shift = members.bit_length() - 1
    return jnp.bitwise_xor(jnp.bitwise_and(t, members - 1), m) * NG + jnp.bitwise_xor(
        jnp.right_shift(t, shift), g
    )


def fwd_kernel(members, block, scal, st_ref, en_ref, q_ref, *rest):
    kv_refs = rest[:members]
    o_ref, ob_ref, lse_ref, k_scr, v_scr = rest[members:]
    m_id, g_id = scal[0], scal[1]
    cols = NG * block
    for s in range(members):
        for h in range(HG):
            k_scr[h, s * cols : (s + 1) * cols, :] = kv_refs[s][h * HD : (h + 1) * HD, :].T
        v_scr[:, s * cols : (s + 1) * cols] = kv_refs[s][GW:, :]
    for j in range(NG):
        qs = slice(j * block, (j + 1) * block)
        start = st_ref[:, qs]
        end = en_ref[:, qs]
        qts = [q_ref[h * HD : (h + 1) * HD, qs] for h in range(HG)]

        def step(t, carry, start=start, end=end, qts=qts):
            off = pl.multiple_of(slot_of(t, m_id, g_id, members) * block, block)
            kpos = t * block + lax.broadcasted_iota(jnp.int32, (block, block), 0)
            allowed = (kpos >= start) & (kpos < end)
            out = []
            for h in range(HG):
                top, total, acc = carry[h]
                s = dot(k_scr[h, pl.ds(off, block), :], qts[h]) * (SCALE * LOG2E)
                s = jnp.where(allowed, s, NEG)
                new = jnp.maximum(top, jnp.max(s, axis=0, keepdims=True))
                alpha = jnp.exp2(top - new)
                p = jnp.exp2(s - new)
                total = total * alpha + jnp.sum(p, axis=0, keepdims=True)
                acc = acc * alpha + dot(
                    v_scr[h * HD : (h + 1) * HD, pl.ds(off, block)], p.astype(bf16)
                )
                out.append((new, total, acc))
            return tuple(out)

        init = tuple(
            (
                jnp.full((1, block), NEG, f32),
                jnp.zeros((1, block), f32),
                jnp.zeros((HD, block), f32),
            )
            for _ in range(HG)
        )
        done = lax.fori_loop(scal[2 + j], scal[2 + NG + j], step, init)
        for h in range(HG):
            top, total, acc = done[h]
            o = acc / total
            o_ref[h * HD : (h + 1) * HD, qs] = o
            ob_ref[h * HD : (h + 1) * HD, qs] = o.astype(bf16)
            lse_ref[h : h + 1, qs] = top + jnp.log2(total)


def bwd_kernel(members, block, scal, st_ref, en_ref, q_ref, o_ref, lse_ref, do_ref, *rest):
    kv_refs = rest[:members]
    dq_ref, dkv_ref, k_scr, v_scr, kt_scr, dk_scr, dv_scr = rest[members:]
    m_id, g_id = scal[0], scal[1]
    cols = NG * block
    for s in range(members):
        part = slice(s * cols, (s + 1) * cols)
        for h in range(HG):
            k_scr[h, part, :] = kv_refs[s][h * HD : (h + 1) * HD, :].T
            v_scr[h, part, :] = kv_refs[s][GW + h * HD : GW + (h + 1) * HD, :].T
        kt_scr[:, part] = kv_refs[s][:GW, :]
    dk_scr[...] = jnp.zeros_like(dk_scr)
    dv_scr[...] = jnp.zeros_like(dv_scr)
    for j in range(NG):
        qs = slice(j * block, (j + 1) * block)
        start = st_ref[:, qs]
        end = en_ref[:, qs]
        per_head = []
        for h in range(HG):
            hr = slice(h * HD, (h + 1) * HD)
            qt = q_ref[hr, qs]
            dot_t = do_ref[hr, qs]
            delta = jnp.sum(dot_t.astype(f32) * o_ref[hr, qs], axis=0, keepdims=True)
            per_head.append((qt, qt.T, dot_t, dot_t.T, delta, lse_ref[h : h + 1, qs]))

        def step(t, carry, start=start, end=end, per_head=per_head):
            off = pl.multiple_of(slot_of(t, m_id, g_id, members) * block, block)
            kpos = t * block + lax.broadcasted_iota(jnp.int32, (block, block), 0)
            allowed = (kpos >= start) & (kpos < end)
            out = []
            for h in range(HG):
                qt, q, dot_t, do, delta, lse = per_head[h]
                s = dot(k_scr[h, pl.ds(off, block), :], qt) * (SCALE * LOG2E)
                p = jnp.where(allowed, jnp.exp2(s - lse), 0.0)
                dp = dot(v_scr[h, pl.ds(off, block), :], dot_t)
                ds = (p * (dp - delta)).astype(bf16)
                dv_scr[h, pl.ds(off, block), :] += dot(p.astype(bf16), do)
                dk_scr[h, pl.ds(off, block), :] += dot(ds, q)
                out.append(
                    carry[h] + dot(kt_scr[h * HD : (h + 1) * HD, pl.ds(off, block)], ds)
                )
            return tuple(out)

        init = tuple(jnp.zeros((HD, block), f32) for _ in range(HG))
        done = lax.fori_loop(scal[2 + j], scal[2 + NG + j], step, init)
        for h in range(HG):
            dq_ref[h * HD : (h + 1) * HD, qs] = (done[h] * SCALE).astype(bf16)
    for s in range(members):
        part = slice(s * cols, (s + 1) * cols)
        for h in range(HG):
            dkv_ref[s, h * HD : (h + 1) * HD, :] = (dk_scr[h, part, :] * SCALE).T.astype(bf16)
            dkv_ref[s, GW + h * HD : GW + (h + 1) * HD, :] = dv_scr[h, part, :].T.astype(bf16)


def whole_specs(n):
    return [pl.BlockSpec(memory_space=pltpu.SMEM)] + [
        pl.BlockSpec(memory_space=pltpu.VMEM) for _ in range(n)
    ]


def attend(members, block, scal, starts, ends, q, kvs):
    keys = members * NG * block
    rows = NG * block
    return pl.pallas_call(
        functools.partial(fwd_kernel, members, block),
        out_shape=(
            jax.ShapeDtypeStruct((GW, rows), f32),
            jax.ShapeDtypeStruct((GW, rows), bf16),
            jax.ShapeDtypeStruct((HG, rows), f32),
        ),
        in_specs=whole_specs(3 + members),
        out_specs=[pl.BlockSpec(memory_space=pltpu.VMEM) for _ in range(3)],
        scratch_shapes=[
            pltpu.VMEM((HG, keys, HD), bf16),
            pltpu.VMEM((GW, keys), bf16),
        ],
        compiler_params=pltpu.CompilerParams(vmem_limit_bytes=50 << 20),
        name="attend",
    )(scal, starts, ends, q, *kvs)


def attend_back(members, block, scal, starts, ends, q, o, lse, do, kvs):
    keys = members * NG * block
    rows = NG * block
    return pl.pallas_call(
        functools.partial(bwd_kernel, members, block),
        out_shape=(
            jax.ShapeDtypeStruct((GW, rows), bf16),
            jax.ShapeDtypeStruct((members, 2 * GW, rows), bf16),
        ),
        in_specs=whole_specs(6 + members),
        out_specs=[pl.BlockSpec(memory_space=pltpu.VMEM) for _ in range(2)],
        scratch_shapes=[
            pltpu.VMEM((HG, keys, HD), bf16),
            pltpu.VMEM((HG, keys, HD), bf16),
            pltpu.VMEM((GW, keys), bf16),
            pltpu.VMEM((HG, keys, HD), f32),
            pltpu.VMEM((HG, keys, HD), f32),
        ],
        compiler_params=pltpu.CompilerParams(vmem_limit_bytes=56 << 20),
        name="attend_back",
    )(scal, starts, ends, q, o, lse, do, *kvs)


def on_device(
    tokens,
    query_weight,
    query_bias,
    key_weight,
    value_weight,
    value_bias,
    out_weight,
    out_bias,
    first_gain,
    first_shift,
    inner_weight,
    inner_bias,
    outer_weight,
    outer_bias,
    second_gain,
    second_shift,
    doc_lengths,
    grad_output,
):
    block = tokens.shape[1]
    width = tokens.shape[2]
    ctx = lax.axis_size("ctx")
    fs = lax.axis_size("fsdp")
    members = ctx // NG
    ci = lax.axis_index("ctx")
    fi = lax.axis_index("fsdp")
    g_id = ci // members
    m_id = ci % members
    core = ci % 2
    own_rows = width // fs
    m_bits = []
    b = members // 2
    while b >= 1:
        m_bits.append(b)
        b //= 2
    g_slots = range(NG)

    def bit_of(index, bit):
        return (index // bit) % 2

    def gather_rows(w):
        rows = w.shape[0]
        if fs != 2:
            return lax.all_gather(w, "fsdp", axis=0, tiled=True)
        half = rows // 2
        mine = swap(lax.dynamic_slice_in_dim(w, core * half, half, 0), "fsdp", 1)
        others = swap(mine, "ctx", 1)
        other = ordered(core, mine, others).reshape(w.shape)
        return ordered(fi, w, other).reshape((2 * rows,) + w.shape[1:])

    local = tokens[0]
    x_slots = {0: local}
    x_slots[2] = swap(local, "ctx", 2 * members)
    x_slots[1] = swap(local, "ctx", members)
    x_slots[3] = swap(x_slots[2], "ctx", members)
    x_all = jnp.concatenate([x_slots[j] for j in g_slots], axis=0)

    vectors = [
        query_bias,
        value_bias,
        out_bias,
        first_gain,
        first_shift,
        inner_bias,
        outer_bias,
        second_gain,
        second_shift,
    ]
    sizes = [v.shape[0] for v in vectors]
    packed = lax.all_gather(jnp.concatenate(vectors), "fsdp", axis=0, tiled=False)
    at = 0
    full = []
    for n in sizes:
        full.append(packed[:, at : at + n].reshape(-1).astype(f32))
        at += n
    qbias, vbias, obias, gain_one, shift_one, ibias, outbias, gain_two, shift_two = full

    group_cols = [
        lax.dynamic_slice_in_dim(w, g_id * GW, GW, 1)
        for w in (query_weight, key_weight, value_weight)
    ]
    w_group = lax.all_gather(
        jnp.concatenate(group_cols, axis=1), "fsdp", axis=0, tiled=True
    ) if fs != 2 else None
    if fs == 2:
        mine = jnp.concatenate(group_cols, axis=1)
        w_group = ordered(fi, mine, swap(mine, "fsdp", 1)).reshape(width, 3 * GW)
    out_full = gather_rows(out_weight)
    inner_full = gather_rows(inner_weight)
    outer_full = gather_rows(outer_weight)
    qkv_full = gather_rows(jnp.concatenate([query_weight, key_weight, value_weight], axis=1))

    bias_group = jnp.concatenate(
        [
            lax.dynamic_slice_in_dim(qbias, g_id * GW, GW, 0),
            jnp.zeros((GW,), f32),
            lax.dynamic_slice_in_dim(vbias, g_id * GW, GW, 0),
        ]
    )
    qkv = (dot(w_group, x_all, 0, 1) + bias_group[:, None]).astype(bf16)
    q_t = qkv[:GW]
    kv_slots = {0: qkv[GW:]}
    for b in m_bits:
        for s in sorted(kv_slots):
            kv_slots[s ^ b] = swap(kv_slots[s], "ctx", b)
    kvs = [kv_slots[s] for s in range(members)]

    doc_ends = jnp.cumsum(doc_lengths[0])
    first = jnp.stack([(jnp.bitwise_xor(g_id, j) * members + m_id) * block for j in g_slots])
    places = (first[:, None] + jnp.arange(block, dtype=jnp.int32)[None, :]).reshape(-1)
    before = places[:, None] >= doc_ends[None, :]
    starts = jnp.max(jnp.where(before, doc_ends[None, :], 0), axis=1).astype(jnp.int32)
    ends = jnp.min(jnp.where(before, ctx * block, doc_ends[None, :]), axis=1).astype(jnp.int32)
    low = starts.reshape(NG, block)[:, 0] // block
    high = (ends.reshape(NG, block)[:, -1] + block - 1) // block
    scal = jnp.concatenate([jnp.stack([m_id, g_id]), low, high]).astype(jnp.int32)
    starts = starts[None]
    ends = ends[None]

    o_t, ob_t, lse = attend(members, block, scal, starts, ends, q_t, kvs)

    def column(v, j):
        return v[:, j * block : (j + 1) * block]

    def exchange(parts):
        return [parts[0]] + [swap(parts[j], "ctx", j * members) for j in range(1, NG)]

    def by_group(slots):
        return [
            lax.select_n(g_id, *[slots[a ^ k] for k in g_slots]) for a in g_slots
        ]

    attn_t = jnp.concatenate(by_group(exchange([column(ob_t, j) for j in g_slots])), axis=0)
    branch = dot(attn_t, out_full, 0, 0) + obias
    local_float = local.astype(f32)
    hidden, first_back = jax.vjp(layer_norm, local_float + branch, gain_one, shift_one)
    hidden_low = hidden.astype(bf16)
    inner = dot(hidden_low, inner_full) + ibias
    active, gelu_back = jax.vjp(gelu_exact, inner)
    active_low = active.astype(bf16)
    outer = dot(active_low, outer_full) + outbias
    result, second_back = jax.vjp(layer_norm, hidden + outer, gain_two, shift_two)
    output = result.astype(bf16)[None]
    grad_y = grad_output[0].astype(f32)
    d_second, grad_gain_two, grad_shift_two = second_back(grad_y)
    d_outer_low = d_second.astype(bf16)
    grad_outbias = jnp.sum(d_outer_low.astype(f32), axis=0)
    (d_inner,) = gelu_back(dot(d_outer_low, outer_full, 1, 1))
    d_inner_low = d_inner.astype(bf16)
    grad_ibias = jnp.sum(d_inner_low.astype(f32), axis=0)
    d_hidden = d_second + dot(d_inner_low, inner_full, 1, 1)
    d_first, grad_gain_one, grad_shift_one = first_back(d_hidden)
    d_branch_low = d_first.astype(bf16)
    grad_obias = jnp.sum(d_branch_low.astype(f32), axis=0)
    do_t = dot(out_full, d_branch_low, 1, 1).astype(bf16).reshape(NG, GW, block)
    do_parts = [pick(do_t, jnp.bitwise_xor(g_id, j)) for j in g_slots]
    do_all = jnp.concatenate(exchange(do_parts), axis=1)

    def halve(acc, axis, bit, index):
        acc = acc.reshape((2, acc.shape[0] // 2) + acc.shape[1:])
        mine = bit_of(index, bit)
        got = swap(pick(acc, 1 - mine), axis, bit)
        return (pick(acc, mine).astype(f32) + got.astype(f32)).astype(bf16)

    def reduce_rows(product, left, bits):
        rows = left.shape[0] // (2 * fs)
        split = left.reshape(fs, 2, rows, left.shape[1])
        send = product(pick(split, 1 - core, 1).reshape(fs * rows, -1)).astype(bf16)
        keep = product(pick(split, core, 1).reshape(fs * rows, -1))
        acc = (keep + swap(send, "ctx", 1).astype(f32)).astype(bf16)
        n = fs
        while n > 1:
            n //= 2
            acc = halve(acc, "fsdp", n, fi)
        for b in bits:
            acc = halve(acc, "ctx", b, ci)
        return acc

    def join(acc, bit):
        both = ordered(bit_of(ci, bit), acc, swap(acc, "ctx", bit))
        return both.reshape((2 * acc.shape[0],) + acc.shape[1:])

    x_bits = [b for b in m_bits if b > 1]
    all_bits = x_bits + [members, 2 * members]

    def weight_grad(left_t, right, rdim=0):
        acc = reduce_rows(lambda part: dot(part, right, 1, rdim), left_t, all_bits)
        for b in all_bits[::-1]:
            acc = join(acc, b)
        return join(acc, 1).astype(f32)

    grad_outer = weight_grad(active_low.T, d_outer_low)
    grad_inner = weight_grad(hidden_low.T, d_inner_low)
    grad_out = weight_grad(attn_t, d_branch_low)

    dq_t, dkv = attend_back(members, block, scal, starts, ends, q_t, o_t, lse, do_all, kvs)
    dkv_slots = {s: dkv[s] for s in range(members)}
    for b in m_bits[::-1]:
        for s in sorted(dkv_slots):
            if s & b:
                got = swap(dkv_slots.pop(s), "ctx", b)
                dkv_slots[s ^ b] = (dkv_slots[s ^ b].astype(f32) + got.astype(f32)).astype(bf16)
    d_qkv = jnp.concatenate([dq_t, dkv_slots[0]], axis=0)
    back = by_group(exchange([column(d_qkv, j) for j in g_slots]))
    d_all = jnp.stack(back).reshape(NG, 3, GW, block).transpose(1, 0, 2, 3).reshape(3 * width, block)
    grad_input = d_first + dot(d_all, qkv_full, 0, 1)

    acc = reduce_rows(lambda part: dot(part, d_qkv, 1, 1), x_all.T, x_bits)
    acc = ordered(bit_of(ci, 2 * members), acc, swap(acc, "ctx", 2 * members))
    acc = ordered(bit_of(ci, members), acc, swap(acc, "ctx", members))
    lead = []
    for b in x_bits[::-1] + [1]:
        acc = ordered(bit_of(ci, b), acc, swap(acc, "ctx", b))
        lead.append(2)
    nb = len(lead)
    acc = acc.astype(f32)
    order = tuple(range(nb)) + (nb + 2, nb + 1, nb, nb + 3)
    acc = acc.transpose(order).reshape(own_rows, NG, 3, GW).transpose(2, 0, 1, 3)
    grad_query, grad_key, grad_value = acc.reshape(3, own_rows, width)

    group_sums = jnp.sum(d_qkv.astype(f32), axis=1)
    spread = (jnp.arange(NG) == g_id)[:, None]
    grad_qbias = jnp.where(spread, group_sums[None, :GW], 0.0).reshape(-1)
    grad_vbias = jnp.where(spread, group_sums[None, 2 * GW :], 0.0).reshape(-1)
    terms = [
        grad_qbias,
        grad_vbias,
        grad_obias,
        grad_gain_one,
        grad_shift_one,
        grad_ibias,
        grad_outbias,
        grad_gain_two,
        grad_shift_two,
    ]
    summed = lax.psum(jnp.concatenate([t.reshape(fs, -1) for t in terms], axis=1), ("fsdp", "ctx"))
    mine = pick(summed, fi)
    shares = []
    at = 0
    for n in sizes:
        shares.append(mine[at : at + n])
        at += n
    s_q, s_v, s_o, s_g1, s_s1, s_i, s_out, s_g2, s_s2 = shares
    return (
        output,
        grad_input[None],
        grad_query,
        s_q,
        grad_key,
        grad_value,
        s_v,
        grad_out,
        s_o,
        s_g1,
        s_s1,
        grad_inner,
        s_i,
        grad_outer,
        s_out,
        s_g2,
        s_s2,
    )


def vmem(n):
    return [pl.BlockSpec(memory_space=pltpu.VMEM) for _ in range(n)]


def anyspec(n):
    return [pl.BlockSpec(memory_space=pl.ANY) for _ in range(n)]


CHEAP = pl.CostEstimate(flops=1, transcendentals=0, bytes_accessed=1)
EXTRA = 8
SPARE = 64
SMEM = pl.BlockSpec(memory_space=pltpu.SMEM)


def params(mib=56):
    return pltpu.CompilerParams(vmem_limit_bytes=mib << 20)


def project_kernel(
    block, scal, x0, x1, x2, x3, own, small, small_oth, mine, sib, q_ref, kv_ref, row_scr, bias_scr, w_scr, sems
):
    g_id, fi, core = scal[0], scal[1], scal[2]
    half = own.shape[0]
    quarter = half // 2
    copies = [
        pltpu.make_async_copy(
            part, w_scr.at[pl.ds(pl.multiple_of(c * quarter, 64), quarter), :], sems.at[k]
        )
        for k, (part, c) in enumerate(((mine, core), (sib, 1 - core)))
    ]
    for c in copies:
        c.start()
    w_own = own[...].T
    at_own = pl.multiple_of(fi * half, 128)
    at_oth = pl.multiple_of((1 - fi) * half, 128)
    row_scr[:, pl.ds(at_own, half)] = small[6:8, :].astype(f32)
    row_scr[:, pl.ds(at_oth, half)] = small_oth[6:8, :].astype(f32)
    bias_scr[...] = jnp.zeros_like(bias_scr)
    for g in range(NG):

        @pl.when(g_id == g)
        def _(g=g):
            bias_scr[0:1, :GW] = row_scr[0:1, g * GW : (g + 1) * GW]
            bias_scr[0:1, 2 * GW :] = row_scr[1:2, g * GW : (g + 1) * GW]

    bias = bias_scr[...].T[:, :1]
    for c in copies:
        c.wait()
    w_oth = w_scr[...].T
    for j, x in enumerate((x0, x1, x2, x3)):
        cols = slice(j * block, (j + 1) * block)
        res = dot(w_own, x[:, pl.ds(at_own, half)], 1, 1)
        res += dot(w_oth, x[:, pl.ds(at_oth, half)], 1, 1)
        res = (res + bias).astype(bf16)
        q_ref[:, cols] = res[:GW]
        kv_ref[:, cols] = res[GW:]


def project(block, scal, xs, own, mine, sib, small, small_oth):
    rows = NG * block
    return pl.pallas_call(
        functools.partial(project_kernel, block),
        out_shape=(
            jax.ShapeDtypeStruct((GW, rows), bf16),
            jax.ShapeDtypeStruct((2 * GW, rows), bf16),
        ),
        in_specs=[SMEM] + vmem(7) + anyspec(2),
        out_specs=vmem(2),
        scratch_shapes=[
            pltpu.VMEM((2, 2 * own.shape[0]), f32),
            pltpu.VMEM((8, 3 * GW), f32),
            pltpu.VMEM(own.shape, bf16),
            pltpu.SemaphoreType.DMA((2,)),
        ],
        cost_estimate=CHEAP,
        compiler_params=params(),
        name="project",
    )(scal, *xs, own, small, small_oth, mine, sib)


def pack_kernel(*refs):
    out = refs[-1]
    n = out.shape[1]
    at = 0
    for ref in refs[:-1]:
        for k in range(ref.shape[0] // n):
            out[at : at + 1, :] = ref[k * n : (k + 1) * n].reshape(1, n)
            at += 1


def pack(vectors):
    n = vectors[0].shape[0]
    rows = sum(v.shape[0] for v in vectors) // n
    return pl.pallas_call(
        pack_kernel,
        out_shape=jax.ShapeDtypeStruct((rows, n), bf16),
        in_specs=vmem(len(vectors)),
        out_specs=vmem(1)[0],
        compiler_params=params(),
        name="pack",
    )(*vectors)


def tile_offset(t, scal, members, block):
    return pl.multiple_of(slot_of(t, scal[0], scal[1], members) * block, block)


UNROLL = 4


def key_loop(scal, j, block, tiles, init):
    low, high, inner_low, inner_high = (scal[2 + NG * i + j] for i in range(4))
    many = (inner_high - inner_low) // UNROLL
    rest = inner_low + UNROLL * many
    before = inner_low - low
    edges = before + high - rest

    def several(i, c):
        return tiles([inner_low + UNROLL * i + u for u in range(UNROLL)], None, c)

    def pair(i, c):
        ts, firsts = [], []
        for u in range(2):
            e = 2 * i + u
            t = jnp.minimum(jnp.where(e < before, low + e, rest + e - before), high - 1)
            ts.append(t)
            firsts.append(jnp.where(e < edges, t * block, -(1 << 30)))
        return tiles(ts, firsts, c)

    carry = lax.fori_loop(0, many, several, init)
    return lax.fori_loop(0, (edges + 1) // 2, pair, carry)


def inside(first, start, end, block):
    kpos = first + lax.broadcasted_iota(jnp.int32, (block, block), 0)
    return (kpos >= start) & (kpos < end)


def staged(n, first, second, third):
    one, two = {}, {}
    for i in range(n + 2):
        if i < n:
            one[i] = first(i)
        if 0 <= i - 1 < n:
            two[i - 1] = second(i - 1, one.pop(i - 1))
        if 0 <= i - 2 < n:
            third(i - 2, two.pop(i - 2))


def group_fwd_kernel(members, block, scal, st_ref, en_ref, q_ref, *rest):
    kv_refs = rest[:members]
    o_ref, lse_ref = rest[members : members + 2]
    ob_refs = rest[members + 2 : members + 2 + NG]
    k_scr, v_scr = rest[members + 2 + NG :]
    cols = NG * block
    for s in range(members):
        for h in range(HG):
            k_scr[h, s * cols : (s + 1) * cols, :] = kv_refs[s][h * HD : (h + 1) * HD, :].T
        v_scr[:, s * cols : (s + 1) * cols] = kv_refs[s][GW:, :]

    @pl.loop(0, NG)
    def _(j):
        cut = pl.ds(pl.multiple_of(j * block, block), block)
        start = st_ref[:, cut]
        end = en_ref[:, cut]
        qts = [q_ref[h * HD : (h + 1) * HD, cut] for h in range(HG)]

        def tiles(ts, firsts, carry):
            offs = [tile_offset(t, scal, members, block) for t in ts]
            allowed = firsts and [inside(first, start, end, block) for first in firsts]
            out = [None] * HG

            def first(h):
                return [dot(k_scr[h, pl.ds(off, block), :], qts[h]) for off in offs]

            def second(h, scores):
                top, total, acc = carry[h]
                if allowed:
                    scores = [jnp.where(a, s, NEG) for a, s in zip(allowed, scores)]
                new = top
                for s in scores:
                    new = jnp.maximum(new, jnp.max(s, axis=0, keepdims=True))
                alpha = jnp.exp2((top - new) * (SCALE * LOG2E))
                total = total * alpha
                probs = []
                for s in scores:
                    p = jnp.exp2((s - new) * (SCALE * LOG2E))
                    total += jnp.sum(p, axis=0, keepdims=True)
                    probs.append(p.astype(bf16))
                return probs, new, total, acc * alpha

            def third(h, state):
                probs, new, total, acc = state
                for p, off in zip(probs, offs):
                    acc += dot(v_scr[h * HD : (h + 1) * HD, pl.ds(off, block)], p)
                out[h] = (new, total, acc)

            staged(HG, first, second, third)
            return tuple(out)

        init = tuple(
            (
                jnp.full((1, block), NEG, f32),
                jnp.zeros((1, block), f32),
                jnp.zeros((HD, block), f32),
            )
            for _ in range(HG)
        )
        done = key_loop(scal, j, block, tiles, init)
        for h in range(HG):
            top, total, acc = done[h]
            o = acc / total
            o_ref[h * HD : (h + 1) * HD, cut] = o
            lse_ref[h : h + 1, cut] = top * (SCALE * LOG2E) + jnp.log2(total)

    for k in range(NG):
        ob_refs[k][...] = o_ref[:, k * block : (k + 1) * block].astype(bf16)


def group_fwd(members, block, scal, starts, ends, q, kvs):
    keys = members * NG * block
    rows = NG * block
    return pl.pallas_call(
        functools.partial(group_fwd_kernel, members, block),
        out_shape=(
            jax.ShapeDtypeStruct((GW, rows), f32),
            jax.ShapeDtypeStruct((HG, rows), f32),
        )
        + tuple(jax.ShapeDtypeStruct((GW, block), bf16) for _ in range(NG)),
        in_specs=[SMEM] + vmem(3 + members),
        out_specs=vmem(2 + NG),
        scratch_shapes=[
            pltpu.VMEM((HG, keys, HD), bf16),
            pltpu.VMEM((GW, keys), bf16),
        ],
        cost_estimate=CHEAP,
        compiler_params=params(),
        name="group_fwd",
    )(scal, starts, ends, q, *kvs)


def group_bwd_kernel(members, block, scal, st_ref, en_ref, q_ref, o_ref, lse_ref, *rest):
    do_refs = rest[:NG]
    kv_refs = rest[NG : NG + members]
    dq_ref = rest[NG + members]
    dkv_refs = rest[NG + members + 1 : NG + 2 * members + 1]
    k_scr, v_scr, dk_scr, dv_scr, do_scr = rest[NG + 2 * members + 1 :]
    cols = NG * block
    heads = [slice(h * HD, (h + 1) * HD) for h in range(HG)]
    for s in range(members):
        part = slice(s * cols, (s + 1) * cols)
        k_scr[:, part] = kv_refs[s][:GW, :]
        v_scr[:, part] = kv_refs[s][GW:, :]
    dk_scr[...] = jnp.zeros_like(dk_scr)
    dv_scr[...] = jnp.zeros_like(dv_scr)
    for k in range(NG):
        do_scr[:, k * block : (k + 1) * block] = do_refs[k][...]

    @pl.loop(0, NG)
    def _(j):
        cut = pl.ds(pl.multiple_of(j * block, block), block)
        start = st_ref[:, cut]
        end = en_ref[:, cut]
        per_head = []
        for h in range(HG):
            do = do_scr[heads[h], cut]
            delta = jnp.sum(do.astype(f32) * o_ref[heads[h], cut], axis=0, keepdims=True)
            per_head.append((q_ref[heads[h], cut], do, delta, lse_ref[h : h + 1, cut]))

        def tiles(ts, firsts, carry):
            out = list(carry)
            work = []
            for u, t in enumerate(ts):
                keys = pl.ds(tile_offset(t, scal, members, block), block)
                allowed = None if firsts is None else inside(firsts[u], start, end, block)
                work += [(h, keys, allowed) for h in range(HG)]

            def first(i):
                h, keys, _ = work[i]
                q, do, _, _ = per_head[h]
                return dot(k_scr[heads[h], keys], q, 0, 0), dot(v_scr[heads[h], keys], do, 0, 0)

            def second(i, pair):
                h, _, allowed = work[i]
                _, _, delta, lse = per_head[h]
                s, dp = pair
                p = jnp.exp2(s * (SCALE * LOG2E) - lse)
                if allowed is not None:
                    p = jnp.where(allowed, p, 0.0)
                return p.astype(bf16), (p * (dp - delta)).astype(bf16)

            def third(i, pair):
                h, keys, _ = work[i]
                q, do, _, _ = per_head[h]
                p, ds = pair
                dv_scr[heads[h], keys] += dot(do, p, 1, 1)
                dk_scr[heads[h], keys] += dot(q, ds, 1, 1)
                out[h] = out[h] + dot(k_scr[heads[h], keys], ds)

            staged(len(work), first, second, third)
            return tuple(out)

        init = tuple(jnp.zeros((HD, block), f32) for _ in range(HG))
        done = key_loop(scal, j, block, tiles, init)
        for h in range(HG):
            dq_ref[heads[h], cut] = (done[h] * SCALE).astype(bf16)

    for s in range(members):
        part = slice(s * cols, (s + 1) * cols)
        dkv_refs[s][:GW, :] = (dk_scr[:, part] * SCALE).astype(bf16)
        dkv_refs[s][GW:, :] = dv_scr[:, part].astype(bf16)


def group_bwd(members, block, scal, starts, ends, q, o, lse, dos, kvs):
    keys = members * NG * block
    rows = NG * block
    return pl.pallas_call(
        functools.partial(group_bwd_kernel, members, block),
        out_shape=(jax.ShapeDtypeStruct((GW, rows), bf16),)
        + tuple(jax.ShapeDtypeStruct((2 * GW, rows), bf16) for _ in range(members)),
        in_specs=[SMEM] + vmem(5 + NG + members),
        out_specs=vmem(1 + members),
        scratch_shapes=[
            pltpu.VMEM((GW, keys), bf16),
            pltpu.VMEM((GW, keys), bf16),
            pltpu.VMEM((GW, keys), f32),
            pltpu.VMEM((GW, keys), f32),
            pltpu.VMEM((GW, rows), bf16),
        ],
        cost_estimate=CHEAP,
        compiler_params=params(),
        name="group_bwd",
    )(scal, starts, ends, q, o, lse, *dos, *kvs)


def normalize(r, width):
    mean = jnp.sum(r, axis=1, keepdims=True) * (1.0 / width)
    centered = r - mean
    var = jnp.sum(centered * centered, axis=1, keepdims=True) * (1.0 / width)
    rstd = lax.rsqrt(var + eps)
    return centered * rstd, rstd


def norm_back(dy, hat, rstd, gain, width):
    dhat = dy * gain
    one = jnp.sum(dhat, axis=1, keepdims=True) * (1.0 / width)
    two = jnp.sum(dhat * hat, axis=1, keepdims=True) * (1.0 / width)
    return rstd * (dhat - one - hat * two)


INV_SQRT2 = 0.7071067811865476
INV_SQRT2PI = 0.3989422804014327


def middle_kernel(block, *refs):
    scal = refs[0]
    at = 1
    o_refs = refs[at : at + NG]
    at += NG
    x_ref, dy_ref, small, small_oth = refs[at : at + 4]
    at += 4
    out_parts = refs[at : at + 3]
    inner_parts = refs[at + 3 : at + 8]
    outer_parts = refs[at + 8 : at + 13]
    at += 13
    y_ref, dr_ref = refs[at : at + 2]
    at += 2
    do_refs = refs[at : at + NG]
    at += NG
    grad_outs = refs[at : at + 4]
    at += 4
    ot_scr, wout, winner, wouter, hbt, gt_scr, gp_scr, dot_scr, vec_ref, ib_ref, sums_ref, acc_ref = refs[at : at + 12]
    grad_refs = refs[at + 12 : at + 16]
    keeps, sends = grad_refs[:2], grad_refs[2:]
    sems = refs[at + 16]
    g_id, fi, core = scal[0], scal[1], scal[2]
    width = x_ref.shape[1]
    ffq = winner.shape[2]
    half = width // 2
    quarter = width // 4

    copies = []

    def load(src, dst):
        copies.append(pltpu.make_async_copy(src, dst, sems.at[len(copies)]))
        copies[-1].start()

    def rows_of(full):
        own = fi * (full // 2)
        oth = (1 - fi) * (full // 2)
        q = full // 4
        return (
            pl.ds(pl.multiple_of(own, 64), full // 2),
            pl.ds(pl.multiple_of(oth + core * q, 64), q),
            pl.ds(pl.multiple_of(oth + (1 - core) * q, 64), q),
        )

    for part, rows in zip(out_parts, rows_of(width)):
        load(part, wout.at[rows, :])
    own, mine, sib = (r.start for r in rows_of(width))
    unit = width // 16
    inner_rows = [pl.ds(own, 8 * unit)] + [
        pl.ds(pl.multiple_of(first + k * unit, 16), n * unit)
        for first in (mine, sib)
        for k, n in ((0, 1), (1, 3))
    ]
    for a in range(4):
        for part, rows in zip(inner_parts, inner_rows):
            load(part.at[:, a * ffq : (a + 1) * ffq], winner.at[a, rows, :])
    own, mine, sib = (r.start for r in rows_of(4 * ffq))
    unit = ffq // 4
    outer_rows = [pl.ds(own, 8 * unit)] + [
        pl.ds(pl.multiple_of(first + k * unit, 16), n * unit)
        for first in (mine, sib)
        for k, n in ((0, 1), (1, 3))
    ]
    for part, rows in zip(outer_parts, outer_rows):
        load(part, wouter.at[rows, :])

    for j in range(NG):
        row = pl.multiple_of(jnp.bitwise_xor(g_id, j) * GW, HD)
        ot_scr[pl.ds(row, GW), :] = o_refs[j][...]
    for side, y in ((small, fi), (small_oth, 1 - fi)):
        vec_ref[:, pl.ds(pl.multiple_of(y * half, 128), half)] = side[:8, :].astype(f32)
        for c in range(2):
            for k in range(2):
                ib_ref[pl.ds(2 * y + c, 1), k * half : (k + 1) * half] = side[
                    8 + 2 * c + k : 9 + 2 * c + k, :
                ].astype(f32)
    for c in copies[:3]:
        c.wait()
    vec = [vec_ref[i : i + 1, :] for i in range(8)]
    obias, gain1, shift1, outbias, gain2, shift2 = vec[:6]
    attn = ot_scr[...].T
    r1 = x_ref[...].astype(f32) + dot(attn, wout[...]) + obias
    hat1, rstd1 = normalize(r1, width)
    hn = hat1 * gain1 + shift1
    hb = hn.astype(bf16)
    hb_t = hb.T
    for y in range(2):
        for c in range(2):
            piece = hb_t[(2 * y + c) * quarter : (2 * y + c + 1) * quarter]

            @pl.when(core == c)
            def _(piece=piece, y=y):
                hbt[y * quarter : (y + 1) * quarter, :] = piece

            @pl.when(core != c)
            def _(piece=piece, y=y):
                hbt[half + y * quarter : half + (y + 1) * quarter, :] = piece

    for c in copies[3:]:
        c.wait()
    acc_ref[...] = hn + outbias

    @pl.loop(0, 4)
    def _(a):
        u = dot(hb, winner[a]) + ib_ref[pl.ds(a, 1), :]
        phi = 0.5 + 0.5 * lax.erf(u * INV_SQRT2)
        g = (u * phi).astype(bf16)
        gp_scr[a] = phi + u * (jnp.exp(u * u * -0.5) * INV_SQRT2PI)
        gt_scr[a] = g.T
        acc_ref[...] += dot(g, wouter[pl.ds(pl.multiple_of(a * ffq, ffq), ffq), :])

    z = acc_ref[...]
    hat2, rstd2 = normalize(z, width)
    y_ref[...] = (hat2 * gain2 + shift2).astype(bf16)
    dy = dy_ref[...].astype(f32)
    sums_ref[4:5, :] = jnp.sum(dy * hat2, axis=0, keepdims=True)
    sums_ref[5:6, :] = jnp.sum(dy, axis=0, keepdims=True)
    dz = norm_back(dy, hat2, rstd2, gain2, width)
    dzb = dz.astype(bf16)
    sums_ref[3:4, :] = jnp.sum(dzb.astype(f32), axis=0, keepdims=True)
    acc_ref[...] = dz

    @pl.loop(0, 4)
    def _(a):
        dg = dot(dzb, wouter[pl.ds(pl.multiple_of(a * ffq, ffq), ffq), :], 1, 1)
        du = (dg * gp_scr[a]).astype(bf16)
        sums_ref[pl.ds(6 + a, 1), :] = jnp.sum(du.astype(f32), axis=0, keepdims=True)
        acc_ref[...] += dot(du, winner[a], 1, 1)
        grad = dot(hbt[...], du).astype(bf16)
        rows = pl.ds(pl.multiple_of(a * quarter, 64), quarter)
        for y in range(2):
            keeps[0][y, rows] = grad[y * quarter : (y + 1) * quarter]
            sends[0][y, rows] = grad[half + y * quarter : half + (y + 1) * quarter]
        grad = dot(gt_scr[a], dzb).astype(bf16)
        mine = core == jnp.bitwise_and(a, 1)

        @pl.when(mine)
        def _():
            keeps[1][jnp.right_shift(a, 1), :ffq] = grad

        @pl.when(jnp.logical_not(mine))
        def _():
            sends[1][jnp.right_shift(a, 1), :ffq] = grad

    dh = acc_ref[...]
    stored = []

    def store(rows):
        for src, dst in zip(grad_refs, grad_outs):
            part = slice(*rows(src.shape[1]))
            sem = sems.at[len(copies) + len(stored)]
            stored.append(pltpu.make_async_copy(src.at[:, part], dst.at[:, part], sem))
            stored[-1].start()

    store(lambda n: (0, ffq))
    sums_ref[1:2, :] = jnp.sum(dh * hat1, axis=0, keepdims=True)
    sums_ref[2:3, :] = jnp.sum(dh, axis=0, keepdims=True)
    dr = norm_back(dh, hat1, rstd1, gain1, width)
    dr_ref[...] = dr
    dab = dr.astype(bf16)
    sums_ref[0:1, :] = jnp.sum(dab.astype(f32), axis=0, keepdims=True)
    for y in range(2):
        top = jnp.concatenate([sums_ref[0:6, :], sums_ref[6 + 2 * y : 8 + 2 * y, :]], axis=0)
        spare = jnp.concatenate([top, jnp.zeros((SPARE - 8, width), f32)], axis=0).astype(bf16)
        none = jnp.zeros((SPARE, width), bf16)

        @pl.when(core == 0)
        def _(y=y, spare=spare, none=none):
            keeps[0][y, 4 * quarter :] = spare
            sends[0][y, 4 * quarter :] = none

        @pl.when(core != 0)
        def _(y=y, spare=spare, none=none):
            keeps[0][y, 4 * quarter :] = none
            sends[0][y, 4 * quarter :] = spare

    dot_scr[...] = dot(wout[...], dab, 1, 1).astype(bf16)
    for j in range(NG):
        row = pl.multiple_of(jnp.bitwise_xor(g_id, j) * GW, HD)
        do_refs[j][...] = dot_scr[pl.ds(row, GW), :]
    grad = dot(ot_scr[...], dab).astype(bf16)
    for y in range(2):
        for c in range(2):
            piece = grad[(2 * y + c) * quarter : (2 * y + c + 1) * quarter]

            @pl.when(core == c)
            def _(piece=piece, y=y):
                keeps[1][y, ffq:] = piece

            @pl.when(core != c)
            def _(piece=piece, y=y):
                sends[1][y, ffq:] = piece

    store(lambda n: (ffq, n))
    for c in stored:
        c.wait()


def middle(block, scal, os, x, dy, small, small_oth, outs, inners, outers):
    width = x.shape[1]
    ffq = inners[0].shape[1] // 4
    q = width // 4
    grads = [
        jax.ShapeDtypeStruct((2, 4 * q + SPARE, ffq), bf16),
        jax.ShapeDtypeStruct((2, ffq + q, width), bf16),
    ]
    return pl.pallas_call(
        functools.partial(middle_kernel, block),
        out_shape=(
            jax.ShapeDtypeStruct((block, width), bf16),
            jax.ShapeDtypeStruct((block, width), f32),
        )
        + tuple(jax.ShapeDtypeStruct((GW, block), bf16) for _ in range(NG))
        + tuple(grads)
        + tuple(grads),
        in_specs=[SMEM] + vmem(NG + 4) + anyspec(13),
        out_specs=vmem(2 + NG) + anyspec(4),
        scratch_shapes=[
            pltpu.VMEM((width, block), bf16),
            pltpu.VMEM((width, width), bf16),
            pltpu.VMEM((4, width, ffq), bf16),
            pltpu.VMEM((4 * ffq, width), bf16),
            pltpu.VMEM((width, block), bf16),
            pltpu.VMEM((4, ffq, block), bf16),
            pltpu.VMEM((4, block, ffq), f32),
            pltpu.VMEM((width, block), bf16),
            pltpu.VMEM((8, width), f32),
            pltpu.VMEM((4, ffq), f32),
            pltpu.VMEM((16, width), f32),
            pltpu.VMEM((block, width), f32),
        ]
        + [pltpu.VMEM(g.shape, g.dtype) for g in grads + grads]
        + [
            pltpu.SemaphoreType.DMA((36,)),
        ],
        cost_estimate=CHEAP,
        compiler_params=params(60),
        name="middle",
    )(scal, *os, x, dy, small, small_oth, *outs, *inners, *outers)


def turn_kernel(scal, x0, x1, x2, x3, xt):
    core = scal[1]
    block, width = x0.shape
    half, quarter = width // 2, width // 4
    for j, x in enumerate((x0, x1, x2, x3)):
        cols = slice(j * block, (j + 1) * block)
        turned = x[...].T
        for y in range(2):
            for c in range(2):
                piece = turned[(2 * y + c) * quarter : (2 * y + c + 1) * quarter]

                @pl.when(core == c)
                def _(piece=piece, y=y):
                    xt[y * quarter : (y + 1) * quarter, cols] = piece

                @pl.when(core != c)
                def _(piece=piece, y=y):
                    xt[half + y * quarter : half + (y + 1) * quarter, cols] = piece


def turn(scal, xs):
    block, width = xs[0].shape
    return pl.pallas_call(
        turn_kernel,
        out_shape=jax.ShapeDtypeStruct((width, NG * block), bf16),
        in_specs=[SMEM] + vmem(NG),
        out_specs=vmem(1)[0],
        compiler_params=params(),
        name="turn",
    )(scal, *xs)


def qkv_grad_kernel(scal, xt, dq_ref, dkv_ref, keep, send, d_scr):
    g_id, core = scal[0], scal[2]
    d_scr[:GW, :] = dq_ref[...]
    d_scr[GW:, :] = dkv_ref[...]
    d = d_scr[...]
    quarter = xt.shape[0] // 4
    part = quarter // 2
    step = part + EXTRA
    grad = dot(xt[...], d, 1, 1).astype(bf16)
    ones = jnp.where(lax.broadcasted_iota(jnp.int32, (EXTRA, d.shape[1]), 0) == 0, 1.0, 0.0)
    sums = dot(ones.astype(bf16), d, 1, 1).astype(bf16)
    none = jnp.zeros_like(sums)
    for k, out in enumerate((keep, send)):
        for y in range(2):
            at = (2 * k + y) * quarter
            for x in range(2):
                out[y, x * step : x * step + part] = grad[at + x * part : at + (x + 1) * part]
                out[y, x * step + part : (x + 1) * step] = none
    for y in range(2):
        mine = jnp.right_shift(g_id, 1) == y

        @pl.when(mine & (core == 0))
        def _(y=y):
            keep[y, part:step] = sums

        @pl.when(mine & (core != 0))
        def _(y=y):
            send[y, part:step] = sums


def qkv_grad(scal, xt, dq, dkv):
    width, rows = xt.shape
    q = width // 4 + 2 * EXTRA
    return pl.pallas_call(
        qkv_grad_kernel,
        out_shape=(
            jax.ShapeDtypeStruct((2, q, 3 * GW), bf16),
            jax.ShapeDtypeStruct((2, q, 3 * GW), bf16),
        ),
        in_specs=[SMEM] + vmem(3),
        out_specs=vmem(2),
        scratch_shapes=[pltpu.VMEM((3 * GW, rows), bf16)],
        compiler_params=params(),
        name="qkv_grad",
    )(scal, xt, dq, dkv)


def each_part(scal, fn):
    xi, core = scal[1], scal[2]
    for c in range(2):
        for x in range(2):
            fn(c, x, jnp.bitwise_xor(core, c) * 2 + jnp.bitwise_xor(xi, x))


def unpack_kernel(place, scal, *refs):
    parts, outs, bias_ref = refs[0], refs[1:4], refs[4]
    rows = parts.shape[2] - EXTRA
    fi = place[1]

    def put(c, x, s):
        at = (2 * c + x) * rows
        for g in range(NG):
            v = parts[s, g, :rows].astype(f32)
            for part in range(3):
                outs[part][at : at + rows, g * GW : (g + 1) * GW] = v[
                    :, part * GW : (part + 1) * GW
                ]
        if (c, x) == (0, 0):
            for k in range(2):
                row = parts[s, 2 * fi + k, rows:].astype(f32)
                bias_ref[0:1, k * GW : (k + 1) * GW] = row[:1, :GW]
                bias_ref[1:2, k * GW : (k + 1) * GW] = row[:1, 2 * GW :]

    each_part(scal, put)


def spread_rows(segments, first, v):
    base = 0
    for n, place in segments:
        lo, hi = max(first, base), min(first + v.shape[0], base + n)
        if lo < hi:
            place(lo - base, v[lo - first : hi - first])
        base += n


def finish_kernel(scal, *refs):
    parts_a, whole_b = refs[:2]
    outer_ref, inner_ref, out_ref, vec_ref = refs[2:]
    ffq = inner_ref.shape[1] // 4
    quarter = inner_ref.shape[0] // 2
    g_id = scal[0]
    n_a, n_b = parts_a.shape[2], whole_b.shape[1]

    def put_a(c, x, s):
        def outer(row, v):
            outer_ref[c * ffq + row : c * ffq + row + v.shape[0], :] = v

        def out(row, v):
            out_ref[c * quarter + row : c * quarter + row + v.shape[0], :] = v

        for g in range(NG):
            j = jnp.bitwise_xor(g_id, g)
            v = parts_a[s, jnp.bitwise_and(j, 1) * 2 + jnp.right_shift(j, 1)].astype(f32)
            spread_rows(((ffq, outer), (quarter, out)), (NG * x + g) * n_a, v)

    each_part(scal, put_a)
    for i in range(whole_b.shape[0]):
        g, x, c = i >> 2, i >> 1 & 1, i & 1
        def inner(a, row, v, c=c):
            at = c * quarter + row
            inner_ref[at : at + v.shape[0], a * ffq : (a + 1) * ffq] = v

        def sums(row, v, c=c):
            if c == 0 and row < 8:
                vec_ref[row : min(8, row + v.shape[0]), :] = v[: 8 - row]

        spread_rows(
            tuple((quarter, functools.partial(inner, a)) for a in range(4)) + ((SPARE, sums),),
            (NG * x + g) * n_b,
            whole_b[i].astype(f32),
        )


def ending_kernel(place, spot, *refs):
    parts, whole_b, parts_q = refs[:4], refs[4], refs[5:9]
    dr_ref, d_refs, w_parts = refs[9], refs[10 : 10 + 2 * NG], refs[10 + 2 * NG : 13 + 2 * NG]
    outs = refs[13 + 2 * NG : 21 + 2 * NG]
    dx_ref = refs[21 + 2 * NG]
    staged_refs = refs[22 + 2 * NG : 30 + 2 * NG]
    w_scr, d_scr, a_scr, q_scr, sems = refs[30 + 2 * NG :]
    g_id, fi, core = place[0], place[1], place[2]
    width = w_scr.shape[0]
    q = width // 4
    oth = (1 - fi) * 2 * q
    rows = (
        pl.ds(pl.multiple_of(fi * 2 * q, 64), 2 * q),
        pl.ds(pl.multiple_of(oth + core * q, 64), q),
        pl.ds(pl.multiple_of(oth + (1 - core) * q, 64), q),
    )
    loads = [
        pltpu.make_async_copy(p, w_scr.at[r, :], sems.at[i])
        for i, (p, r) in enumerate(zip(w_parts, rows))
    ]
    pieces = [
        pltpu.make_async_copy(src, scr.at[s], sems.at[11 + 4 * k + s])
        for k, (group, scr) in enumerate(((parts, a_scr), (parts_q, q_scr)))
        for s, src in enumerate(group)
    ]
    for c in pieces + loads:
        c.start()
    stores = [
        pltpu.make_async_copy(src, dst, sems.at[3 + i])
        for i, (src, dst) in enumerate(zip(staged_refs, outs))
    ]
    for c in pieces[:4]:
        c.wait()
    finish_kernel(spot, a_scr, whole_b, *staged_refs[:4])
    for c in stores[:4]:
        c.start()
    for c in pieces[4:]:
        c.wait()
    unpack_kernel(place, spot, q_scr, *staged_refs[4:])
    for c in stores[4:]:
        c.start()
    for j in range(NG):
        base = jnp.bitwise_xor(g_id, j) * GW
        for part in range(3):
            at = pl.multiple_of(part * width + base, HD)
            src = d_refs[j][...] if part == 0 else d_refs[NG + j][(part - 1) * GW : part * GW, :]
            d_scr[pl.ds(at, GW), :] = src
    for c in loads:
        c.wait()
    dx_ref[...] = dr_ref[...] + dot(w_scr[...], d_scr[...]).T
    for c in stores:
        c.wait()


def ending(place, spot, parts_a, whole_b, parts_q, dr, d_parts, w_parts, shapes):
    block, width = dr.shape
    wide = [
        *shapes,
        (8, width),
        *((width // 2, width) for _ in range(3)),
        (2, 2 * GW),
    ]
    return pl.pallas_call(
        ending_kernel,
        out_shape=tuple(jax.ShapeDtypeStruct(s, f32) for s in wide)
        + (jax.ShapeDtypeStruct((block, width), f32),),
        in_specs=[SMEM, SMEM] + anyspec(4) + vmem(1) + anyspec(4) + vmem(1 + 2 * NG) + anyspec(3),
        out_specs=anyspec(8) + vmem(1),
        scratch_shapes=[pltpu.VMEM(s, f32) for s in wide]
        + [
            pltpu.VMEM((width, 3 * width), bf16),
            pltpu.VMEM((3 * width, block), bf16),
            pltpu.VMEM((4,) + parts_a[0].shape, bf16),
            pltpu.VMEM((4,) + parts_q[0].shape, bf16),
            pltpu.SemaphoreType.DMA((19,)),
        ],
        cost_estimate=CHEAP,
        compiler_params=params(60),
        name="ending",
    )(place, spot, *parts_a, whole_b, *parts_q, dr, *d_parts, *w_parts)


def fast_device(
    tokens,
    query_weight,
    query_bias,
    key_weight,
    value_weight,
    value_bias,
    out_weight,
    out_bias,
    first_gain,
    first_shift,
    inner_weight,
    inner_bias,
    outer_weight,
    outer_bias,
    second_gain,
    second_shift,
    doc_lengths,
    grad_output,
):
    block = tokens.shape[1]
    width = tokens.shape[2]
    ctx = lax.axis_size("ctx")
    members = ctx // NG
    ci = lax.axis_index("ctx")
    fi = lax.axis_index("fsdp")
    g_id = ci // members
    m_id = ci % members
    core = ci % 2
    xi = m_id // 2
    half = width // 2
    tie = lax.optimization_barrier

    def zswap(v, j):
        return swap(v, "ctx", j * members)

    def xswap(v):
        return swap(v, "ctx", 2)

    def cswap(v):
        return swap(v, "ctx", 1)

    def yswap(v):
        return swap(v, "fsdp", 1)

    local = tokens[0]
    x2 = zswap(local, 2)
    x1 = zswap(local, 1)
    w_own = jnp.concatenate(
        [
            lax.dynamic_slice_in_dim(w, g_id * GW, GW, 1)
            for w in (query_weight, key_weight, value_weight)
        ],
        axis=1,
    )
    small = pack(
        [
            out_bias,
            first_gain,
            first_shift,
            outer_bias,
            second_gain,
            second_shift,
            query_bias,
            value_bias,
            inner_bias,
        ]
    )

    def half_of(w):
        rows = w.shape[0] // 2
        return lax.dynamic_slice_in_dim(w, core * rows, rows, 0)

    w_mine = yswap(half_of(w_own))
    out_mine = yswap(half_of(out_weight))
    w_sib = cswap(w_mine)
    out_mine, small, w_mine, w_sib, x2, x1, inner_raw, outer_raw, doc_lengths = tie(
        (out_mine, small, w_mine, w_sib, x2, x1, inner_weight, outer_weight, doc_lengths)
    )
    x3 = zswap(x2, 1)
    small_oth = yswap(small)
    inner_half, outer_half = half_of(inner_raw), half_of(outer_raw)
    cut = inner_half.shape[0] // 4
    inner_one = yswap(inner_half[:cut])

    doc_ends = jnp.cumsum(doc_lengths[0])
    first = jnp.stack([(jnp.bitwise_xor(g_id, j) * members + m_id) * block for j in range(NG)])
    places = (first[:, None] + jnp.arange(block, dtype=jnp.int32)[None, :]).reshape(-1)
    before = places[:, None] >= doc_ends[None, :]
    starts = jnp.max(jnp.where(before, doc_ends[None, :], 0), axis=1).astype(jnp.int32)
    ends = jnp.min(jnp.where(before, ctx * block, doc_ends[None, :]), axis=1).astype(jnp.int32)
    low = starts.reshape(NG, block)[:, 0] // block
    high = (ends.reshape(NG, block)[:, -1] + block - 1) // block
    plain_low = (starts.reshape(NG, block)[:, -1] + block - 1) // block
    plain_high = ends.reshape(NG, block)[:, 0] // block
    whole = plain_low < plain_high
    plain_low = jnp.where(whole, plain_low, high)
    plain_high = jnp.where(whole, plain_high, high)
    scal = jnp.concatenate(
        [jnp.stack([m_id, g_id]), low, high, plain_low, plain_high]
    ).astype(jnp.int32)
    starts = starts[None]
    ends = ends[None]
    place = jnp.stack([g_id, fi, core]).astype(jnp.int32)
    spot = jnp.stack([g_id, xi, core]).astype(jnp.int32)
    dev = jnp.stack([fi, core]).astype(jnp.int32)
    tied = (small_oth, place, spot, dev, x3, inner_one, inner_half, outer_half, scal, starts, ends)
    small_oth, place, spot, dev, x3, inner_one, inner_half, outer_half, scal, starts, ends = tie(tied)

    xs = [local, x1, x2, x3]
    q_t, kv = project(block, place, xs, w_own, w_mine, w_sib, small, small_oth)

    kv_x = xswap(kv)
    inner_two = yswap(inner_half[cut:])
    cut = outer_half.shape[0] // 4
    outer_one = yswap(outer_half[:cut])
    sibs = [cswap(out_mine), cswap(inner_one)]
    tied = tie((kv_x, inner_two, outer_one) + tuple(sibs))
    (kv_x, inner_two, outer_one), sibs = tied[:3], list(tied[3:])
    kv_c = cswap(kv)
    kv_xc = cswap(kv_x)
    kv, kv_c, kv_x, kv_xc, inner_two, outer_one, outer_half = tie(
        (kv, kv_c, kv_x, kv_xc, inner_two, outer_one, outer_half)
    )
    kvs = [kv, kv_c, kv_x, kv_xc]
    outer_two = yswap(outer_half[cut:])
    sibs += [cswap(inner_two), cswap(outer_one)]
    res = group_fwd(members, block, scal, starts, ends, q_t, kvs)
    qkv_shard = jnp.concatenate([query_weight, key_weight, value_weight], axis=1)
    qkv_half = half_of(qkv_shard)
    tied = tie(tuple(res) + (outer_two, qkv_shard, qkv_half) + tuple(sibs))
    res, (outer_two, qkv_shard, qkv_half), sibs = tied[: 2 + NG], tied[2 + NG : 5 + NG], list(tied[5 + NG :])
    o_t, lse = res[:2]
    o_cols = list(res[2:])
    o_parts = [o_cols[0]] + [zswap(o_cols[j], j) for j in range(1, NG)]
    sibs.append(cswap(outer_two))
    tied = tie(tuple(o_parts) + (sibs[-1], qkv_half))
    o_parts, sibs[-1], qkv_half = list(tied[:NG]), tied[NG], tied[NG + 1]
    outs = (out_weight, out_mine, sibs[0])
    inners = (inner_weight, inner_one, inner_two, sibs[1], sibs[2])
    outers = (outer_weight, outer_one, outer_two, sibs[3], sibs[4])
    qkv_mine = yswap(qkv_half)

    mid = middle(block, place, o_parts, local, grad_output[0], small, small_oth, outs, inners, outers)
    tied = tie(tuple(mid) + (qkv_mine,))
    mid, qkv_mine = tied[:-1], tied[-1]
    output, d_first = mid[:2]
    dos = list(mid[2 : 2 + NG])
    keep_a, keep_b, send_a, send_b = mid[2 + NG :]

    state = [output]

    def then(v):
        v, _ = tie((v, state[0]))
        state[0] = v
        return v

    def rows_at(v, index, parts, axis=0):
        n = v.shape[axis] // parts
        return lax.dynamic_slice_in_dim(v, index * n, n, axis)

    def low_sum(terms, cut):
        return then(sum(cut(t).astype(f32) for t in terms).astype(bf16))

    z1 = g_id % 2
    z2 = g_id // 2

    keep_a, keep_b, send_a, send_b = keep_b, keep_a, send_b, send_a
    core_a = cswap(send_a)
    core_b = cswap(send_b)
    dos = [dos[0]] + [zswap(dos[j], j) for j in range(1, NG)]
    terms_b = [keep_b, core_b]
    terms_a = [keep_a, core_a]
    send_a = low_sum(terms_a, lambda v: pick(v, 1 - fi))
    send_b = low_sum(terms_b, lambda v: rows_at(v, 1 - xi, 2, 1))
    tied = tie(tuple(dos) + (send_a, send_b))
    dos, (send_a, send_b) = list(tied[:NG]), tied[NG:]
    got_a = yswap(send_a)
    got_b = xswap(send_b)
    res = group_bwd(members, block, scal, starts, ends, q_t, o_t, lse, dos, kvs)
    tied = tie(tuple(res) + (got_a, got_b))
    res, (got_a, got_b) = tied[:-2], tied[-2:]
    state[0] = got_b
    terms_a = [pick(t, fi) for t in terms_a] + [got_a]
    terms_b = [rows_at(t, xi, 2, 1) for t in terms_b] + [got_b]

    send_a = low_sum(terms_a, lambda v: rows_at(v, 1 - xi, 2))
    send_b = low_sum(terms_b, lambda v: pick(v, 1 - fi))
    got_a, got_b = xswap(send_a), yswap(send_b)
    dq, slots = res[0], res[1:]
    k1, k3 = cswap(slots[1]), cswap(slots[3])
    qkv_sib = cswap(qkv_mine)
    got_a, got_b, k1, k3, qkv_sib = tie((got_a, got_b, k1, k3, qkv_sib))
    terms_a = [rows_at(t, xi, 2) for t in terms_a] + [got_a]
    terms_b = [pick(t, fi) for t in terms_b] + [got_b]
    sum_a = sum(t.astype(f32) for t in terms_a).astype(bf16).reshape(NG, -1, width)
    sum_b = sum(t.astype(f32) for t in terms_b).astype(bf16).reshape(NG, -1, width)
    n_a, n_b = sum_a.shape[1], sum_b.shape[1]
    chunk = then(jnp.concatenate([sum_a, sum_b], axis=1).reshape(-1, width))
    columns = [[m + members * g for g in range(NG)] for m in range(members)]
    piece = lax.psum_scatter(
        chunk, "ctx", scatter_dimension=0, tiled=True, axis_index_groups=columns
    )
    got_kv = xswap(low_sum([slots[2], k3], lambda v: v))
    xt = turn(dev, tie(tuple(xs) + (state[0],))[:NG])
    dq_parts = [dq[:, j * block : (j + 1) * block] for j in range(NG)]
    dq_parts = tie(tuple(dq_parts) + (state[0],))[:NG]
    dq_parts = [dq_parts[0]] + [zswap(dq_parts[j], j) for j in range(1, NG)]
    tied = tie((got_kv, xt) + tuple(dq_parts))
    got_kv, xt, dq_parts = tied[0], tied[1], list(tied[2:])
    dkv = low_sum([slots[0], k1, got_kv], lambda v: v)
    dkv_parts = [dkv[:, j * block : (j + 1) * block] for j in range(NG)]
    keep_q, send_q = qkv_grad(place, xt, dq, dkv)
    terms_q = [keep_q, cswap(send_q)]
    got_q = yswap(low_sum(terms_q, lambda v: pick(v, 1 - fi)))
    terms_q = [pick(t, fi) for t in terms_q] + [got_q]

    piece = tie((piece, state[0]))[0]
    piece_a = piece[:n_a]
    whole_b = lax.all_gather(piece[n_a:], "ctx", axis=0)
    far_a = zswap(piece_a, 2)
    got_q = xswap(low_sum(terms_q, lambda v: rows_at(v, 1 - xi, 2)))
    far_a = tie((far_a, state[0]))[0]
    pair_a = then(jnp.stack([piece_a, far_a]))
    near_a = zswap(pair_a, 1)
    got_q = tie((got_q, state[0]))[0]
    terms_q = [rows_at(t, xi, 2) for t in terms_q] + [got_q]
    piece_q = low_sum(terms_q, lambda v: v)
    far_q = zswap(piece_q, 2)
    near_a = tie((near_a, state[0]))[0]
    col_a = then(jnp.stack([pair_a, near_a]))
    side_a = xswap(col_a)
    far_q = tie((far_q, state[0]))[0]
    piece_q = then(ordered(z2, piece_q, far_q))
    near_q = zswap(piece_q, 1)
    piece_q = then(ordered(z1, piece_q, near_q).transpose(1, 0, 2, 3).reshape(NG, -1, 3 * GW))
    side_q = xswap(piece_q)
    dkv_parts = tie(tuple(dkv_parts) + (state[0],))[:NG]
    dkv_parts = [dkv_parts[0]] + [zswap(dkv_parts[j], j) for j in range(1, NG)]
    tied = tie((side_a, side_q) + tuple(dkv_parts))
    side_a, side_q, dkv_parts = tied[0], tied[1], tied[2:]
    parts_q = [piece_q, side_q, cswap(piece_q), cswap(side_q)]
    core_a, core_side = cswap(col_a), cswap(side_a)
    tied = tie(tuple(parts_q) + (core_a, core_side))
    parts_q, core_a, core_side = tied[:4], tied[4], tied[5]
    parts_a = [v.reshape(NG, n_a, width) for v in (col_a, side_a, core_a, core_side)]
    tied = tie(tuple(parts_q) + tuple(parts_a) + (whole_b,) + tuple(dq_parts) + tuple(dkv_parts))
    parts_q, parts_a, whole_b, d_parts = tied[:4], tied[4:8], tied[8], tied[9:]
    (
        grad_outer,
        grad_inner,
        grad_out,
        vecs,
        grad_query,
        grad_key,
        grad_value,
        bias_rows,
        grad_input,
    ) = ending(
        place,
        spot,
        parts_a,
        whole_b,
        parts_q,
        d_first,
        d_parts,
        (qkv_shard, qkv_mine, qkv_sib),
        (outer_weight.shape, inner_weight.shape, out_weight.shape),
    )

    mine = lax.dynamic_slice_in_dim(vecs, fi * half, half, 1)
    return (
        output[None],
        grad_input[None],
        grad_query,
        bias_rows[0],
        grad_key,
        grad_value,
        bias_rows[1],
        grad_out,
        mine[0],
        mine[1],
        mine[2],
        grad_inner,
        vecs[6:8].reshape(-1),
        grad_outer,
        mine[3],
        mine[4],
        mine[5],
    )


def solution(mesh):
    placed = (
        P("fsdp", "ctx", None),
        P("fsdp", None),
        P("fsdp"),
        P("fsdp", None),
        P("fsdp", None),
        P("fsdp"),
        P("fsdp", None),
        P("fsdp"),
        P("fsdp"),
        P("fsdp"),
        P("fsdp", None),
        P("fsdp"),
        P("fsdp", None),
        P("fsdp"),
        P("fsdp"),
        P("fsdp"),
        P("fsdp", None),
        P("fsdp", "ctx", None),
    )
    quick = mesh.shape["fsdp"] == 2 and mesh.shape["ctx"] == 4 * NG
    return jax.shard_map(
        fast_device if quick else on_device,
        mesh=mesh,
        in_specs=placed,
        out_specs=(
            P("fsdp", "ctx", None),
            P("fsdp", "ctx", None),
            P("fsdp", None),
            P("fsdp"),
            P("fsdp", None),
            P("fsdp", None),
            P("fsdp"),
            P("fsdp", None),
            P("fsdp"),
            P("fsdp"),
            P("fsdp"),
            P("fsdp", None),
            P("fsdp"),
            P("fsdp", None),
            P("fsdp"),
            P("fsdp"),
            P("fsdp"),
        ),
        check_vma=False,
    )
```

```python
import functools
import math

import jax
import jax.numpy as jnp
from jax import lax
from jax.experimental import pallas as pl
from jax.experimental.pallas import tpu as pltpu
from jax.sharding import PartitionSpec as P

H = 12
HD = 64
NG = 4
HG = H // NG
GW = HG * HD

eps = 1e-12
NEG = -1e30
LOG2E = 1.4426950408889634
SCALE = 1.0 / math.sqrt(HD)
bf16 = jnp.bfloat16
f32 = jnp.float32


def layer_norm(r, gain, shift):
    mean = jnp.mean(r, axis=-1, keepdims=True)
    centered = r - mean
    var = jnp.mean(centered * centered, axis=-1, keepdims=True)
    return centered * lax.rsqrt(var + eps) * gain + shift


def gelu_exact(v):
    return jax.nn.gelu(v, approximate=False)


def dot(left, right, ldim=1, rdim=0):
    return lax.dot_general(
        left, right, (((ldim,), (rdim,)), ((), ())), preferred_element_type=f32
    )


def swap(v, axis, bit):
    n = lax.axis_size(axis)
    return lax.ppermute(v, axis, [(i, i ^ bit) for i in range(n)])


def pick(v, index, axis=0):
    return lax.dynamic_index_in_dim(v, index, axis, keepdims=False)


def ordered(bit, own, other):
    return jnp.where(bit == 0, jnp.stack([own, other]), jnp.stack([other, own]))


def slot_of(t, m, g, members):
    shift = members.bit_length() - 1
    return jnp.bitwise_xor(jnp.bitwise_and(t, members - 1), m) * NG + jnp.bitwise_xor(
        jnp.right_shift(t, shift), g
    )


def fwd_kernel(members, block, scal, st_ref, en_ref, q_ref, *rest):
    kv_refs = rest[:members]
    o_ref, ob_ref, lse_ref, k_scr, v_scr = rest[members:]
    m_id, g_id = scal[0], scal[1]
    cols = NG * block
    for s in range(members):
        for h in range(HG):
            k_scr[h, s * cols : (s + 1) * cols, :] = kv_refs[s][h * HD : (h + 1) * HD, :].T
        v_scr[:, s * cols : (s + 1) * cols] = kv_refs[s][GW:, :]
    for j in range(NG):
        qs = slice(j * block, (j + 1) * block)
        start = st_ref[:, qs]
        end = en_ref[:, qs]
        qts = [q_ref[h * HD : (h + 1) * HD, qs] for h in range(HG)]

        def step(t, carry, start=start, end=end, qts=qts):
            off = pl.multiple_of(slot_of(t, m_id, g_id, members) * block, block)
            kpos = t * block + lax.broadcasted_iota(jnp.int32, (block, block), 0)
            allowed = (kpos >= start) & (kpos < end)
            out = []
            for h in range(HG):
                top, total, acc = carry[h]
                s = dot(k_scr[h, pl.ds(off, block), :], qts[h]) * (SCALE * LOG2E)
                s = jnp.where(allowed, s, NEG)
                new = jnp.maximum(top, jnp.max(s, axis=0, keepdims=True))
                alpha = jnp.exp2(top - new)
                p = jnp.exp2(s - new)
                total = total * alpha + jnp.sum(p, axis=0, keepdims=True)
                acc = acc * alpha + dot(
                    v_scr[h * HD : (h + 1) * HD, pl.ds(off, block)], p.astype(bf16)
                )
                out.append((new, total, acc))
            return tuple(out)

        init = tuple(
            (
                jnp.full((1, block), NEG, f32),
                jnp.zeros((1, block), f32),
                jnp.zeros((HD, block), f32),
            )
            for _ in range(HG)
        )
        done = lax.fori_loop(scal[2 + j], scal[2 + NG + j], step, init)
        for h in range(HG):
            top, total, acc = done[h]
            o = acc / total
            o_ref[h * HD : (h + 1) * HD, qs] = o
            ob_ref[h * HD : (h + 1) * HD, qs] = o.astype(bf16)
            lse_ref[h : h + 1, qs] = top + jnp.log2(total)


def bwd_kernel(members, block, scal, st_ref, en_ref, q_ref, o_ref, lse_ref, do_ref, *rest):
    kv_refs = rest[:members]
    dq_ref, dkv_ref, k_scr, v_scr, kt_scr, dk_scr, dv_scr = rest[members:]
    m_id, g_id = scal[0], scal[1]
    cols = NG * block
    for s in range(members):
        part = slice(s * cols, (s + 1) * cols)
        for h in range(HG):
            k_scr[h, part, :] = kv_refs[s][h * HD : (h + 1) * HD, :].T
            v_scr[h, part, :] = kv_refs[s][GW + h * HD : GW + (h + 1) * HD, :].T
        kt_scr[:, part] = kv_refs[s][:GW, :]
    dk_scr[...] = jnp.zeros_like(dk_scr)
    dv_scr[...] = jnp.zeros_like(dv_scr)
    for j in range(NG):
        qs = slice(j * block, (j + 1) * block)
        start = st_ref[:, qs]
        end = en_ref[:, qs]
        per_head = []
        for h in range(HG):
            hr = slice(h * HD, (h + 1) * HD)
            qt = q_ref[hr, qs]
            dot_t = do_ref[hr, qs]
            delta = jnp.sum(dot_t.astype(f32) * o_ref[hr, qs], axis=0, keepdims=True)
            per_head.append((qt, qt.T, dot_t, dot_t.T, delta, lse_ref[h : h + 1, qs]))

        def step(t, carry, start=start, end=end, per_head=per_head):
            off = pl.multiple_of(slot_of(t, m_id, g_id, members) * block, block)
            kpos = t * block + lax.broadcasted_iota(jnp.int32, (block, block), 0)
            allowed = (kpos >= start) & (kpos < end)
            out = []
            for h in range(HG):
                qt, q, dot_t, do, delta, lse = per_head[h]
                s = dot(k_scr[h, pl.ds(off, block), :], qt) * (SCALE * LOG2E)
                p = jnp.where(allowed, jnp.exp2(s - lse), 0.0)
                dp = dot(v_scr[h, pl.ds(off, block), :], dot_t)
                ds = (p * (dp - delta)).astype(bf16)
                dv_scr[h, pl.ds(off, block), :] += dot(p.astype(bf16), do)
                dk_scr[h, pl.ds(off, block), :] += dot(ds, q)
                out.append(
                    carry[h] + dot(kt_scr[h * HD : (h + 1) * HD, pl.ds(off, block)], ds)
                )
            return tuple(out)

        init = tuple(jnp.zeros((HD, block), f32) for _ in range(HG))
        done = lax.fori_loop(scal[2 + j], scal[2 + NG + j], step, init)
        for h in range(HG):
            dq_ref[h * HD : (h + 1) * HD, qs] = (done[h] * SCALE).astype(bf16)
    for s in range(members):
        part = slice(s * cols, (s + 1) * cols)
        for h in range(HG):
            dkv_ref[s, h * HD : (h + 1) * HD, :] = (dk_scr[h, part, :] * SCALE).T.astype(bf16)
            dkv_ref[s, GW + h * HD : GW + (h + 1) * HD, :] = dv_scr[h, part, :].T.astype(bf16)


def whole_specs(n):
    return [pl.BlockSpec(memory_space=pltpu.SMEM)] + [
        pl.BlockSpec(memory_space=pltpu.VMEM) for _ in range(n)
    ]


def attend(members, block, scal, starts, ends, q, kvs):
    keys = members * NG * block
    rows = NG * block
    return pl.pallas_call(
        functools.partial(fwd_kernel, members, block),
        out_shape=(
            jax.ShapeDtypeStruct((GW, rows), f32),
            jax.ShapeDtypeStruct((GW, rows), bf16),
            jax.ShapeDtypeStruct((HG, rows), f32),
        ),
        in_specs=whole_specs(3 + members),
        out_specs=[pl.BlockSpec(memory_space=pltpu.VMEM) for _ in range(3)],
        scratch_shapes=[
            pltpu.VMEM((HG, keys, HD), bf16),
            pltpu.VMEM((GW, keys), bf16),
        ],
        compiler_params=pltpu.CompilerParams(vmem_limit_bytes=50 << 20),
        name="attend",
    )(scal, starts, ends, q, *kvs)


def attend_back(members, block, scal, starts, ends, q, o, lse, do, kvs):
    keys = members * NG * block
    rows = NG * block
    return pl.pallas_call(
        functools.partial(bwd_kernel, members, block),
        out_shape=(
            jax.ShapeDtypeStruct((GW, rows), bf16),
            jax.ShapeDtypeStruct((members, 2 * GW, rows), bf16),
        ),
        in_specs=whole_specs(6 + members),
        out_specs=[pl.BlockSpec(memory_space=pltpu.VMEM) for _ in range(2)],
        scratch_shapes=[
            pltpu.VMEM((HG, keys, HD), bf16),
            pltpu.VMEM((HG, keys, HD), bf16),
            pltpu.VMEM((GW, keys), bf16),
            pltpu.VMEM((HG, keys, HD), f32),
            pltpu.VMEM((HG, keys, HD), f32),
        ],
        compiler_params=pltpu.CompilerParams(vmem_limit_bytes=56 << 20),
        name="attend_back",
    )(scal, starts, ends, q, o, lse, do, *kvs)


def on_device(
    tokens,
    query_weight,
    query_bias,
    key_weight,
    value_weight,
    value_bias,
    out_weight,
    out_bias,
    first_gain,
    first_shift,
    inner_weight,
    inner_bias,
    outer_weight,
    outer_bias,
    second_gain,
    second_shift,
    doc_lengths,
    grad_output,
):
    block = tokens.shape[1]
    width = tokens.shape[2]
    ctx = lax.axis_size("ctx")
    fs = lax.axis_size("fsdp")
    members = ctx // NG
    ci = lax.axis_index("ctx")
    fi = lax.axis_index("fsdp")
    g_id = ci // members
    m_id = ci % members
    core = ci % 2
    own_rows = width // fs
    m_bits = []
    b = members // 2
    while b >= 1:
        m_bits.append(b)
        b //= 2
    g_slots = range(NG)

    def bit_of(index, bit):
        return (index // bit) % 2

    def gather_rows(w):
        rows = w.shape[0]
        if fs != 2:
            return lax.all_gather(w, "fsdp", axis=0, tiled=True)
        half = rows // 2
        mine = swap(lax.dynamic_slice_in_dim(w, core * half, half, 0), "fsdp", 1)
        others = swap(mine, "ctx", 1)
        other = ordered(core, mine, others).reshape(w.shape)
        return ordered(fi, w, other).reshape((2 * rows,) + w.shape[1:])

    local = tokens[0]
    x_slots = {0: local}
    x_slots[2] = swap(local, "ctx", 2 * members)
    x_slots[1] = swap(local, "ctx", members)
    x_slots[3] = swap(x_slots[2], "ctx", members)
    x_all = jnp.concatenate([x_slots[j] for j in g_slots], axis=0)

    vectors = [
        query_bias,
        value_bias,
        out_bias,
        first_gain,
        first_shift,
        inner_bias,
        outer_bias,
        second_gain,
        second_shift,
    ]
    sizes = [v.shape[0] for v in vectors]
    packed = lax.all_gather(jnp.concatenate(vectors), "fsdp", axis=0, tiled=False)
    at = 0
    full = []
    for n in sizes:
        full.append(packed[:, at : at + n].reshape(-1).astype(f32))
        at += n
    qbias, vbias, obias, gain_one, shift_one, ibias, outbias, gain_two, shift_two = full

    group_cols = [
        lax.dynamic_slice_in_dim(w, g_id * GW, GW, 1)
        for w in (query_weight, key_weight, value_weight)
    ]
    w_group = lax.all_gather(
        jnp.concatenate(group_cols, axis=1), "fsdp", axis=0, tiled=True
    ) if fs != 2 else None
    if fs == 2:
        mine = jnp.concatenate(group_cols, axis=1)
        w_group = ordered(fi, mine, swap(mine, "fsdp", 1)).reshape(width, 3 * GW)
    out_full = gather_rows(out_weight)
    inner_full = gather_rows(inner_weight)
    outer_full = gather_rows(outer_weight)
    qkv_full = gather_rows(jnp.concatenate([query_weight, key_weight, value_weight], axis=1))

    bias_group = jnp.concatenate(
        [
            lax.dynamic_slice_in_dim(qbias, g_id * GW, GW, 0),
            jnp.zeros((GW,), f32),
            lax.dynamic_slice_in_dim(vbias, g_id * GW, GW, 0),
        ]
    )
    qkv = (dot(w_group, x_all, 0, 1) + bias_group[:, None]).astype(bf16)
    q_t = qkv[:GW]
    kv_slots = {0: qkv[GW:]}
    for b in m_bits:
        for s in sorted(kv_slots):
            kv_slots[s ^ b] = swap(kv_slots[s], "ctx", b)
    kvs = [kv_slots[s] for s in range(members)]

    doc_ends = jnp.cumsum(doc_lengths[0])
    first = jnp.stack([(jnp.bitwise_xor(g_id, j) * members + m_id) * block for j in g_slots])
    places = (first[:, None] + jnp.arange(block, dtype=jnp.int32)[None, :]).reshape(-1)
    before = places[:, None] >= doc_ends[None, :]
    starts = jnp.max(jnp.where(before, doc_ends[None, :], 0), axis=1).astype(jnp.int32)
    ends = jnp.min(jnp.where(before, ctx * block, doc_ends[None, :]), axis=1).astype(jnp.int32)
    low = starts.reshape(NG, block)[:, 0] // block
    high = (ends.reshape(NG, block)[:, -1] + block - 1) // block
    scal = jnp.concatenate([jnp.stack([m_id, g_id]), low, high]).astype(jnp.int32)
    starts = starts[None]
    ends = ends[None]

    o_t, ob_t, lse = attend(members, block, scal, starts, ends, q_t, kvs)

    def column(v, j):
        return v[:, j * block : (j + 1) * block]

    def exchange(parts):
        return [parts[0]] + [swap(parts[j], "ctx", j * members) for j in range(1, NG)]

    def by_group(slots):
        return [
            lax.select_n(g_id, *[slots[a ^ k] for k in g_slots]) for a in g_slots
        ]

    attn_t = jnp.concatenate(by_group(exchange([column(ob_t, j) for j in g_slots])), axis=0)
    branch = dot(attn_t, out_full, 0, 0) + obias
    local_float = local.astype(f32)
    hidden, first_back = jax.vjp(layer_norm, local_float + branch, gain_one, shift_one)
    hidden_low = hidden.astype(bf16)
    inner = dot(hidden_low, inner_full) + ibias
    active, gelu_back = jax.vjp(gelu_exact, inner)
    active_low = active.astype(bf16)
    outer = dot(active_low, outer_full) + outbias
    result, second_back = jax.vjp(layer_norm, hidden + outer, gain_two, shift_two)
    output = result.astype(bf16)[None]
    grad_y = grad_output[0].astype(f32)
    d_second, grad_gain_two, grad_shift_two = second_back(grad_y)
    d_outer_low = d_second.astype(bf16)
    grad_outbias = jnp.sum(d_outer_low.astype(f32), axis=0)
    (d_inner,) = gelu_back(dot(d_outer_low, outer_full, 1, 1))
    d_inner_low = d_inner.astype(bf16)
    grad_ibias = jnp.sum(d_inner_low.astype(f32), axis=0)
    d_hidden = d_second + dot(d_inner_low, inner_full, 1, 1)
    d_first, grad_gain_one, grad_shift_one = first_back(d_hidden)
    d_branch_low = d_first.astype(bf16)
    grad_obias = jnp.sum(d_branch_low.astype(f32), axis=0)
    do_t = dot(out_full, d_branch_low, 1, 1).astype(bf16).reshape(NG, GW, block)
    do_parts = [pick(do_t, jnp.bitwise_xor(g_id, j)) for j in g_slots]
    do_all = jnp.concatenate(exchange(do_parts), axis=1)

    def halve(acc, axis, bit, index):
        acc = acc.reshape((2, acc.shape[0] // 2) + acc.shape[1:])
        mine = bit_of(index, bit)
        got = swap(pick(acc, 1 - mine), axis, bit)
        return (pick(acc, mine).astype(f32) + got.astype(f32)).astype(bf16)

    def reduce_rows(product, left, bits):
        rows = left.shape[0] // (2 * fs)
        split = left.reshape(fs, 2, rows, left.shape[1])
        send = product(pick(split, 1 - core, 1).reshape(fs * rows, -1)).astype(bf16)
        keep = product(pick(split, core, 1).reshape(fs * rows, -1))
        acc = (keep + swap(send, "ctx", 1).astype(f32)).astype(bf16)
        n = fs
        while n > 1:
            n //= 2
            acc = halve(acc, "fsdp", n, fi)
        for b in bits:
            acc = halve(acc, "ctx", b, ci)
        return acc

    def join(acc, bit):
        both = ordered(bit_of(ci, bit), acc, swap(acc, "ctx", bit))
        return both.reshape((2 * acc.shape[0],) + acc.shape[1:])

    x_bits = [b for b in m_bits if b > 1]
    all_bits = x_bits + [members, 2 * members]

    def weight_grad(left_t, right, rdim=0):
        acc = reduce_rows(lambda part: dot(part, right, 1, rdim), left_t, all_bits)
        for b in all_bits[::-1]:
            acc = join(acc, b)
        return join(acc, 1).astype(f32)

    grad_outer = weight_grad(active_low.T, d_outer_low)
    grad_inner = weight_grad(hidden_low.T, d_inner_low)
    grad_out = weight_grad(attn_t, d_branch_low)

    dq_t, dkv = attend_back(members, block, scal, starts, ends, q_t, o_t, lse, do_all, kvs)
    dkv_slots = {s: dkv[s] for s in range(members)}
    for b in m_bits[::-1]:
        for s in sorted(dkv_slots):
            if s & b:
                got = swap(dkv_slots.pop(s), "ctx", b)
                dkv_slots[s ^ b] = (dkv_slots[s ^ b].astype(f32) + got.astype(f32)).astype(bf16)
    d_qkv = jnp.concatenate([dq_t, dkv_slots[0]], axis=0)
    back = by_group(exchange([column(d_qkv, j) for j in g_slots]))
    d_all = jnp.stack(back).reshape(NG, 3, GW, block).transpose(1, 0, 2, 3).reshape(3 * width, block)
    grad_input = d_first + dot(d_all, qkv_full, 0, 1)

    acc = reduce_rows(lambda part: dot(part, d_qkv, 1, 1), x_all.T, x_bits)
    acc = ordered(bit_of(ci, 2 * members), acc, swap(acc, "ctx", 2 * members))
    acc = ordered(bit_of(ci, members), acc, swap(acc, "ctx", members))
    lead = []
    for b in x_bits[::-1] + [1]:
        acc = ordered(bit_of(ci, b), acc, swap(acc, "ctx", b))
        lead.append(2)
    nb = len(lead)
    acc = acc.astype(f32)
    order = tuple(range(nb)) + (nb + 2, nb + 1, nb, nb + 3)
    acc = acc.transpose(order).reshape(own_rows, NG, 3, GW).transpose(2, 0, 1, 3)
    grad_query, grad_key, grad_value = acc.reshape(3, own_rows, width)

    group_sums = jnp.sum(d_qkv.astype(f32), axis=1)
    spread = (jnp.arange(NG) == g_id)[:, None]
    grad_qbias = jnp.where(spread, group_sums[None, :GW], 0.0).reshape(-1)
    grad_vbias = jnp.where(spread, group_sums[None, 2 * GW :], 0.0).reshape(-1)
    terms = [
        grad_qbias,
        grad_vbias,
        grad_obias,
        grad_gain_one,
        grad_shift_one,
        grad_ibias,
        grad_outbias,
        grad_gain_two,
        grad_shift_two,
    ]
    summed = lax.psum(jnp.concatenate([t.reshape(fs, -1) for t in terms], axis=1), ("fsdp", "ctx"))
    mine = pick(summed, fi)
    shares = []
    at = 0
    for n in sizes:
        shares.append(mine[at : at + n])
        at += n
    s_q, s_v, s_o, s_g1, s_s1, s_i, s_out, s_g2, s_s2 = shares
    return (
        output,
        grad_input[None],
        grad_query,
        s_q,
        grad_key,
        grad_value,
        s_v,
        grad_out,
        s_o,
        s_g1,
        s_s1,
        grad_inner,
        s_i,
        grad_outer,
        s_out,
        s_g2,
        s_s2,
    )


def vmem(n):
    return [pl.BlockSpec(memory_space=pltpu.VMEM) for _ in range(n)]


def anyspec(n):
    return [pl.BlockSpec(memory_space=pl.ANY) for _ in range(n)]


CHEAP = pl.CostEstimate(flops=1, transcendentals=0, bytes_accessed=1)
EXTRA = 8
SPARE = 64
OUT_A = 128
SMEM = pl.BlockSpec(memory_space=pltpu.SMEM)


def params(mib=56):
    return pltpu.CompilerParams(vmem_limit_bytes=mib << 20)


def project_kernel(
    block, scal, x0, x1, x2, x3, own, small, small_oth, mine, sib, q_ref, kv_ref, row_scr, bias_scr, w_scr, sems
):
    g_id, fi, core = scal[0], scal[1], scal[2]
    half = own.shape[0]
    quarter = half // 2
    copies = [
        pltpu.make_async_copy(
            part, w_scr.at[pl.ds(pl.multiple_of(c * quarter, 64), quarter), :], sems.at[k]
        )
        for k, (part, c) in enumerate(((mine, core), (sib, 1 - core)))
    ]
    for c in copies:
        c.start()
    w_own = own[...].T
    at_own = pl.multiple_of(fi * half, 128)
    at_oth = pl.multiple_of((1 - fi) * half, 128)
    row_scr[:, pl.ds(at_own, half)] = small[6:8, :].astype(f32)
    row_scr[:, pl.ds(at_oth, half)] = small_oth[6:8, :].astype(f32)
    bias_scr[...] = jnp.zeros_like(bias_scr)
    for g in range(NG):

        @pl.when(g_id == g)
        def _(g=g):
            bias_scr[0:1, :GW] = row_scr[0:1, g * GW : (g + 1) * GW]
            bias_scr[0:1, 2 * GW :] = row_scr[1:2, g * GW : (g + 1) * GW]

    bias = bias_scr[...].T[:, :1]
    for c in copies:
        c.wait()
    w_oth = w_scr[...].T
    for j, x in enumerate((x0, x1, x2, x3)):
        cols = slice(j * block, (j + 1) * block)
        res = dot(w_own, x[:, pl.ds(at_own, half)], 1, 1)
        res += dot(w_oth, x[:, pl.ds(at_oth, half)], 1, 1)
        res = (res + bias).astype(bf16)
        q_ref[:, cols] = res[:GW]
        kv_ref[:, cols] = res[GW:]


def project(block, scal, xs, own, mine, sib, small, small_oth):
    rows = NG * block
    return pl.pallas_call(
        functools.partial(project_kernel, block),
        out_shape=(
            jax.ShapeDtypeStruct((GW, rows), bf16),
            jax.ShapeDtypeStruct((2 * GW, rows), bf16),
        ),
        in_specs=[SMEM] + vmem(7) + anyspec(2),
        out_specs=vmem(2),
        scratch_shapes=[
            pltpu.VMEM((2, 2 * own.shape[0]), f32),
            pltpu.VMEM((8, 3 * GW), f32),
            pltpu.VMEM(own.shape, bf16),
            pltpu.SemaphoreType.DMA((2,)),
        ],
        cost_estimate=CHEAP,
        compiler_params=params(),
        name="project",
    )(scal, *xs, own, small, small_oth, mine, sib)


def pack_kernel(*refs):
    out = refs[-1]
    n = out.shape[1]
    at = 0
    for ref in refs[:-1]:
        for k in range(ref.shape[0] // n):
            out[at : at + 1, :] = ref[k * n : (k + 1) * n].reshape(1, n)
            at += 1


def pack(vectors):
    n = vectors[0].shape[0]
    rows = sum(v.shape[0] for v in vectors) // n
    return pl.pallas_call(
        pack_kernel,
        out_shape=jax.ShapeDtypeStruct((rows, n), bf16),
        in_specs=vmem(len(vectors)),
        out_specs=vmem(1)[0],
        compiler_params=params(),
        name="pack",
    )(*vectors)


def tile_offset(t, scal, members, block):
    return pl.multiple_of(slot_of(t, scal[0], scal[1], members) * block, block)


UNROLL = 4


def key_loop(scal, j, block, tiles, init):
    low, high, inner_low, inner_high = (scal[2 + NG * i + j] for i in range(4))
    many = (inner_high - inner_low) // UNROLL
    rest = inner_low + UNROLL * many
    before = inner_low - low
    edges = before + high - rest

    def several(i, c):
        return tiles([inner_low + UNROLL * i + u for u in range(UNROLL)], None, c)

    def pair(i, c):
        ts, firsts = [], []
        for u in range(2):
            e = 2 * i + u
            t = jnp.minimum(jnp.where(e < before, low + e, rest + e - before), high - 1)
            ts.append(t)
            firsts.append(jnp.where(e < edges, t * block, -(1 << 30)))
        return tiles(ts, firsts, c)

    carry = lax.fori_loop(0, many, several, init)
    return lax.fori_loop(0, (edges + 1) // 2, pair, carry)


def inside(first, start, end, block):
    kpos = first + lax.broadcasted_iota(jnp.int32, (block, block), 0)
    return (kpos >= start) & (kpos < end)


def staged(n, first, second, third):
    one, two = {}, {}
    for i in range(n + 2):
        if i < n:
            one[i] = first(i)
        if 0 <= i - 1 < n:
            two[i - 1] = second(i - 1, one.pop(i - 1))
        if 0 <= i - 2 < n:
            third(i - 2, two.pop(i - 2))


def group_fwd_kernel(members, block, scal, st_ref, en_ref, q_ref, *rest):
    kv_refs = rest[:members]
    o_ref, lse_ref = rest[members : members + 2]
    ob_refs = rest[members + 2 : members + 2 + NG]
    k_scr, v_scr = rest[members + 2 + NG :]
    cols = NG * block
    for s in range(members):
        for h in range(HG):
            k_scr[h, s * cols : (s + 1) * cols, :] = kv_refs[s][h * HD : (h + 1) * HD, :].T
        v_scr[:, s * cols : (s + 1) * cols] = kv_refs[s][GW:, :]

    @pl.loop(0, NG)
    def _(j):
        cut = pl.ds(pl.multiple_of(j * block, block), block)
        start = st_ref[:, cut]
        end = en_ref[:, cut]
        qts = [q_ref[h * HD : (h + 1) * HD, cut] for h in range(HG)]

        def tiles(ts, firsts, carry):
            offs = [tile_offset(t, scal, members, block) for t in ts]
            allowed = firsts and [inside(first, start, end, block) for first in firsts]
            out = [None] * HG

            def first(h):
                return [dot(k_scr[h, pl.ds(off, block), :], qts[h]) for off in offs]

            def second(h, scores):
                top, total, acc = carry[h]
                if allowed:
                    scores = [jnp.where(a, s, NEG) for a, s in zip(allowed, scores)]
                new = top
                for s in scores:
                    new = jnp.maximum(new, jnp.max(s, axis=0, keepdims=True))
                alpha = jnp.exp2((top - new) * (SCALE * LOG2E))
                total = total * alpha
                probs = []
                for s in scores:
                    p = jnp.exp2((s - new) * (SCALE * LOG2E))
                    total += jnp.sum(p, axis=0, keepdims=True)
                    probs.append(p.astype(bf16))
                return probs, new, total, acc * alpha

            def third(h, state):
                probs, new, total, acc = state
                for p, off in zip(probs, offs):
                    acc += dot(v_scr[h * HD : (h + 1) * HD, pl.ds(off, block)], p)
                out[h] = (new, total, acc)

            staged(HG, first, second, third)
            return tuple(out)

        init = tuple(
            (
                jnp.full((1, block), NEG, f32),
                jnp.zeros((1, block), f32),
                jnp.zeros((HD, block), f32),
            )
            for _ in range(HG)
        )
        done = key_loop(scal, j, block, tiles, init)
        for h in range(HG):
            top, total, acc = done[h]
            o = acc / total
            o_ref[h * HD : (h + 1) * HD, cut] = o
            lse_ref[h : h + 1, cut] = top * (SCALE * LOG2E) + jnp.log2(total)

    for k in range(NG):
        ob_refs[k][...] = o_ref[:, k * block : (k + 1) * block].astype(bf16)


def group_fwd(members, block, scal, starts, ends, q, kvs):
    keys = members * NG * block
    rows = NG * block
    return pl.pallas_call(
        functools.partial(group_fwd_kernel, members, block),
        out_shape=(
            jax.ShapeDtypeStruct((GW, rows), f32),
            jax.ShapeDtypeStruct((HG, rows), f32),
        )
        + tuple(jax.ShapeDtypeStruct((GW, block), bf16) for _ in range(NG)),
        in_specs=[SMEM] + vmem(3 + members),
        out_specs=vmem(2 + NG),
        scratch_shapes=[
            pltpu.VMEM((HG, keys, HD), bf16),
            pltpu.VMEM((GW, keys), bf16),
        ],
        cost_estimate=CHEAP,
        compiler_params=params(),
        name="group_fwd",
    )(scal, starts, ends, q, *kvs)


def group_bwd_kernel(members, block, scal, st_ref, en_ref, q_ref, o_ref, lse_ref, *rest):
    do_refs = rest[:NG]
    kv_refs = rest[NG : NG + members]
    dq_ref = rest[NG + members]
    dkv_refs = rest[NG + members + 1 : NG + 2 * members + 1]
    k_scr, v_scr, dk_scr, dv_scr, do_scr = rest[NG + 2 * members + 1 :]
    cols = NG * block
    heads = [slice(h * HD, (h + 1) * HD) for h in range(HG)]
    for s in range(members):
        part = slice(s * cols, (s + 1) * cols)
        k_scr[:, part] = kv_refs[s][:GW, :]
        v_scr[:, part] = kv_refs[s][GW:, :]
    dk_scr[...] = jnp.zeros_like(dk_scr)
    dv_scr[...] = jnp.zeros_like(dv_scr)
    for k in range(NG):
        do_scr[:, k * block : (k + 1) * block] = do_refs[k][...]

    @pl.loop(0, NG)
    def _(j):
        cut = pl.ds(pl.multiple_of(j * block, block), block)
        start = st_ref[:, cut]
        end = en_ref[:, cut]
        per_head = []
        for h in range(HG):
            do = do_scr[heads[h], cut]
            delta = jnp.sum(do.astype(f32) * o_ref[heads[h], cut], axis=0, keepdims=True)
            per_head.append((q_ref[heads[h], cut], do, delta, lse_ref[h : h + 1, cut]))

        def tiles(ts, firsts, carry):
            out = list(carry)
            work = []
            for u, t in enumerate(ts):
                keys = pl.ds(tile_offset(t, scal, members, block), block)
                allowed = None if firsts is None else inside(firsts[u], start, end, block)
                work += [(h, keys, allowed) for h in range(HG)]

            def first(i):
                h, keys, _ = work[i]
                q, do, _, _ = per_head[h]
                return dot(k_scr[heads[h], keys], q, 0, 0), dot(v_scr[heads[h], keys], do, 0, 0)

            def second(i, pair):
                h, _, allowed = work[i]
                _, _, delta, lse = per_head[h]
                s, dp = pair
                p = jnp.exp2(s * (SCALE * LOG2E) - lse)
                if allowed is not None:
                    p = jnp.where(allowed, p, 0.0)
                return p.astype(bf16), (p * (dp - delta)).astype(bf16)

            def third(i, pair):
                h, keys, _ = work[i]
                q, do, _, _ = per_head[h]
                p, ds = pair
                dv_scr[heads[h], keys] += dot(do, p, 1, 1)
                dk_scr[heads[h], keys] += dot(q, ds, 1, 1)
                out[h] = out[h] + dot(k_scr[heads[h], keys], ds)

            staged(len(work), first, second, third)
            return tuple(out)

        init = tuple(jnp.zeros((HD, block), f32) for _ in range(HG))
        done = key_loop(scal, j, block, tiles, init)
        for h in range(HG):
            dq_ref[heads[h], cut] = (done[h] * SCALE).astype(bf16)

    for s in range(members):
        part = slice(s * cols, (s + 1) * cols)
        dkv_refs[s][:GW, :] = (dk_scr[:, part] * SCALE).astype(bf16)
        dkv_refs[s][GW:, :] = dv_scr[:, part].astype(bf16)


def group_bwd(members, block, scal, starts, ends, q, o, lse, dos, kvs):
    keys = members * NG * block
    rows = NG * block
    return pl.pallas_call(
        functools.partial(group_bwd_kernel, members, block),
        out_shape=(jax.ShapeDtypeStruct((GW, rows), bf16),)
        + tuple(jax.ShapeDtypeStruct((2 * GW, rows), bf16) for _ in range(members)),
        in_specs=[SMEM] + vmem(5 + NG + members),
        out_specs=vmem(1 + members),
        scratch_shapes=[
            pltpu.VMEM((GW, keys), bf16),
            pltpu.VMEM((GW, keys), bf16),
            pltpu.VMEM((GW, keys), f32),
            pltpu.VMEM((GW, keys), f32),
            pltpu.VMEM((GW, rows), bf16),
        ],
        cost_estimate=CHEAP,
        compiler_params=params(),
        name="group_bwd",
    )(scal, starts, ends, q, o, lse, *dos, *kvs)


def normalize(r, width):
    mean = jnp.sum(r, axis=1, keepdims=True) * (1.0 / width)
    centered = r - mean
    var = jnp.sum(centered * centered, axis=1, keepdims=True) * (1.0 / width)
    rstd = lax.rsqrt(var + eps)
    return centered * rstd, rstd


def norm_back(dy, hat, rstd, gain, width):
    dhat = dy * gain
    one = jnp.sum(dhat, axis=1, keepdims=True) * (1.0 / width)
    two = jnp.sum(dhat * hat, axis=1, keepdims=True) * (1.0 / width)
    return rstd * (dhat - one - hat * two)


INV_SQRT2 = 0.7071067811865476
INV_SQRT2PI = 0.3989422804014327


def middle_kernel(block, *refs):
    scal = refs[0]
    at = 1
    o_refs = refs[at : at + NG]
    at += NG
    x_ref, dy_ref, small, small_oth = refs[at : at + 4]
    at += 4
    out_parts = refs[at : at + 3]
    inner_parts = refs[at + 3 : at + 8]
    outer_parts = refs[at + 8 : at + 13]
    at += 13
    y_ref, dr_ref = refs[at : at + 2]
    at += 2
    do_refs = refs[at : at + NG]
    at += NG
    grad_outs = refs[at : at + 4]
    at += 4
    ot_scr, wout, winner, wouter, hbt, gt_scr, gp_scr, dot_scr, vec_ref, ib_ref, sums_ref, acc_ref = refs[at : at + 12]
    grad_refs = refs[at + 12 : at + 16]
    keeps, sends = grad_refs[:2], grad_refs[2:]
    sems = refs[at + 16]
    g_id, fi, core = scal[0], scal[1], scal[2]
    width = x_ref.shape[1]
    ffq = winner.shape[2]
    half = width // 2
    quarter = width // 4

    copies = []

    def load(src, dst):
        copies.append(pltpu.make_async_copy(src, dst, sems.at[len(copies)]))
        copies[-1].start()

    def rows_of(full):
        own = fi * (full // 2)
        oth = (1 - fi) * (full // 2)
        q = full // 4
        return (
            pl.ds(pl.multiple_of(own, 64), full // 2),
            pl.ds(pl.multiple_of(oth + core * q, 64), q),
            pl.ds(pl.multiple_of(oth + (1 - core) * q, 64), q),
        )

    for part, rows in zip(out_parts, rows_of(width)):
        load(part, wout.at[rows, :])
    own, mine, sib = (r.start for r in rows_of(width))
    unit = width // 16
    inner_rows = [pl.ds(own, 8 * unit)] + [
        pl.ds(pl.multiple_of(first + k * unit, 16), n * unit)
        for first in (mine, sib)
        for k, n in ((0, 1), (1, 3))
    ]
    for a in range(4):
        for part, rows in zip(inner_parts, inner_rows):
            load(part.at[:, a * ffq : (a + 1) * ffq], winner.at[a, rows, :])
    own, mine, sib = (r.start for r in rows_of(4 * ffq))
    unit = ffq // 4
    outer_rows = [pl.ds(own, 8 * unit)] + [
        pl.ds(pl.multiple_of(first + k * unit, 16), n * unit)
        for first in (mine, sib)
        for k, n in ((0, 1), (1, 3))
    ]
    for part, rows in zip(outer_parts, outer_rows):
        load(part, wouter.at[rows, :])

    for j in range(NG):
        row = pl.multiple_of(jnp.bitwise_xor(g_id, j) * GW, HD)
        ot_scr[pl.ds(row, GW), :] = o_refs[j][...]
    for side, y in ((small, fi), (small_oth, 1 - fi)):
        vec_ref[:, pl.ds(pl.multiple_of(y * half, 128), half)] = side[:8, :].astype(f32)
        for c in range(2):
            for k in range(2):
                ib_ref[pl.ds(2 * y + c, 1), k * half : (k + 1) * half] = side[
                    8 + 2 * c + k : 9 + 2 * c + k, :
                ].astype(f32)
    for c in copies[:3]:
        c.wait()
    vec = [vec_ref[i : i + 1, :] for i in range(8)]
    obias, gain1, shift1, outbias, gain2, shift2 = vec[:6]
    attn = ot_scr[...].T
    r1 = x_ref[...].astype(f32) + dot(attn, wout[...]) + obias
    hat1, rstd1 = normalize(r1, width)
    hn = hat1 * gain1 + shift1
    hb = hn.astype(bf16)
    hb_t = hb.T
    for y in range(2):
        for c in range(2):
            piece = hb_t[(2 * y + c) * quarter : (2 * y + c + 1) * quarter]

            @pl.when(core == c)
            def _(piece=piece, y=y):
                hbt[y * quarter : (y + 1) * quarter, :] = piece

            @pl.when(core != c)
            def _(piece=piece, y=y):
                hbt[half + y * quarter : half + (y + 1) * quarter, :] = piece

    for c in copies[3:]:
        c.wait()
    acc_ref[...] = hn + outbias

    @pl.loop(0, 4)
    def _(a):
        u = dot(hb, winner[a]) + ib_ref[pl.ds(a, 1), :]
        phi = 0.5 + 0.5 * lax.erf(u * INV_SQRT2)
        g = (u * phi).astype(bf16)
        gp_scr[a] = phi + u * (jnp.exp(u * u * -0.5) * INV_SQRT2PI)
        gt_scr[a] = g.T
        acc_ref[...] += dot(g, wouter[pl.ds(pl.multiple_of(a * ffq, ffq), ffq), :])

    z = acc_ref[...]
    hat2, rstd2 = normalize(z, width)
    y_ref[...] = (hat2 * gain2 + shift2).astype(bf16)
    dy = dy_ref[...].astype(f32)
    sums_ref[4:5, :] = jnp.sum(dy * hat2, axis=0, keepdims=True)
    sums_ref[5:6, :] = jnp.sum(dy, axis=0, keepdims=True)
    dz = norm_back(dy, hat2, rstd2, gain2, width)
    dzb = dz.astype(bf16)
    sums_ref[3:4, :] = jnp.sum(dzb.astype(f32), axis=0, keepdims=True)
    acc_ref[...] = dz

    @pl.loop(0, 4)
    def _(a):
        dg = dot(dzb, wouter[pl.ds(pl.multiple_of(a * ffq, ffq), ffq), :], 1, 1)
        du = (dg * gp_scr[a]).astype(bf16)
        sums_ref[pl.ds(6 + a, 1), :] = jnp.sum(du.astype(f32), axis=0, keepdims=True)
        acc_ref[...] += dot(du, winner[a], 1, 1)
        grad = dot(hbt[...], du).astype(bf16)
        rows = pl.ds(pl.multiple_of(a * quarter, 64), quarter)
        for y in range(2):
            keeps[0][y, rows] = grad[y * quarter : (y + 1) * quarter]
            sends[0][y, rows] = grad[half + y * quarter : half + (y + 1) * quarter]
        grad = dot(gt_scr[a], dzb).astype(bf16)
        mine = core == jnp.bitwise_and(a, 1)

        @pl.when(mine)
        def _():
            keeps[1][jnp.right_shift(a, 1), :ffq] = grad

        @pl.when(jnp.logical_not(mine))
        def _():
            sends[1][jnp.right_shift(a, 1), :ffq] = grad

    dh = acc_ref[...]
    stored = []

    def store(rows):
        for src, dst in zip(grad_refs, grad_outs):
            part = slice(*rows(src.shape[1]))
            sem = sems.at[len(copies) + len(stored)]
            stored.append(pltpu.make_async_copy(src.at[:, part], dst.at[:, part], sem))
            stored[-1].start()

    store(lambda n: (0, ffq))
    sums_ref[1:2, :] = jnp.sum(dh * hat1, axis=0, keepdims=True)
    sums_ref[2:3, :] = jnp.sum(dh, axis=0, keepdims=True)
    dr = norm_back(dh, hat1, rstd1, gain1, width)
    dr_ref[...] = dr
    dab = dr.astype(bf16)
    sums_ref[0:1, :] = jnp.sum(dab.astype(f32), axis=0, keepdims=True)
    for y in range(2):
        top = jnp.concatenate([sums_ref[0:6, :], sums_ref[6 + 2 * y : 8 + 2 * y, :]], axis=0)
        spare = jnp.concatenate([top, jnp.zeros((SPARE - 8, width), f32)], axis=0).astype(bf16)
        none = jnp.zeros((SPARE, width), bf16)

        @pl.when(core == 0)
        def _(y=y, spare=spare, none=none):
            keeps[0][y, 4 * quarter : 4 * quarter + SPARE] = spare
            sends[0][y, 4 * quarter : 4 * quarter + SPARE] = none

        @pl.when(core != 0)
        def _(y=y, spare=spare, none=none):
            keeps[0][y, 4 * quarter : 4 * quarter + SPARE] = none
            sends[0][y, 4 * quarter : 4 * quarter + SPARE] = spare

    dot_scr[...] = dot(wout[...], dab, 1, 1).astype(bf16)
    for j in range(NG):
        row = pl.multiple_of(jnp.bitwise_xor(g_id, j) * GW, HD)
        do_refs[j][...] = dot_scr[pl.ds(row, GW), :]
    grad = dot(ot_scr[...], dab).astype(bf16)
    for y in range(2):
        for c in range(2):
            piece = grad[(2 * y + c) * quarter : (2 * y + c + 1) * quarter]

            @pl.when(core == c)
            def _(piece=piece, y=y):
                keeps[1][y, ffq:] = piece[:OUT_A]
                keeps[0][y, 4 * quarter + SPARE :] = piece[OUT_A:]

            @pl.when(core != c)
            def _(piece=piece, y=y):
                sends[1][y, ffq:] = piece[:OUT_A]
                sends[0][y, 4 * quarter + SPARE :] = piece[OUT_A:]

    store(lambda n: (ffq, n))
    for c in stored:
        c.wait()


def middle(block, scal, os, x, dy, small, small_oth, outs, inners, outers):
    width = x.shape[1]
    ffq = inners[0].shape[1] // 4
    q = width // 4
    grads = [
        jax.ShapeDtypeStruct((2, 5 * q + SPARE - OUT_A, ffq), bf16),
        jax.ShapeDtypeStruct((2, ffq + OUT_A, width), bf16),
    ]
    return pl.pallas_call(
        functools.partial(middle_kernel, block),
        out_shape=(
            jax.ShapeDtypeStruct((block, width), bf16),
            jax.ShapeDtypeStruct((block, width), f32),
        )
        + tuple(jax.ShapeDtypeStruct((GW, block), bf16) for _ in range(NG))
        + tuple(grads)
        + tuple(grads),
        in_specs=[SMEM] + vmem(NG + 4) + anyspec(13),
        out_specs=vmem(2 + NG) + anyspec(4),
        scratch_shapes=[
            pltpu.VMEM((width, block), bf16),
            pltpu.VMEM((width, width), bf16),
            pltpu.VMEM((4, width, ffq), bf16),
            pltpu.VMEM((4 * ffq, width), bf16),
            pltpu.VMEM((width, block), bf16),
            pltpu.VMEM((4, ffq, block), bf16),
            pltpu.VMEM((4, block, ffq), f32),
            pltpu.VMEM((width, block), bf16),
            pltpu.VMEM((8, width), f32),
            pltpu.VMEM((4, ffq), f32),
            pltpu.VMEM((16, width), f32),
            pltpu.VMEM((block, width), f32),
        ]
        + [pltpu.VMEM(g.shape, g.dtype) for g in grads + grads]
        + [
            pltpu.SemaphoreType.DMA((36,)),
        ],
        cost_estimate=CHEAP,
        compiler_params=params(60),
        name="middle",
    )(scal, *os, x, dy, small, small_oth, *outs, *inners, *outers)


def turn_kernel(scal, x0, x1, x2, x3, xt):
    core = scal[1]
    block, width = x0.shape
    half, quarter = width // 2, width // 4
    for j, x in enumerate((x0, x1, x2, x3)):
        cols = slice(j * block, (j + 1) * block)
        turned = x[...].T
        for y in range(2):
            for c in range(2):
                piece = turned[(2 * y + c) * quarter : (2 * y + c + 1) * quarter]

                @pl.when(core == c)
                def _(piece=piece, y=y):
                    xt[y * quarter : (y + 1) * quarter, cols] = piece

                @pl.when(core != c)
                def _(piece=piece, y=y):
                    xt[half + y * quarter : half + (y + 1) * quarter, cols] = piece


def turn(scal, xs):
    block, width = xs[0].shape
    return pl.pallas_call(
        turn_kernel,
        out_shape=jax.ShapeDtypeStruct((width, NG * block), bf16),
        in_specs=[SMEM] + vmem(NG),
        out_specs=vmem(1)[0],
        compiler_params=params(),
        name="turn",
    )(scal, *xs)


def qkv_grad_kernel(scal, xt, dq_ref, dkv_ref, keep, send, d_scr):
    g_id, core = scal[0], scal[2]
    d_scr[:GW, :] = dq_ref[...]
    d_scr[GW:, :] = dkv_ref[...]
    d = d_scr[...]
    quarter = xt.shape[0] // 4
    part = quarter // 2
    step = part + EXTRA
    grad = dot(xt[...], d, 1, 1).astype(bf16)
    ones = jnp.where(lax.broadcasted_iota(jnp.int32, (EXTRA, d.shape[1]), 0) == 0, 1.0, 0.0)
    sums = dot(ones.astype(bf16), d, 1, 1).astype(bf16)
    none = jnp.zeros_like(sums)
    for k, out in enumerate((keep, send)):
        for y in range(2):
            at = (2 * k + y) * quarter
            for x in range(2):
                out[y, x * step : x * step + part] = grad[at + x * part : at + (x + 1) * part]
                out[y, x * step + part : (x + 1) * step] = none
    for y in range(2):
        mine = jnp.right_shift(g_id, 1) == y

        @pl.when(mine & (core == 0))
        def _(y=y):
            keep[y, part:step] = sums

        @pl.when(mine & (core != 0))
        def _(y=y):
            send[y, part:step] = sums


def qkv_grad(scal, xt, dq, dkv):
    width, rows = xt.shape
    q = width // 4 + 2 * EXTRA
    return pl.pallas_call(
        qkv_grad_kernel,
        out_shape=(
            jax.ShapeDtypeStruct((2, q, 3 * GW), bf16),
            jax.ShapeDtypeStruct((2, q, 3 * GW), bf16),
        ),
        in_specs=[SMEM] + vmem(3),
        out_specs=vmem(2),
        scratch_shapes=[pltpu.VMEM((3 * GW, rows), bf16)],
        compiler_params=params(),
        name="qkv_grad",
    )(scal, xt, dq, dkv)


def each_part(scal, fn):
    xi, core = scal[1], scal[2]
    for c in range(2):
        for x in range(2):
            fn(c, x, jnp.bitwise_xor(core, c) * 2 + jnp.bitwise_xor(xi, x))


def unpack_kernel(place, scal, *refs):
    parts, outs, bias_ref = refs[0], refs[1:4], refs[4]
    rows = parts.shape[2] - EXTRA
    fi = place[1]

    def put(c, x, s):
        at = (2 * c + x) * rows
        for g in range(NG):
            v = parts[s, g, :rows].astype(f32)
            for part in range(3):
                outs[part][at : at + rows, g * GW : (g + 1) * GW] = v[
                    :, part * GW : (part + 1) * GW
                ]
        if (c, x) == (0, 0):
            for k in range(2):
                row = parts[s, 2 * fi + k, rows:].astype(f32)
                bias_ref[0:1, k * GW : (k + 1) * GW] = row[:1, :GW]
                bias_ref[1:2, k * GW : (k + 1) * GW] = row[:1, 2 * GW :]

    each_part(scal, put)


def spread_rows(segments, first, v):
    base = 0
    for n, place in segments:
        lo, hi = max(first, base), min(first + v.shape[0], base + n)
        if lo < hi:
            place(lo - base, v[lo - first : hi - first])
        base += n


def finish_kernel(scal, *refs):
    parts_a, whole_b = refs[:2]
    outer_ref, inner_ref, out_ref, vec_ref = refs[2:]
    ffq = inner_ref.shape[1] // 4
    quarter = inner_ref.shape[0] // 2
    g_id = scal[0]
    n_a, n_b = parts_a.shape[2], whole_b.shape[1]

    def put_a(c, x, s):
        def outer(row, v):
            outer_ref[c * ffq + row : c * ffq + row + v.shape[0], :] = v

        def out(row, v):
            out_ref[c * quarter + row : c * quarter + row + v.shape[0], :] = v

        for g in range(NG):
            j = jnp.bitwise_xor(g_id, g)
            v = parts_a[s, jnp.bitwise_and(j, 1) * 2 + jnp.right_shift(j, 1)].astype(f32)
            spread_rows(((ffq, outer), (OUT_A, out)), (NG * x + g) * n_a, v)

    each_part(scal, put_a)
    for i in range(whole_b.shape[0]):
        g, x, c = i >> 2, i >> 1 & 1, i & 1
        def inner(a, row, v, c=c):
            at = c * quarter + row
            inner_ref[at : at + v.shape[0], a * ffq : (a + 1) * ffq] = v

        def out(row, v, c=c):
            at = c * quarter + OUT_A + row
            out_ref[at : at + v.shape[0], :] = v

        def sums(row, v, c=c):
            if c == 0 and row < 8:
                vec_ref[row : min(8, row + v.shape[0]), :] = v[: 8 - row]

        spread_rows(
            tuple((quarter, functools.partial(inner, a)) for a in range(4))
            + ((SPARE, sums), (quarter - OUT_A, out)),
            (NG * x + g) * n_b,
            whole_b[i].astype(f32),
        )


def ending_kernel(place, spot, *refs):
    parts, whole_b, parts_q = refs[:4], refs[4], refs[5:9]
    dr_ref, d_refs, w_parts = refs[9], refs[10 : 10 + 2 * NG], refs[10 + 2 * NG : 13 + 2 * NG]
    outs = refs[13 + 2 * NG : 21 + 2 * NG]
    dx_ref = refs[21 + 2 * NG]
    staged_refs = refs[22 + 2 * NG : 30 + 2 * NG]
    w_scr, d_scr, a_scr, q_scr, sems = refs[30 + 2 * NG :]
    g_id, fi, core = place[0], place[1], place[2]
    width = w_scr.shape[0]
    q = width // 4
    oth = (1 - fi) * 2 * q
    rows = (
        pl.ds(pl.multiple_of(fi * 2 * q, 64), 2 * q),
        pl.ds(pl.multiple_of(oth + core * q, 64), q),
        pl.ds(pl.multiple_of(oth + (1 - core) * q, 64), q),
    )
    loads = [
        pltpu.make_async_copy(p, w_scr.at[r, :], sems.at[i])
        for i, (p, r) in enumerate(zip(w_parts, rows))
    ]
    pieces = [
        pltpu.make_async_copy(src, scr.at[s], sems.at[11 + 4 * k + s])
        for k, (group, scr) in enumerate(((parts, a_scr), (parts_q, q_scr)))
        for s, src in enumerate(group)
    ]
    for c in pieces + loads:
        c.start()
    stores = [
        pltpu.make_async_copy(src, dst, sems.at[3 + i])
        for i, (src, dst) in enumerate(zip(staged_refs, outs))
    ]
    for c in pieces[:4]:
        c.wait()
    finish_kernel(spot, a_scr, whole_b, *staged_refs[:4])
    for c in stores[:4]:
        c.start()
    for c in pieces[4:]:
        c.wait()
    unpack_kernel(place, spot, q_scr, *staged_refs[4:])
    for c in stores[4:]:
        c.start()
    for j in range(NG):
        base = jnp.bitwise_xor(g_id, j) * GW
        for part in range(3):
            at = pl.multiple_of(part * width + base, HD)
            src = d_refs[j][...] if part == 0 else d_refs[NG + j][(part - 1) * GW : part * GW, :]
            d_scr[pl.ds(at, GW), :] = src
    for c in loads:
        c.wait()
    dx_ref[...] = dr_ref[...] + dot(w_scr[...], d_scr[...]).T
    for c in stores:
        c.wait()


def ending(place, spot, parts_a, whole_b, parts_q, dr, d_parts, w_parts, shapes):
    block, width = dr.shape
    wide = [
        *shapes,
        (8, width),
        *((width // 2, width) for _ in range(3)),
        (2, 2 * GW),
    ]
    return pl.pallas_call(
        ending_kernel,
        out_shape=tuple(jax.ShapeDtypeStruct(s, f32) for s in wide)
        + (jax.ShapeDtypeStruct((block, width), f32),),
        in_specs=[SMEM, SMEM] + anyspec(4) + vmem(1) + anyspec(4) + vmem(1 + 2 * NG) + anyspec(3),
        out_specs=anyspec(8) + vmem(1),
        scratch_shapes=[pltpu.VMEM(s, f32) for s in wide]
        + [
            pltpu.VMEM((width, 3 * width), bf16),
            pltpu.VMEM((3 * width, block), bf16),
            pltpu.VMEM((4,) + parts_a[0].shape, bf16),
            pltpu.VMEM((4,) + parts_q[0].shape, bf16),
            pltpu.SemaphoreType.DMA((19,)),
        ],
        cost_estimate=CHEAP,
        compiler_params=params(60),
        name="ending",
    )(place, spot, *parts_a, whole_b, *parts_q, dr, *d_parts, *w_parts)


def fast_device(
    tokens,
    query_weight,
    query_bias,
    key_weight,
    value_weight,
    value_bias,
    out_weight,
    out_bias,
    first_gain,
    first_shift,
    inner_weight,
    inner_bias,
    outer_weight,
    outer_bias,
    second_gain,
    second_shift,
    doc_lengths,
    grad_output,
):
    block = tokens.shape[1]
    width = tokens.shape[2]
    ctx = lax.axis_size("ctx")
    members = ctx // NG
    ci = lax.axis_index("ctx")
    fi = lax.axis_index("fsdp")
    g_id = ci // members
    m_id = ci % members
    core = ci % 2
    xi = m_id // 2
    half = width // 2
    tie = lax.optimization_barrier

    def zswap(v, j):
        return swap(v, "ctx", j * members)

    def xswap(v):
        return swap(v, "ctx", 2)

    def cswap(v):
        return swap(v, "ctx", 1)

    def yswap(v):
        return swap(v, "fsdp", 1)

    local = tokens[0]
    x2 = zswap(local, 2)
    x1 = zswap(local, 1)
    w_own = jnp.concatenate(
        [
            lax.dynamic_slice_in_dim(w, g_id * GW, GW, 1)
            for w in (query_weight, key_weight, value_weight)
        ],
        axis=1,
    )
    small = pack(
        [
            out_bias,
            first_gain,
            first_shift,
            outer_bias,
            second_gain,
            second_shift,
            query_bias,
            value_bias,
            inner_bias,
        ]
    )

    def half_of(w):
        rows = w.shape[0] // 2
        return lax.dynamic_slice_in_dim(w, core * rows, rows, 0)

    w_mine = yswap(half_of(w_own))
    out_mine = yswap(half_of(out_weight))
    w_sib = cswap(w_mine)
    out_mine, small, w_mine, w_sib, x2, x1, inner_raw, outer_raw, doc_lengths = tie(
        (out_mine, small, w_mine, w_sib, x2, x1, inner_weight, outer_weight, doc_lengths)
    )
    x3 = zswap(x2, 1)
    small_oth = yswap(small)
    inner_half, outer_half = half_of(inner_raw), half_of(outer_raw)
    cut = inner_half.shape[0] // 4
    inner_one = yswap(inner_half[:cut])

    doc_ends = jnp.cumsum(doc_lengths[0])
    first = jnp.stack([(jnp.bitwise_xor(g_id, j) * members + m_id) * block for j in range(NG)])
    places = (first[:, None] + jnp.arange(block, dtype=jnp.int32)[None, :]).reshape(-1)
    before = places[:, None] >= doc_ends[None, :]
    starts = jnp.max(jnp.where(before, doc_ends[None, :], 0), axis=1).astype(jnp.int32)
    ends = jnp.min(jnp.where(before, ctx * block, doc_ends[None, :]), axis=1).astype(jnp.int32)
    low = starts.reshape(NG, block)[:, 0] // block
    high = (ends.reshape(NG, block)[:, -1] + block - 1) // block
    plain_low = (starts.reshape(NG, block)[:, -1] + block - 1) // block
    plain_high = ends.reshape(NG, block)[:, 0] // block
    whole = plain_low < plain_high
    plain_low = jnp.where(whole, plain_low, high)
    plain_high = jnp.where(whole, plain_high, high)
    scal = jnp.concatenate(
        [jnp.stack([m_id, g_id]), low, high, plain_low, plain_high]
    ).astype(jnp.int32)
    starts = starts[None]
    ends = ends[None]
    place = jnp.stack([g_id, fi, core]).astype(jnp.int32)
    spot = jnp.stack([g_id, xi, core]).astype(jnp.int32)
    dev = jnp.stack([fi, core]).astype(jnp.int32)
    tied = (small_oth, place, spot, dev, x3, inner_one, inner_half, outer_half, scal, starts, ends)
    small_oth, place, spot, dev, x3, inner_one, inner_half, outer_half, scal, starts, ends = tie(tied)

    xs = [local, x1, x2, x3]
    q_t, kv = project(block, place, xs, w_own, w_mine, w_sib, small, small_oth)

    kv_x = xswap(kv)
    inner_two = yswap(inner_half[cut:])
    cut = outer_half.shape[0] // 4
    outer_one = yswap(outer_half[:cut])
    sibs = [cswap(out_mine), cswap(inner_one)]
    tied = tie((kv_x, inner_two, outer_one) + tuple(sibs))
    (kv_x, inner_two, outer_one), sibs = tied[:3], list(tied[3:])
    kv_c = cswap(kv)
    kv_xc = cswap(kv_x)
    kv, kv_c, kv_x, kv_xc, inner_two, outer_one, outer_half = tie(
        (kv, kv_c, kv_x, kv_xc, inner_two, outer_one, outer_half)
    )
    kvs = [kv, kv_c, kv_x, kv_xc]
    outer_two = yswap(outer_half[cut:])
    sibs += [cswap(inner_two), cswap(outer_one)]
    res = group_fwd(members, block, scal, starts, ends, q_t, kvs)
    qkv_shard = jnp.concatenate([query_weight, key_weight, value_weight], axis=1)
    qkv_half = half_of(qkv_shard)
    tied = tie(tuple(res) + (outer_two, qkv_shard, qkv_half) + tuple(sibs))
    res, (outer_two, qkv_shard, qkv_half), sibs = tied[: 2 + NG], tied[2 + NG : 5 + NG], list(tied[5 + NG :])
    o_t, lse = res[:2]
    o_cols = list(res[2:])
    o_parts = [o_cols[0]] + [zswap(o_cols[j], j) for j in range(1, NG)]
    sibs.append(cswap(outer_two))
    tied = tie(tuple(o_parts) + (sibs[-1], qkv_half))
    o_parts, sibs[-1], qkv_half = list(tied[:NG]), tied[NG], tied[NG + 1]
    outs = (out_weight, out_mine, sibs[0])
    inners = (inner_weight, inner_one, inner_two, sibs[1], sibs[2])
    outers = (outer_weight, outer_one, outer_two, sibs[3], sibs[4])
    qkv_mine = yswap(qkv_half)

    mid = middle(block, place, o_parts, local, grad_output[0], small, small_oth, outs, inners, outers)
    tied = tie(tuple(mid) + (qkv_mine,))
    mid, qkv_mine = tied[:-1], tied[-1]
    output, d_first = mid[:2]
    dos = list(mid[2 : 2 + NG])
    keep_a, keep_b, send_a, send_b = mid[2 + NG :]

    state = [output]

    def then(v):
        v, _ = tie((v, state[0]))
        state[0] = v
        return v

    def rows_at(v, index, parts, axis=0):
        n = v.shape[axis] // parts
        return lax.dynamic_slice_in_dim(v, index * n, n, axis)

    def low_sum(terms, cut):
        return then(sum(cut(t).astype(f32) for t in terms).astype(bf16))

    z1 = g_id % 2
    z2 = g_id // 2

    keep_a, keep_b, send_a, send_b = keep_b, keep_a, send_b, send_a
    core_a = cswap(send_a)
    core_b = cswap(send_b)
    dos = [dos[0]] + [zswap(dos[j], j) for j in range(1, NG)]
    terms_b = [keep_b, core_b]
    terms_a = [keep_a, core_a]
    send_a = low_sum(terms_a, lambda v: pick(v, 1 - fi))
    send_b = low_sum(terms_b, lambda v: rows_at(v, 1 - xi, 2, 1))
    tied = tie(tuple(dos) + (send_a, send_b))
    dos, (send_a, send_b) = list(tied[:NG]), tied[NG:]
    got_a = yswap(send_a)
    got_b = xswap(send_b)
    res = group_bwd(members, block, scal, starts, ends, q_t, o_t, lse, dos, kvs)
    tied = tie(tuple(res) + (got_a, got_b))
    res, (got_a, got_b) = tied[:-2], tied[-2:]
    state[0] = got_b
    terms_a = [pick(t, fi) for t in terms_a] + [got_a]
    terms_b = [rows_at(t, xi, 2, 1) for t in terms_b] + [got_b]

    send_a = low_sum(terms_a, lambda v: rows_at(v, 1 - xi, 2))
    send_b = low_sum(terms_b, lambda v: pick(v, 1 - fi))
    got_a, got_b = xswap(send_a), yswap(send_b)
    dq, slots = res[0], res[1:]
    k1, k3 = cswap(slots[1]), cswap(slots[3])
    qkv_sib = cswap(qkv_mine)
    got_a, got_b, k1, k3, qkv_sib = tie((got_a, got_b, k1, k3, qkv_sib))
    terms_a = [rows_at(t, xi, 2) for t in terms_a] + [got_a]
    terms_b = [pick(t, fi) for t in terms_b] + [got_b]
    sum_a = sum(t.astype(f32) for t in terms_a).astype(bf16).reshape(NG, -1, width)
    sum_b = sum(t.astype(f32) for t in terms_b).astype(bf16).reshape(NG, -1, width)
    n_a, n_b = sum_a.shape[1], sum_b.shape[1]
    chunk = then(jnp.concatenate([sum_a, sum_b], axis=1).reshape(-1, width))
    columns = [[m + members * g for g in range(NG)] for m in range(members)]
    piece = lax.psum_scatter(
        chunk, "ctx", scatter_dimension=0, tiled=True, axis_index_groups=columns
    )
    got_kv = xswap(low_sum([slots[2], k3], lambda v: v))
    xt = turn(dev, tie(tuple(xs) + (state[0],))[:NG])
    dq_parts = [dq[:, j * block : (j + 1) * block] for j in range(NG)]
    dq_parts = tie(tuple(dq_parts) + (state[0],))[:NG]
    dq_parts = [dq_parts[0]] + [zswap(dq_parts[j], j) for j in range(1, NG)]
    tied = tie((got_kv, xt) + tuple(dq_parts))
    got_kv, xt, dq_parts = tied[0], tied[1], list(tied[2:])
    dkv = low_sum([slots[0], k1, got_kv], lambda v: v)
    dkv_parts = [dkv[:, j * block : (j + 1) * block] for j in range(NG)]
    keep_q, send_q = qkv_grad(place, xt, dq, dkv)
    terms_q = [keep_q, cswap(send_q)]
    got_q = yswap(low_sum(terms_q, lambda v: pick(v, 1 - fi)))
    terms_q = [pick(t, fi) for t in terms_q] + [got_q]

    piece = tie((piece, state[0]))[0]
    piece_a = piece[:n_a]
    whole_b = lax.all_gather(piece[n_a:], "ctx", axis=0)
    far_a = zswap(piece_a, 2)
    got_q = xswap(low_sum(terms_q, lambda v: rows_at(v, 1 - xi, 2)))
    far_a = tie((far_a, state[0]))[0]
    pair_a = then(jnp.stack([piece_a, far_a]))
    near_a = zswap(pair_a, 1)
    got_q = tie((got_q, state[0]))[0]
    terms_q = [rows_at(t, xi, 2) for t in terms_q] + [got_q]
    piece_q = low_sum(terms_q, lambda v: v)
    far_q = zswap(piece_q, 2)
    near_a = tie((near_a, state[0]))[0]
    col_a = then(jnp.stack([pair_a, near_a]))
    side_a = xswap(col_a)
    far_q = tie((far_q, state[0]))[0]
    piece_q = then(ordered(z2, piece_q, far_q))
    near_q = zswap(piece_q, 1)
    piece_q = then(ordered(z1, piece_q, near_q).transpose(1, 0, 2, 3).reshape(NG, -1, 3 * GW))
    side_q = xswap(piece_q)
    dkv_parts = tie(tuple(dkv_parts) + (state[0],))[:NG]
    dkv_parts = [dkv_parts[0]] + [zswap(dkv_parts[j], j) for j in range(1, NG)]
    tied = tie((side_a, side_q) + tuple(dkv_parts))
    side_a, side_q, dkv_parts = tied[0], tied[1], tied[2:]
    parts_q = [piece_q, side_q, cswap(piece_q), cswap(side_q)]
    core_a, core_side = cswap(col_a), cswap(side_a)
    tied = tie(tuple(parts_q) + (core_a, core_side))
    parts_q, core_a, core_side = tied[:4], tied[4], tied[5]
    parts_a = [v.reshape(NG, n_a, width) for v in (col_a, side_a, core_a, core_side)]
    tied = tie(tuple(parts_q) + tuple(parts_a) + (whole_b,) + tuple(dq_parts) + tuple(dkv_parts))
    parts_q, parts_a, whole_b, d_parts = tied[:4], tied[4:8], tied[8], tied[9:]
    (
        grad_outer,
        grad_inner,
        grad_out,
        vecs,
        grad_query,
        grad_key,
        grad_value,
        bias_rows,
        grad_input,
    ) = ending(
        place,
        spot,
        parts_a,
        whole_b,
        parts_q,
        d_first,
        d_parts,
        (qkv_shard, qkv_mine, qkv_sib),
        (outer_weight.shape, inner_weight.shape, out_weight.shape),
    )

    mine = lax.dynamic_slice_in_dim(vecs, fi * half, half, 1)
    return (
        output[None],
        grad_input[None],
        grad_query,
        bias_rows[0],
        grad_key,
        grad_value,
        bias_rows[1],
        grad_out,
        mine[0],
        mine[1],
        mine[2],
        grad_inner,
        vecs[6:8].reshape(-1),
        grad_outer,
        mine[3],
        mine[4],
        mine[5],
    )


def solution(mesh):
    placed = (
        P("fsdp", "ctx", None),
        P("fsdp", None),
        P("fsdp"),
        P("fsdp", None),
        P("fsdp", None),
        P("fsdp"),
        P("fsdp", None),
        P("fsdp"),
        P("fsdp"),
        P("fsdp"),
        P("fsdp", None),
        P("fsdp"),
        P("fsdp", None),
        P("fsdp"),
        P("fsdp"),
        P("fsdp"),
        P("fsdp", None),
        P("fsdp", "ctx", None),
    )
    quick = mesh.shape["fsdp"] == 2 and mesh.shape["ctx"] == 4 * NG
    return jax.shard_map(
        fast_device if quick else on_device,
        mesh=mesh,
        in_specs=placed,
        out_specs=(
            P("fsdp", "ctx", None),
            P("fsdp", "ctx", None),
            P("fsdp", None),
            P("fsdp"),
            P("fsdp", None),
            P("fsdp", None),
            P("fsdp"),
            P("fsdp", None),
            P("fsdp"),
            P("fsdp"),
            P("fsdp"),
            P("fsdp", None),
            P("fsdp"),
            P("fsdp", None),
            P("fsdp"),
            P("fsdp"),
            P("fsdp"),
        ),
        check_vma=False,
    )
```
